128 devices in a mesh: gx: 8 (over z, core), gy: 16 (over x, y).
Axes of the slice: x: 4, y: 4, z: 4, core: 2. Of those that a mesh axis runs over, the one named last changes fastest.
Arguments:
- control: float32 [4, 64, 128, 4096], P(None, None, 'gx', 'gy'), may hold values from -6 to 6
- background: float32 [4, 64, 128, 4096], P(None, None, 'gx', 'gy'), may hold values from -6 to 6
- vert_factor: float32 [4, 64, 64], replicated, may hold values from -0.75 to 0.75
- length_rates: float32 [2, 4, 64], replicated, may hold values from 0.5 to 40
- flash_weights: float32 [4, 64], replicated, may hold values from -3 to 3
- level_weights: float32 [64], replicated, may hold values from -0.75 to 0.75
- obs_owner: int32 [65536, 1], P(('gx', 'gy')), may hold values from 0 to 127; in each aligned block of 512 rows (0 to 511, 512 to 1023, ...) at most 8 rows name the same one
- obs_cell: int32 [65536], P(('gx', 'gy')), may hold values from 0 to 4095
- obs_count: int32 [128], P(('gx', 'gy')), may hold values from 256 to 512, as said below
- flash_obs: float32 [65536], P(('gx', 'gy')), may hold values from 0.1 to 3
- obs_error: float32 [65536], P(('gx', 'gy')), may hold values from 0.3 to 1
Outputs:
- grad: float32 [4, 64, 128, 4096], P(None, None, 'gx', 'gy')
- departure: float32 [65536], P(('gx', 'gy'))
The draws below stay inside these ranges and needn't reach their ends.
Inputs may be any that keep to these rules, and one draw needn't show every extreme that they name: `obs_owner`: among one device's 512 slots no owner is named more than 8 times, a bound that some block reaches. Only the first obs_count slots of a device are live; some device has all 512 live.
All inputs are finite; a program needn't handle non-finite values.
Results may differ from the reference program's by a relative error of at most 0.0003.
Values sent between devices are 32-bit elements; how exact they have to be, the bound alone decides.
No kernel may reach another device: no remote copies, remote signals or barrier semaphores. Data moves between devices by JAX's collectives and lax.ppermute only.
A program may use at most 128 MiB of HBM per device.

```python
import math
import jax
import jax.numpy as jnp
import numpy as np
from jax import lax

NV = 4
LEV = 64
CX = 16
CY = 256
OBS_DEV = 512
NX = 128
NY = 4096
NOBS = 65536
CAP = 8
N_GX = 8
N_GY = 16
DEVICES = 128


def draw_obs_count(key, part):
    counts = jax.random.randint(key, (DEVICES,), OBS_DEV // 2, OBS_DEV + 1)
    fullest = jax.random.randint(jax.random.fold_in(key, 7), (), 0, DEVICES)
    return counts.at[fullest].set(OBS_DEV).astype(jnp.int32)


def with_ends(drawn, key, low, high):
    longest = drawn.shape.index(max(drawn.shape))
    spots = []
    for shift in (0, 1):
        where = [jax.random.randint(jax.random.fold_in(key, axis), (), 0, length) for axis, length in enumerate(drawn.shape)]
        where[longest] = (where[longest] + shift) % drawn.shape[longest]
        spots.append(tuple(where))
    return drawn.at[spots[0]].set(low).at[spots[1]].set(high)


def block_scale(key, shape, cuts, smallest, high):
    loudness, own = 1.0, jax.random.fold_in(key, 6)
    for dim, shards_of in cuts:
        draws = jnp.exp(jax.random.uniform(jax.random.fold_in(own, dim), (shards_of,), jnp.float32, smallest / len(cuts), high / len(cuts)))
        loudness = loudness * jnp.repeat(draws, shape[dim] // shards_of).reshape([-1 if axis == dim else 1 for axis in range(len(shape))])
    return loudness


def shared_out(stream_key, own, number, rows, number_of, top, most, lean):
    sequence = jax.random.permutation(stream_key, number_of)
    packed, common = load_shares(number_of, rows * top, most, lean, True), load_shares(number_of, rows * top, most, lean, False)
    places = jnp.arange(number_of)

    def named(tallies, rotation):
        used = int((tallies > 0).sum())
        fixed = max(1, used // 4)
        moved = fixed + (places - fixed + rotation * (used - fixed)) % max(1, number_of - fixed)
        return jnp.zeros((number_of,), jnp.int32).at[sequence[jnp.where(places < fixed, places, moved)]].set(jnp.asarray(tallies, jnp.int32))

    tallies = jnp.where(number % 4 == 0, named(packed, number // 4), named(common, number - number // 4 - 1))
    mixed = jax.random.permutation(jax.random.fold_in(own, 3), number_of)
    source_of, receiver = mixed[0:number_of // 2 * 2:2], mixed[1:number_of // 2 * 2:2]
    room = jnp.minimum(tallies[source_of] - 1, most - tallies[receiver]) // 2
    room = jnp.where((source_of == sequence[0]) | (receiver == sequence[0]) | (tallies[receiver] == 0), 0, jnp.maximum(room, 0))
    moved = jax.random.randint(jax.random.fold_in(own, 4), (number_of // 2,), 0, 1 << 20) % (room + 1)
    tallies = tallies.at[source_of].add(-moved).at[receiver].add(moved)
    members = jnp.searchsorted(jnp.cumsum(tallies), jnp.arange(rows * top), side="right").astype(jnp.int32)
    listing = members.reshape(top, rows).T
    listing = listing[jax.random.permutation(jax.random.fold_in(own, 1), rows)]
    rotation = jax.random.randint(jax.random.fold_in(own, 2), (rows, 1), 0, top)
    return jnp.take_along_axis(listing, (jnp.arange(top)[None, :] + rotation) % top, axis=1)


def load_shares(amount, total, limit, lean, full):
    loads = [(1 << 20) // math.isqrt(standing ** lean) + 1 for standing in range(1, amount + 1)]
    largest = limit if full else min(limit, max(-(-total // amount), total * loads[0] // sum(loads)))
    least = 1 if total - largest >= amount - 1 else 0
    holding, rest = [largest] + [least] * (amount - 1), total - largest - least * (amount - 1)
    while rest > 0:
        movable = [i for i in range(1, amount) if holding[i] < largest] or [i for i in range(1, amount) if holding[i] < limit]
        pool, left = sum([loads[i] for i in movable]), rest
        for i in movable:
            extra = min(limit - holding[i], max(1, left * loads[i] // pool), rest)
            holding[i] = holding[i] + extra
            rest = rest - extra
    return np.array(holding)


def gaussian(stream_key, shape, width, reach, cuts=(), dtype=jnp.bfloat16):
    array = jax.random.normal(stream_key, shape, jnp.float32) * width
    if len(cuts) > 0:
        array = block_scale(stream_key, shape, cuts, -0.22, 0.18) * array
    return jnp.clip(array, min=-reach, max=reach).astype(dtype)


def setup_inputs(seed: int = 0) -> dict:
    streams_of = jax.random.split(jax.random.key(seed), 12)
    control = gaussian(streams_of[0], (NV, LEV, NX, NY), 1.0, 6.0, ((2, 8), (3, 16)), jnp.float32)
    background = gaussian(streams_of[1], (NV, LEV, NX, NY), 1.0, 6.0, ((2, 8), (3, 16)), jnp.float32)
    vert_factor = gaussian(streams_of[2], (NV, LEV, LEV), LEV ** -0.5, 0.75, (), jnp.float32)
    length_rates = jnp.clip(jnp.exp(jax.random.uniform(streams_of[3], (2, NV, LEV), jnp.float32, math.log(0.5), math.log(40.0))), 0.5, 40.0)
    flash_weights = gaussian(streams_of[4], (NV, LEV), NV ** -0.5, 3.0, (), jnp.float32)
    level_weights = gaussian(streams_of[5], (LEV,), LEV ** -0.5, 0.75, (), jnp.float32)
    obs_owner_keys = jax.random.split(jax.random.fold_in(streams_of[6], 1), NOBS // OBS_DEV)
    obs_owner_turns = jax.random.permutation(jax.random.fold_in(streams_of[6], 3), NOBS // OBS_DEV)
    obs_owner = jax.vmap(lambda own, number: shared_out(jax.random.fold_in(streams_of[6], 2), own, number, OBS_DEV, N_GX * N_GY, 1, CAP, 2))(obs_owner_keys, obs_owner_turns).reshape((NOBS, 1))
    obs_cell = with_ends(jax.random.randint(streams_of[7], (NOBS,), 0, CX * CY), jax.random.fold_in(streams_of[7], 1), 0, (CX * CY) - 1).astype(jnp.int32)
    obs_count = draw_obs_count(jax.random.fold_in(streams_of[11], 71), 0)
    flash_obs = jnp.clip(jnp.exp(math.log(3.0) - 3.4011974 * jax.random.uniform(streams_of[9], (NOBS,), jnp.float32) ** block_scale(streams_of[9], (NOBS,), ((0, 128),), -0.2, 0.2)), 0.1, 3.0)
    obs_error = jnp.clip(jnp.exp(math.log(1.0) - 1.2039728 * jax.random.uniform(streams_of[10], (NOBS,), jnp.float32) ** block_scale(streams_of[10], (NOBS,), ((0, 128),), -0.2, 0.2)), 0.3, 1.0)
    return dict(control=control, background=background, vert_factor=vert_factor, length_rates=length_rates, flash_weights=flash_weights, level_weights=level_weights, obs_owner=obs_owner, obs_cell=obs_cell, obs_count=obs_count, flash_obs=flash_obs, obs_error=obs_error)


highest = lax.Precision.HIGHEST

def recursive_pass(field, step, axis, reverse):
    decay = jnp.exp(-step)[:, :, None]
    gain = jnp.sqrt(-jnp.expm1(-2.0 * step))[:, :, None]
    moved = jnp.moveaxis(field, axis, 0)

    def advance(carry, column):
        carry = decay * carry + gain * column
        return (carry, carry)
    start = jnp.zeros(moved.shape[1:], jnp.float32)
    _, result = lax.scan(advance, start, moved, reverse=reverse)
    return jnp.moveaxis(result, 0, axis)

def observe(columns, flash, sigma, flash_weights, level_weights):
    levels = jnp.einsum('nvk,vk->nk', columns, flash_weights, precision=highest)
    total = jnp.dot(jax.nn.softplus(levels), level_weights, precision=highest)
    miss = jax.nn.softplus(total) - flash
    weight = miss / (sigma * sigma) * jax.nn.sigmoid(total)
    adjoint = weight[:, None, None] * (level_weights[None, :] * jax.nn.sigmoid(levels))[:, None, :] * flash_weights[None]
    return (miss, adjoint)

def reference(control, background, vert_factor, length_rates, flash_weights, level_weights, obs_owner, obs_cell, obs_count, flash_obs, obs_error):
    step_x = length_rates[0] / NX
    step_y = length_rates[1] / NY
    smooth = recursive_pass(recursive_pass(control, step_y, 3, False), step_x, 2, False)
    state = background + jnp.einsum('vkj,vjxy->vkxy', vert_factor, smooth, precision=highest)
    owner = obs_owner[:, 0]
    row_index = owner // N_GY * CX + obs_cell // CY
    col_index = owner % N_GY * CY + obs_cell % CY
    slots = jnp.arange(NOBS).astype(jnp.int32)
    live = slots % OBS_DEV < jnp.repeat(obs_count, OBS_DEV)
    livef = live.astype(jnp.float32)
    columns = jnp.transpose(state[:, :, row_index, col_index], (2, 0, 1))
    miss, adjoint = observe(columns, flash_obs, obs_error, flash_weights, level_weights)
    departure = miss * livef
    adjoint = adjoint * livef[:, None, None]
    forcing = jnp.zeros_like(state).at[:, :, row_index, col_index].add(jnp.transpose(adjoint, (1, 2, 0)))
    back = jnp.einsum('vjk,vjxy->vkxy', vert_factor, forcing, precision=highest)
    grad = control + recursive_pass(recursive_pass(back, step_x, 2, True), step_y, 3, True)
    return (grad, departure)
```

```python
import functools

import jax
import jax.numpy as jnp
from jax import lax
from jax.experimental import pallas as pl
from jax.experimental.pallas import tpu as pltpu
from jax.sharding import PartitionSpec as P

highest = lax.Precision.HIGHEST
f32 = jnp.float32
bf16 = jnp.bfloat16

CH, LEVELS, XB, YB = 256, 64, 16, 256
OBS, PEERS, CAP = 512, 128, 8
N_X, N_Y = 8, 16
BLOCK = 32
REQ = 32
VMEM_LIMIT = 60 * 1024 * 1024


def iota(shape, dim):
    return lax.broadcasted_iota(jnp.int32, shape, dim)


def split(value):
    high = value.astype(bf16)
    return high, (value - high.astype(f32)).astype(bf16)


def split3(value):
    high = value.astype(bf16)
    rest = value - high.astype(f32)
    middle = rest.astype(bf16)
    return high, middle, (rest - middle.astype(f32)).astype(bf16)


def mm(a, b):
    return jnp.dot(a, b, preferred_element_type=f32)


def mm_nt(a, b):
    return lax.dot_general(a, b, (((1,), (1,)), ((), ())), preferred_element_type=f32)


def column(row):
    halves = [jnp.broadcast_to(row[:, i : i + 128], (128, 128)).T for i in range(0, CH, 128)]
    return jnp.concatenate(halves, axis=0)


def wide(col):
    return jnp.concatenate([col, col], axis=1)


def upper():
    return jnp.where(iota((YB, YB), 0) <= iota((YB, YB), 1), 1.0, 0.0).astype(bf16)


def lower():
    return jnp.where(iota((YB, YB), 0) >= iota((YB, YB), 1), 1.0, 0.0).astype(bf16)


def softplus(x):
    return jnp.maximum(x, 0.0) + jnp.log1p(jnp.exp(-jnp.abs(x)))


def sigmoid(x):
    return 1.0 / (1.0 + jnp.exp(-x))


def take_plane(halves, x, rows, *lead):
    at = lead + (pl.ds(x, rows, stride=XB), slice(None))
    return jnp.concatenate([half[at] for half in halves], axis=1)


def params(**more):
    return pltpu.CompilerParams(vmem_limit_bytes=VMEM_LIMIT, **more)


def edges_kernel(count, control_a, control_b, rates, owner, cell, flash, sigma, sx, msg, rank_out, colx, coly):
    b = pl.program_id(0)

    @pl.when(b == 0)
    def _():
        colx[...] = column(rates[0:1, :] * (1.0 / 128.0))
        coly[...] = column(rates[1:2, :] * (1.0 / 4096.0))
        live = iota((PEERS, OBS), 1) < count[0]
        chosen = (owner[...] == iota((PEERS, OBS), 0)) & live
        earlier = jnp.where(iota((OBS, OBS), 0) < iota((OBS, OBS), 1), 1.0, 0.0).astype(bf16)
        rank = mm(jnp.where(chosen, 1.0, 0.0).astype(bf16), earlier)
        rank = jnp.where(chosen, rank, -1.0)
        rank_out[...] = rank
        rows = iota((8, OBS), 0)
        values = jnp.where(
            rows == 0,
            cell[...].astype(f32) + 1.0,
            jnp.where(rows == 1, flash[...], jnp.where(rows == 2, sigma[...], 0.0)),
        )
        values = jnp.concatenate([values, jnp.zeros((120, OBS), f32)], axis=0)
        pieces = [
            jnp.concatenate([values[:, i : i + 128].T for i in range(0, OBS, 128)], axis=0)
        ]
        pieces = split3(pieces[0])
        total = jnp.zeros((PEERS, 128), f32)
        for r in range(CAP):
            taken = jnp.where(rank == float(r), 1.0, 0.0).astype(bf16)
            found = (mm(taken, pieces[0]) + mm(taken, pieces[1])) + mm(taken, pieces[2])
            total = total + pltpu.roll(found, REQ + 3 * r, 1)
        msg[...] = total

    rows = pl.ds(pl.multiple_of(b * BLOCK, BLOCK), BLOCK)
    cx = wide(colx[rows, :])
    lanes = iota((BLOCK, YB), 1).astype(f32)
    grow_y = jnp.exp(wide(coly[rows, :]) * lanes)
    running = jnp.zeros((BLOCK, YB), f32)
    place = iota((BLOCK, 128), 1) - 16 * (b // 4)
    sums = jnp.zeros((BLOCK, 128), f32)
    for x in range(XB):
        plane = take_plane((control_a, control_b), x, BLOCK)
        running = running + plane * (grow_y * jnp.exp(cx * float(x)))
        sums = jnp.where(place == x, jnp.sum(running, axis=1, keepdims=True), sums)
    sx[...] = running
    back = pl.ds(pl.multiple_of((b % 4) * BLOCK, BLOCK), BLOCK)
    msg[back, :] = msg[back, :] + sums


def edges(count, control, rates, owner, cell, flash, sigma):
    whole = lambda shape: pl.BlockSpec(shape, lambda b: (0, 0))
    return pl.pallas_call(
        edges_kernel,
        grid=(CH // BLOCK,),
        in_specs=[
            pl.BlockSpec(memory_space=pltpu.SMEM),
            pl.BlockSpec((BLOCK * XB, 128), lambda b: (b, 0)),
            pl.BlockSpec((BLOCK * XB, 128), lambda b: (b, 1)),
            whole((2, CH)),
            whole((1, OBS)),
            whole((1, OBS)),
            whole((1, OBS)),
            whole((1, OBS)),
        ],
        out_specs=[
            pl.BlockSpec((BLOCK, YB), lambda b: (b, 0)),
            whole((PEERS, 128)),
            whole((PEERS, OBS)),
        ],
        out_shape=[
            jax.ShapeDtypeStruct((CH, YB), f32),
            jax.ShapeDtypeStruct((PEERS, 128), f32),
            jax.ShapeDtypeStruct((PEERS, OBS), f32),
        ],
        scratch_shapes=[pltpu.VMEM((CH, 128), f32), pltpu.VMEM((CH, 128), f32)],
        compiler_params=params(),
        name="edges",
    )(count, control, control, rates, owner, cell, flash, sigma)


def local_kernel(control_a, control_b, rates, background_a, background_b, weights, matrix, matrix_t, cc, share, mh, ml, th, tl, colx, coly):
    b = pl.program_id(0)

    @pl.when(b == 0)
    def _():
        colx[...] = column(rates[0:1, :] * (1.0 / 128.0))
        coly[...] = column(rates[1:2, :] * (1.0 / 4096.0))

    rows = pl.ds(pl.multiple_of(b * BLOCK, BLOCK), BLOCK)
    cx = wide(colx[rows, :])
    lanes = iota((BLOCK, YB), 1).astype(f32)
    grow_y = jnp.exp(wide(coly[rows, :]) * lanes)
    running = jnp.zeros((BLOCK, YB), f32)
    sums = upper()
    highs, lows = [], []
    for x in range(XB):
        plane = take_plane((control_a, control_b), x, BLOCK)
        running = running + plane * (grow_y * jnp.exp(cx * float(x)))
        high, low = split(running)
        highs.append(high)
        lows.append(low)
    summed = mm(jnp.concatenate(highs, axis=0), sums) + mm(jnp.concatenate(lows, axis=0), sums)
    cc[...] = summed.reshape(XB, BLOCK, YB)
    for x in range(XB):
        part = jnp.zeros((8, YB), f32)
        for v in range(4):
            part = part + take_plane((background_a, background_b), x, 8, v) * weights[:, v : v + 1]
        share[x] = part
    for i in range(2):
        x = (2 * b + i).astype(f32)
        scaled = matrix[...] * jnp.exp(rates[0:1, :] * (x * (-1.0 / 128.0)))
        mh[i], ml[i] = split(scaled)
        scaled_t = matrix_t[...] * jnp.exp(colx[:, :64] * -x)
        th[i], tl[i] = split(scaled_t)


def local(control, rates, background, weights, matrix, matrix_t):
    whole = lambda shape: pl.BlockSpec(shape, lambda b: (0, 0))
    return pl.pallas_call(
        local_kernel,
        grid=(CH // BLOCK,),
        in_specs=[
            pl.BlockSpec((BLOCK * XB, 128), lambda b: (b, 0)),
            pl.BlockSpec((BLOCK * XB, 128), lambda b: (b, 1)),
            whole((2, CH)),
            pl.BlockSpec((4, 128, 128), lambda b: (0, b, 0)),
            pl.BlockSpec((4, 128, 128), lambda b: (0, b, 1)),
            pl.BlockSpec((8, 4), lambda b: (b, 0)),
            whole((LEVELS, CH)),
            whole((CH, LEVELS)),
        ],
        out_specs=[
            pl.BlockSpec((XB, BLOCK, YB), lambda b: (0, b, 0)),
            pl.BlockSpec((XB, 8, YB), lambda b: (0, b, 0)),
            pl.BlockSpec((2, LEVELS, CH), lambda b: (b, 0, 0)),
            pl.BlockSpec((2, LEVELS, CH), lambda b: (b, 0, 0)),
            pl.BlockSpec((2, CH, LEVELS), lambda b: (b, 0, 0)),
            pl.BlockSpec((2, CH, LEVELS), lambda b: (b, 0, 0)),
        ],
        out_shape=[
            jax.ShapeDtypeStruct((XB, CH, YB), f32),
            jax.ShapeDtypeStruct((XB, LEVELS, YB), f32),
            jax.ShapeDtypeStruct((XB, LEVELS, CH), bf16),
            jax.ShapeDtypeStruct((XB, LEVELS, CH), bf16),
            jax.ShapeDtypeStruct((XB, CH, LEVELS), bf16),
            jax.ShapeDtypeStruct((XB, CH, LEVELS), bf16),
        ],
        scratch_shapes=[pltpu.VMEM((CH, 128), f32), pltpu.VMEM((CH, 128), f32)],
        compiler_params=params(),
        cost_estimate=pl.CostEstimate(flops=2 * 2 * 4096 * 256 * 256, bytes_accessed=15 << 20, transcendentals=1 << 20),
        name="local",
    )(control, control, rates, background, background, weights, matrix, matrix_t)


def carry_kernel(reverse, place, sums, rates, out):
    me = place[2]
    d, e = iota((PEERS, PEERS), 0), iota((PEERS, PEERS), 1)
    far_x = (d // N_Y) - (e // N_Y)
    far_y = (d % N_Y) - (e % N_Y)
    if reverse:
        far_x, far_y = -far_x, -far_y
    fx, fy = far_x.astype(f32), far_y.astype(f32)
    lanes = iota((PEERS, 128), 1)
    left, right = [], []
    for c in range(2):
        mine = iota((2, CH), 1) == me + 128 * c
        rate = jnp.sum(jnp.where(mine, rates[...], 0.0), axis=1, keepdims=True)
        down_x = rate[0:1, :] * (XB / 128.0)
        down_y = rate[1:2, :] * (YB / 4096.0)
        along = jnp.exp(-jnp.maximum(fy, 0.0) * down_y)
        left.append(jnp.where((far_x == 0) & (far_y > 0), along, 0.0))
        across = along * jnp.exp(-jnp.maximum(fx, 0.0) * down_x)
        left.append(jnp.where((far_x > 0) & (far_y > 0), across, 0.0))
        own = (lanes >= 16 * c) & (lanes < 16 * c + 16)
        right.append(jnp.where(own, sums[...], 0.0))
        last = 16 * c if reverse else 16 * c + 15
        total = jnp.sum(jnp.where(lanes == last, sums[...], 0.0), axis=1, keepdims=True)
        right.append(jnp.where(own, total, 0.0))
    out[...] = jnp.dot(
        jnp.concatenate(left, axis=1),
        jnp.concatenate(right, axis=0),
        precision=highest,
        preferred_element_type=f32,
    )


def carry(place, sums, rates, reverse):
    return pl.pallas_call(
        functools.partial(carry_kernel, reverse),
        in_specs=[
            pl.BlockSpec(memory_space=pltpu.SMEM),
            pl.BlockSpec(memory_space=pltpu.VMEM),
            pl.BlockSpec(memory_space=pltpu.VMEM),
        ],
        out_specs=pl.BlockSpec(memory_space=pltpu.VMEM),
        out_shape=jax.ShapeDtypeStruct((PEERS, 128), f32),
        compiler_params=params(),
        name="carry_back" if reverse else "carry",
    )(place, sums, rates)


def entering_rows(place, gathered, colx, reverse):
    mine = place[0]
    total = None
    for g in range(N_X):
        far = (g - mine) if reverse else (mine - g)
        decay = jnp.exp(colx * (-float(XB) * jnp.maximum(far, 0).astype(f32)))
        decay = jnp.where(far > 0, decay, 0.0)
        term = wide(decay) * gathered[g]
        total = term if total is None else total + term
    return total


def observe_kernel(
    place, cc, share, mh, ml, th, tl, gathered, cols, asked, rates, level_weights,
    running_out, sx, msg, lh, ll, forced,
):
    colx = column(rates[0:1, :] * (1.0 / 128.0))
    coly = column(rates[1:2, :] * (1.0 / 4096.0))
    decay_y = jnp.exp(-wide(coly) * iota((CH, YB), 1).astype(f32))
    entering = entering_rows(place, gathered, colx, False)
    high, low = split(entering)
    sums = upper()
    entering = mm(high, sums) + mm(low, sums)

    for x in range(XB):
        col = jnp.concatenate([cols[:, x : x + 1], cols[:, 16 + x : 17 + x]], axis=0)
        smooth = decay_y * ((cc[x] + entering) + col)
        high, low = split(smooth)
        level = (mm(mh[x], high) + (mm(ml[x], high) + mm(mh[x], low))) + share[x]
        lh[x * LEVELS : (x + 1) * LEVELS, :], ll[x * LEVELS : (x + 1) * LEVELS, :] = split(level)

    requests = asked[...].T
    weights = level_weights[...]
    departures = []
    for r in range(0, CAP, 2):
        row = lambda i: jnp.concatenate(
            [requests[REQ + 3 * r + i : REQ + 3 * r + i + 1, :], requests[REQ + 3 * r + 3 + i : REQ + 3 * r + 4 + i, :]], axis=1
        )
        where = row(0).astype(jnp.int32) - 1
        valid = where >= 0
        at_x, at_y = where // YB, where % YB
        at_x = jnp.where(valid, at_x, -1)
        chosen = jnp.where(iota((YB, 256), 0) == at_y, 1.0, 0.0).astype(bf16)
        picked = mm(lh[...], chosen) + mm(ll[...], chosen)
        levels = jnp.zeros((LEVELS, 256), f32)
        for x in range(XB):
            levels = jnp.where(at_x == x, picked[x * LEVELS : (x + 1) * LEVELS, :], levels)
        total = jnp.sum(weights * softplus(levels), axis=0, keepdims=True)
        miss = jnp.where(valid, softplus(total) - row(1), 0.0)
        error = jnp.where(valid, row(2), 1.0)
        scale = miss / (error * error) * sigmoid(total)
        adjoint = scale * (weights * sigmoid(levels))
        high, low = adjoint.astype(bf16).astype(f32), None
        low = adjoint - high
        spread_high = jnp.concatenate([jnp.where(at_x == x, high, 0.0).astype(bf16) for x in range(XB)], axis=0)
        spread_low = jnp.concatenate([jnp.where(at_x == x, low, 0.0).astype(bf16) for x in range(XB)], axis=0)
        part = mm_nt(spread_high, chosen) + mm_nt(spread_low, chosen)
        if r == 0:
            forced[...] = part
        else:
            forced[...] = forced[...] + part
        departures += [miss[:, :128], miss[:, 128:]]

    running = jnp.zeros((CH, YB), f32)
    lanes = iota((PEERS, 128), 1)
    message = pltpu.roll(
        jnp.concatenate(departures + [jnp.zeros((120, 128), f32)], axis=0).T, REQ, 1
    )
    for x in range(XB - 1, -1, -1):
        high, low = split(forced[x * LEVELS : (x + 1) * LEVELS, :])
        back = mm(th[x], high) + (mm(tl[x], high) + mm(th[x], low))
        running = running + back * decay_y
        running_out[x] = running
        total = jnp.sum(running, axis=1, keepdims=True)
        message = jnp.where(lanes == x, total[:128], message)
        message = jnp.where(lanes == 16 + x, total[128:], message)
    sx[...] = running
    msg[...] = message


def observations(place, cc, share, mh, ml, th, tl, gathered, cols, asked, rates, level_weights):
    vmem = pl.BlockSpec(memory_space=pltpu.VMEM)
    return pl.pallas_call(
        observe_kernel,
        in_specs=[pl.BlockSpec(memory_space=pltpu.SMEM)] + [vmem] * 11,
        out_specs=[vmem] * 3,
        out_shape=[
            jax.ShapeDtypeStruct((XB, CH, YB), f32),
            jax.ShapeDtypeStruct((CH, YB), f32),
            jax.ShapeDtypeStruct((PEERS, 128), f32),
        ],
        scratch_shapes=[
            pltpu.VMEM((XB * LEVELS, YB), bf16),
            pltpu.VMEM((XB * LEVELS, YB), bf16),
            pltpu.VMEM((XB * LEVELS, YB), f32),
        ],
        compiler_params=params(),
        name="observations",
    )(place, cc, share, mh, ml, th, tl, gathered, cols, asked, rates, level_weights)


def local_back_kernel(control_a, control_b, running, rates, out, colx, coly):
    b = pl.program_id(0)
    columns_once(rates, colx, coly)
    rows = pl.ds(pl.multiple_of(b * BLOCK, BLOCK), BLOCK)
    high, low = split(running[...].reshape(XB * BLOCK, YB))
    sums = lower()
    summed = mm(high, sums) + mm(low, sums)
    cx = wide(colx[rows, :])
    grow_y = jnp.exp(wide(coly[rows, :]) * iota((BLOCK, YB), 1).astype(f32))
    for x in range(XB):
        scale = grow_y * jnp.exp(cx * float(x))
        plane = take_plane((control_a, control_b), x, BLOCK)
        out[x] = plane + scale * summed[x * BLOCK : (x + 1) * BLOCK, :]


def columns_once(rates, colx, coly):
    @pl.when(pl.program_id(0) == 0)
    def _():
        colx[...] = column(rates[0:1, :] * (1.0 / 128.0))
        coly[...] = column(rates[1:2, :] * (1.0 / 4096.0))


def final_kernel(place, partial, gathered, cols, rates, out, colx, coly, whole_a, whole_b, sems):
    b = pl.program_id(0)
    columns_once(rates, colx, coly)
    rows = pl.ds(pl.multiple_of(b * BLOCK, BLOCK), BLOCK)
    cx = wide(colx[rows, :])
    grow_y = jnp.exp(wide(coly[rows, :]) * iota((BLOCK, YB), 1).astype(f32))
    entering = entering_rows(place, gathered, colx[rows, :], True)
    high, low = split(entering)
    sums = lower()
    entering = mm(high, sums) + mm(low, sums)
    back = pl.ds(pl.multiple_of((b % 4) * BLOCK, BLOCK), BLOCK)
    mine = jnp.where(b < 4, cols[back, :], pltpu.roll(cols[back, :], 112, 1))
    for x in range(XB):
        scale = grow_y * jnp.exp(cx * float(x))
        plane = partial[x] + scale * (entering + mine[:, x : x + 1])
        at = pl.ds(b * (BLOCK * XB) + x, BLOCK, stride=XB)
        whole_a[at, :] = plane[:, :128]
        whole_b[at, :] = plane[:, 128:]

    def copies(step):
        at = pl.ds(pl.multiple_of(step * (BLOCK * XB), BLOCK * XB), BLOCK * XB)
        return (
            pltpu.make_async_copy(whole_a.at[at, :], out.at[at, pl.ds(0, 128)], sems.at[step, 0]),
            pltpu.make_async_copy(whole_b.at[at, :], out.at[at, pl.ds(128, 128)], sems.at[step, 1]),
        )

    for copy in copies(b):
        copy.start()

    @pl.when(b == CH // BLOCK - 1)
    def _():
        for step in range(CH // BLOCK):
            for copy in copies(step):
                copy.wait()


def local_back(control, running, rates):
    return pl.pallas_call(
        local_back_kernel,
        grid=(CH // BLOCK,),
        in_specs=[
            pl.BlockSpec((BLOCK * XB, 128), lambda b: (b, 0)),
            pl.BlockSpec((BLOCK * XB, 128), lambda b: (b, 1)),
            pl.BlockSpec((XB, BLOCK, YB), lambda b: (0, b, 0)),
            pl.BlockSpec((2, CH), lambda b: (0, 0)),
        ],
        out_specs=pl.BlockSpec((XB, BLOCK, YB), lambda b: (0, b, 0)),
        out_shape=jax.ShapeDtypeStruct((XB, CH, YB), f32),
        scratch_shapes=[pltpu.VMEM((CH, 128), f32), pltpu.VMEM((CH, 128), f32)],
        compiler_params=params(),
        cost_estimate=pl.CostEstimate(flops=2 * 2 * 4096 * 256 * 256, bytes_accessed=12 << 20, transcendentals=1 << 20),
        name="local_back",
    )(control, control, running, rates)


def final(place, partial, gathered, cols, rates):
    return pl.pallas_call(
        final_kernel,
        grid=(CH // BLOCK,),
        in_specs=[
            pl.BlockSpec(memory_space=pltpu.SMEM),
            pl.BlockSpec((XB, BLOCK, YB), lambda b: (0, b, 0)),
            pl.BlockSpec((N_X, BLOCK, YB), lambda b: (0, b, 0)),
            pl.BlockSpec((PEERS, 128), lambda b: (0, 0)),
            pl.BlockSpec((2, CH), lambda b: (0, 0)),
        ],
        out_specs=pl.BlockSpec(memory_space=pl.ANY),
        out_shape=jax.ShapeDtypeStruct((CH * XB, YB), f32),
        scratch_shapes=[
            pltpu.VMEM((CH, 128), f32),
            pltpu.VMEM((CH, 128), f32),
            pltpu.VMEM((CH * XB, 128), f32),
            pltpu.VMEM((CH * XB, 128), f32),
            pltpu.SemaphoreType.DMA((CH // BLOCK, 2)),
        ],
        compiler_params=params(),
        name="final",
    )(place, partial, gathered, cols, rates)


def departures_kernel(rank, returned, out):
    total = jnp.zeros((1, OBS), f32)
    for r in range(CAP):
        value = returned[:, REQ + r : REQ + r + 1]
        total = total + jnp.sum(jnp.where(rank[...] == float(r), value, 0.0), axis=0, keepdims=True)
    out[...] = total


def departures(rank, returned):
    vmem = pl.BlockSpec(memory_space=pltpu.VMEM)
    return pl.pallas_call(
        departures_kernel,
        in_specs=[vmem] * 2,
        out_specs=vmem,
        out_shape=jax.ShapeDtypeStruct((1, OBS), f32),
        compiler_params=params(),
        cost_estimate=pl.CostEstimate(flops=1 << 20, bytes_accessed=1 << 19, transcendentals=0),
        name="departures",
    )(rank, returned)


def everywhere(rows):
    shaped = rows.reshape(PEERS, 1, 128)
    return lax.all_to_all(shaped, ("gx", "gy"), split_axis=0, concat_axis=0, tiled=True).reshape(PEERS, 128)


def body(
    control,
    background,
    vert_factor,
    length_rates,
    flash_weights,
    level_weights,
    obs_owner,
    obs_cell,
    obs_count,
    flash_obs,
    obs_error,
):
    shape = control.shape
    gx, gy = lax.axis_index("gx"), lax.axis_index("gy")
    place = jnp.stack([gx, gy, gx * N_Y + gy]).astype(jnp.int32)
    flat = control.reshape(CH * XB, YB)
    rates = length_rates.reshape(2, CH)
    sx, msg, rank = edges(
        obs_count, flat, rates, obs_owner.reshape(1, OBS), obs_cell.reshape(1, OBS),
        flash_obs.reshape(1, OBS), obs_error.reshape(1, OBS),
    )
    asked = everywhere(msg)
    gathered = lax.all_gather(sx, "gx")

    step_x, step_y = length_rates[0] / (XB * N_X), length_rates[1] / (YB * N_Y)
    gain = jnp.sqrt(-jnp.expm1(-2.0 * step_x)) * jnp.sqrt(-jnp.expm1(-2.0 * step_y))
    mixed = flash_weights[:, :, None] * vert_factor * gain[:, None, :]
    matrix = mixed.transpose(1, 0, 2).reshape(LEVELS, CH)
    matrix_t = mixed.transpose(0, 2, 1).reshape(CH, LEVELS)
    cc, share, mh, ml, th, tl = local(
        flat, rates, background.reshape(4, LEVELS * XB, YB), flash_weights.T, matrix, matrix_t
    )
    cols = everywhere(carry(place, asked, rates, False))
    running, sx_back, msg_back = observations(
        place, cc, share, mh, ml, th, tl, gathered, cols, asked, rates, level_weights.reshape(LEVELS, 1)
    )
    returned = everywhere(msg_back)
    gathered_back = lax.all_gather(sx_back, "gx")
    partial = local_back(flat, running, rates)
    cols_back = everywhere(carry(place, returned, rates, True))
    departure = departures(rank, returned)
    grad = final(place, partial, gathered_back, cols_back, rates)
    return (grad.reshape(shape), departure.reshape(OBS))


def solution(mesh):
    placed = (
        P(None, None, "gx", "gy"),
        P(None, None, "gx", "gy"),
        P(),
        P(),
        P(),
        P(),
        P(("gx", "gy"), None),
        P(("gx", "gy")),
        P(("gx", "gy")),
        P(("gx", "gy")),
        P(("gx", "gy")),
    )
    return jax.shard_map(
        body,
        mesh=mesh,
        in_specs=placed,
        out_specs=(P(None, None, "gx", "gy"), P(("gx", "gy"))),
        check_vma=False,
    )
```

```python
import functools

import jax
import jax.numpy as jnp
from jax import lax
from jax.experimental import pallas as pl
from jax.experimental.pallas import tpu as pltpu
from jax.sharding import PartitionSpec as P

highest = lax.Precision.HIGHEST
f32 = jnp.float32
bf16 = jnp.bfloat16

CH, LEVELS, XB, YB = 256, 64, 16, 256
OBS, PEERS, CAP = 512, 128, 8
N_X, N_Y = 8, 16
BLOCK = 32
REQ = 32
ROWS = 5
MIB = 1024 * 1024


def iota(shape, dim):
    return lax.broadcasted_iota(jnp.int32, shape, dim)


def split(value):
    high = value.astype(bf16)
    return high, (value - high.astype(f32)).astype(bf16)


def split3(value):
    high = value.astype(bf16)
    rest = value - high.astype(f32)
    middle = rest.astype(bf16)
    return high, middle, (rest - middle.astype(f32)).astype(bf16)


def mm(a, b):
    return jnp.dot(a, b, preferred_element_type=f32)


def mm_nt(a, b):
    return lax.dot_general(a, b, (((1,), (1,)), ((), ())), preferred_element_type=f32)


def wide(col):
    return jnp.concatenate([col, col], axis=1)


def upper():
    return jnp.where(iota((YB, YB), 0) <= iota((YB, YB), 1), 1.0, 0.0).astype(bf16)


def lower():
    return jnp.where(iota((YB, YB), 0) >= iota((YB, YB), 1), 1.0, 0.0).astype(bf16)


def softplus(x):
    return jnp.maximum(x, 0.0) + jnp.log1p(jnp.exp(-jnp.abs(x)))


def sigmoid(x):
    return 1.0 / (1.0 + jnp.exp(-x))


def take_plane(halves, x, rows, *lead):
    at = lead + (pl.ds(x, rows, stride=XB), slice(None))
    return jnp.concatenate([half[at] for half in halves], axis=1)


def params(mib, **more):
    return pltpu.CompilerParams(vmem_limit_bytes=mib * MIB, **more)


def whole(shape):
    return pl.BlockSpec(shape, lambda b: (0,) * len(shape))


VMEM = pl.BlockSpec(memory_space=pltpu.VMEM)
SMEM = pl.BlockSpec(memory_space=pltpu.SMEM)
ANY = pl.BlockSpec(memory_space=pl.ANY)
CONTROL = [
    pl.BlockSpec((BLOCK * XB, 128), lambda b: (b, 0)),
    pl.BlockSpec((BLOCK * XB, 128), lambda b: (b, 1)),
]
PLANES = pl.BlockSpec((XB, BLOCK, YB), lambda b: (0, b, 0))
STEPS = pl.BlockSpec((BLOCK, 128), lambda b: (b, 0))


def grow(step_y, rows, sign=1.0):
    return jnp.exp(wide(step_y) * (iota((rows, YB), 1).astype(f32) * sign))


def edges_kernel(control_a, control_b, rates, msg, colx, coly, line, tail):
    b = pl.program_id(0)

    @pl.when(b == 0)
    def _():
        for i, (out, count) in enumerate(((colx, 128.0), (coly, 4096.0))):
            for v in range(4):
                line[0:1, 0:LEVELS] = rates[i, v : v + 1, :]
                turned = jnp.broadcast_to(line[0:1, :], (128, 128)).T
                out[v * LEVELS : (v + 1) * LEVELS, :] = turned[0:LEVELS, :] * (1.0 / count)
        tail[...] = jnp.zeros((PEERS, 128), f32)

    rows = pl.ds(pl.multiple_of(b * BLOCK, BLOCK), BLOCK)
    factor = wide(jnp.exp(colx[rows, :]))
    scale = grow(coly[rows, :], BLOCK)
    running = jnp.zeros((BLOCK, YB), f32)
    place = iota((BLOCK, 128), 1) - 16 * (b // 4)
    sums = jnp.zeros((BLOCK, 128), f32)
    for x in range(XB):
        running = running + take_plane((control_a, control_b), x, BLOCK) * scale
        scale = scale * factor
        sums = jnp.where(place == x, jnp.sum(running, axis=1, keepdims=True), sums)
    start = (b % 4) * (BLOCK * ROWS) + 2 * (b // 4)
    msg[pl.ds(start, BLOCK, stride=ROWS), :] = running[:, :128]
    msg[pl.ds(start + 1, BLOCK, stride=ROWS), :] = running[:, 128:]
    back = pl.ds(pl.multiple_of((b % 4) * BLOCK, BLOCK), BLOCK)
    tail[back, :] = tail[back, :] + sums

    @pl.when(b == CH // BLOCK - 1)
    def _():
        msg[pl.ds(4, PEERS, stride=ROWS), :] = tail[...]


def edges(control, length_rates):
    return pl.pallas_call(
        edges_kernel,
        grid=(CH // BLOCK,),
        in_specs=CONTROL + [whole((2, 4, LEVELS))],
        out_specs=[whole((PEERS * ROWS, 128)), whole((CH, 128)), whole((CH, 128))],
        out_shape=[
            jax.ShapeDtypeStruct((PEERS * ROWS, 128), f32),
            jax.ShapeDtypeStruct((CH, 128), f32),
            jax.ShapeDtypeStruct((CH, 128), f32),
        ],
        scratch_shapes=[pltpu.VMEM((8, 128), f32), pltpu.VMEM((PEERS, 128), f32)],
        compiler_params=params(57),
        name="edges",
    )(control, control, length_rates)


def prepare_kernel(place, count, rates, owner, cell, flash, sigma, requests, rank_out, ahead, behind, down):
    live = iota((PEERS, OBS), 1) < count[0]
    chosen = (owner[...] == iota((PEERS, OBS), 0)) & live
    earlier = jnp.where(iota((OBS, OBS), 0) < iota((OBS, OBS), 1), 1.0, 0.0).astype(bf16)
    rank = mm(jnp.where(chosen, 1.0, 0.0).astype(bf16), earlier)
    rank = jnp.where(chosen, rank, -1.0)
    rank_out[...] = rank
    rows = iota((8, OBS), 0)
    values = jnp.where(
        rows == 0,
        cell[...].astype(f32) + 1.0,
        jnp.where(rows == 1, flash[...], jnp.where(rows == 2, sigma[...], 0.0)),
    )
    values = jnp.concatenate([values, jnp.zeros((120, OBS), f32)], axis=0)
    pieces = split3(jnp.concatenate([values[:, i : i + 128].T for i in range(0, OBS, 128)], axis=0))
    total = jnp.zeros((PEERS, 128), f32)
    for r in range(CAP):
        taken = jnp.where(rank == float(r), 1.0, 0.0).astype(bf16)
        found = (mm(taken, pieces[0]) + mm(taken, pieces[1])) + mm(taken, pieces[2])
        total = total + pltpu.roll(found, REQ + 3 * r, 1)
    requests[...] = total

    me = place[2]
    d, e = iota((PEERS, PEERS), 0), iota((PEERS, PEERS), 1)
    far_x = (d // N_Y) - (e // N_Y)
    far_y = (d % N_Y) - (e % N_Y)
    for c in range(2):
        mine = iota((2, CH), 1) == me + 128 * c
        rate = jnp.sum(jnp.where(mine, rates[...], 0.0), axis=1, keepdims=True)
        down_x = rate[0:1, :] * (XB / 128.0)
        down_y = rate[1:2, :] * (YB / 4096.0)
        down[c : c + 1, :] = jnp.broadcast_to(jnp.exp(-down_x), (1, 128))
        along = jnp.exp(-jnp.abs(far_y).astype(f32) * down_y)
        across = along * jnp.exp(-jnp.abs(far_x).astype(f32) * down_x)
        for out, sign in ((ahead, 1), (behind, -1)):
            past_x, past_y = far_x * sign > 0, far_y * sign > 0
            out[:, 256 * c : 256 * c + 128] = jnp.where((far_x == 0) & past_y, along, 0.0)
            out[:, 256 * c + 128 : 256 * c + 256] = jnp.where(past_x & past_y, across, 0.0)
    down[2:8, :] = jnp.zeros((6, 128), f32)


def prepare(place, count, rates, owner, cell, flash, sigma):
    return pl.pallas_call(
        prepare_kernel,
        in_specs=[SMEM, SMEM] + [VMEM] * 5,
        out_specs=[VMEM] * 5,
        out_shape=[
            jax.ShapeDtypeStruct((PEERS, 128), f32),
            jax.ShapeDtypeStruct((PEERS, OBS), f32),
            jax.ShapeDtypeStruct((PEERS, 4 * 128), f32),
            jax.ShapeDtypeStruct((PEERS, 4 * 128), f32),
            jax.ShapeDtypeStruct((8, 128), f32),
        ],
        compiler_params=params(16),
        cost_estimate=pl.CostEstimate(flops=1 << 30, bytes_accessed=1 << 20, transcendentals=1 << 16),
        name="prepare",
    )(place, count, rates, owner, cell, flash, sigma)


def local_kernel(
    control_a, control_b, colx, coly, rates, background_a, background_b, weights, matrix, matrix_t, steps,
    cc, share, mh, ml, th, tl,
):
    b = pl.program_id(0)
    factor = wide(jnp.exp(colx[...]))
    scale = grow(coly[...], BLOCK)
    running = jnp.zeros((BLOCK, YB), f32)
    sums = upper()
    highs, lows = [], []
    for x in range(XB):
        running = running + take_plane((control_a, control_b), x, BLOCK) * scale
        scale = scale * factor
        high, low = split(running)
        highs.append(high)
        lows.append(low)
    summed = mm(jnp.concatenate(highs, axis=0), sums) + mm(jnp.concatenate(lows, axis=0), sums)
    cc[...] = summed.reshape(XB, BLOCK, YB)
    for x in range(XB):
        part = jnp.zeros((8, YB), f32)
        for v in range(4):
            part = part + take_plane((background_a, background_b), x, 8, v) * weights[:, v : v + 1]
        share[x] = part
    for i in range(2):
        x = (2 * b + i).astype(f32)
        mh[i], ml[i] = split(matrix[...] * jnp.exp(rates[0:1, :] * (x * (-1.0 / 128.0))))
        th[i], tl[i] = split(matrix_t[...] * jnp.exp(steps[:, :LEVELS] * -x))


def local(control, colx, coly, rates, background, weights, matrix, matrix_t):
    return pl.pallas_call(
        local_kernel,
        grid=(CH // BLOCK,),
        in_specs=CONTROL
        + [
            STEPS,
            STEPS,
            whole((2, CH)),
            pl.BlockSpec((4, 128, 128), lambda b: (0, b, 0)),
            pl.BlockSpec((4, 128, 128), lambda b: (0, b, 1)),
            pl.BlockSpec((8, 4), lambda b: (b, 0)),
            whole((LEVELS, CH)),
            whole((CH, LEVELS)),
            whole((CH, 128)),
        ],
        out_specs=[
            PLANES,
            pl.BlockSpec((XB, 8, YB), lambda b: (0, b, 0)),
            pl.BlockSpec((2, LEVELS, CH), lambda b: (b, 0, 0)),
            pl.BlockSpec((2, LEVELS, CH), lambda b: (b, 0, 0)),
            pl.BlockSpec((2, CH, LEVELS), lambda b: (b, 0, 0)),
            pl.BlockSpec((2, CH, LEVELS), lambda b: (b, 0, 0)),
        ],
        out_shape=[
            jax.ShapeDtypeStruct((XB, CH, YB), f32),
            jax.ShapeDtypeStruct((XB, LEVELS, YB), f32),
            jax.ShapeDtypeStruct((XB, LEVELS, CH), bf16),
            jax.ShapeDtypeStruct((XB, LEVELS, CH), bf16),
            jax.ShapeDtypeStruct((XB, CH, LEVELS), bf16),
            jax.ShapeDtypeStruct((XB, CH, LEVELS), bf16),
        ],
        compiler_params=params(57),
        cost_estimate=pl.CostEstimate(flops=2 * 2 * 4096 * 256 * 256, bytes_accessed=15 << 20, transcendentals=1 << 20),
        name="local",
    )(control, control, colx, coly, rates, background, background, weights, matrix, matrix_t, colx)


def carry_kernel(reverse, sums, weights, down, requests, out):
    order = list(range(N_X))
    if reverse:
        order = order[::-1]
    for row in range(4):
        decay = down[row // 2 : row // 2 + 1, :]
        total = jnp.zeros((N_Y, 128), f32)
        for g in order:
            at = pl.ds(g * N_Y * ROWS + row, N_Y, stride=ROWS)
            out[at, :] = total
            total = decay * (total + sums[at, :])
    tail = sums[pl.ds(4, PEERS, stride=ROWS), :]
    lanes = iota((PEERS, 128), 1)
    right = []
    for c in range(2):
        own = (lanes >= 16 * c) & (lanes < 16 * c + 16)
        right.append(jnp.where(own, tail, 0.0))
        last = 16 * c if reverse else 16 * c + 15
        total = jnp.sum(jnp.where(lanes == last, tail, 0.0), axis=1, keepdims=True)
        right.append(jnp.where(own, total, 0.0))
    entering = jnp.dot(
        weights[...], jnp.concatenate(right, axis=0), precision=highest, preferred_element_type=f32
    )
    if requests is not None:
        entering = entering + requests[...]
    out[pl.ds(4, PEERS, stride=ROWS), :] = entering


def carry(sums, weights, down, requests=None):
    shape = jax.ShapeDtypeStruct((PEERS * ROWS, 128), f32)
    if requests is None:
        kernel = lambda *refs: carry_kernel(True, *refs[:3], None, refs[3])
        return pl.pallas_call(
            kernel, in_specs=[VMEM] * 3, out_specs=VMEM, out_shape=shape,
            compiler_params=params(8), name="carry_back",
        )(sums, weights, down)
    return pl.pallas_call(
        functools.partial(carry_kernel, False), in_specs=[VMEM] * 4, out_specs=VMEM, out_shape=shape,
        compiler_params=params(8), name="carry",
    )(sums, weights, down, requests)


def observe_kernel(
    cc_hbm, share_hbm, mh_hbm, ml_hbm, th, tl, entered, coly, level_weights,
    running_hbm, msg, lh, ll, forced, cc, share, mh, ml, running_out, sems, out_sems,
):
    def arrivals(x):
        return [
            pltpu.make_async_copy(source.at[x], target.at[x], sems.at[x, i])
            for i, (source, target) in enumerate(
                ((cc_hbm, cc), (share_hbm, share), (mh_hbm, mh), (ml_hbm, ml))
            )
        ]

    for x in range(XB):
        for copy in arrivals(x):
            copy.start()

    decay_y = grow(coly[...], CH, -1.0)
    entering = jnp.concatenate(
        [
            jnp.concatenate(
                [entered[pl.ds(2 * c + h, PEERS, stride=ROWS), :] for h in range(2)], axis=1
            )
            for c in range(2)
        ],
        axis=0,
    )
    tail = entered[pl.ds(4, PEERS, stride=ROWS), :]
    high, low = split(entering)
    sums = upper()
    entering = mm(high, sums) + mm(low, sums)

    for x in range(XB):
        for copy in arrivals(x):
            copy.wait()
        col = jnp.concatenate([tail[:, x : x + 1], tail[:, 16 + x : 17 + x]], axis=0)
        smooth = decay_y * ((cc[x] + entering) + col)
        high, low = split(smooth)
        level = (mm(mh[x], high) + (mm(ml[x], high) + mm(mh[x], low))) + share[x]
        at = slice(x * LEVELS, (x + 1) * LEVELS)
        lh[at, :], ll[at, :] = split(level)

    requests = tail.T
    weights = level_weights[...]
    departures = []
    for r in range(0, CAP, 2):
        first, second = REQ + 3 * r, REQ + 3 * r + 3
        row = lambda i: jnp.concatenate(
            [requests[first + i : first + i + 1, :], requests[second + i : second + i + 1, :]], axis=1
        )
        where = row(0).astype(jnp.int32) - 1
        valid = where >= 0
        at_x, at_y = where // YB, where % YB
        at_x = jnp.where(valid, at_x, -1)
        chosen = jnp.where(iota((YB, 256), 0) == at_y, 1.0, 0.0).astype(bf16)
        picked = mm(lh[...], chosen) + mm(ll[...], chosen)
        levels = jnp.zeros((LEVELS, 256), f32)
        for x in range(XB):
            levels = jnp.where(at_x == x, picked[x * LEVELS : (x + 1) * LEVELS, :], levels)
        total = jnp.sum(weights * softplus(levels), axis=0, keepdims=True)
        miss = jnp.where(valid, softplus(total) - row(1), 0.0)
        error = jnp.where(valid, row(2), 1.0)
        scale = miss / (error * error) * sigmoid(total)
        adjoint = scale * (weights * sigmoid(levels))
        high = adjoint.astype(bf16).astype(f32)
        low = adjoint - high
        spread_high = jnp.concatenate([jnp.where(at_x == x, high, 0.0).astype(bf16) for x in range(XB)], axis=0)
        spread_low = jnp.concatenate([jnp.where(at_x == x, low, 0.0).astype(bf16) for x in range(XB)], axis=0)
        part = mm_nt(spread_high, chosen) + mm_nt(spread_low, chosen)
        if r == 0:
            forced[...] = part
        else:
            forced[...] = forced[...] + part
        departures += [miss[:, :128], miss[:, 128:]]

    def leaving(x):
        return pltpu.make_async_copy(running_out.at[x], running_hbm.at[x], out_sems.at[x])

    running = jnp.zeros((CH, YB), f32)
    lanes = iota((PEERS, 128), 1)
    message = pltpu.roll(
        jnp.concatenate(departures + [jnp.zeros((120, 128), f32)], axis=0).T, REQ, 1
    )
    for x in range(XB - 1, -1, -1):
        high, low = split(forced[x * LEVELS : (x + 1) * LEVELS, :])
        back = mm(th[x], high) + (mm(tl[x], high) + mm(th[x], low))
        running = running + back * decay_y
        running_out[x] = running
        leaving(x).start()
        total = jnp.sum(running, axis=1, keepdims=True)
        message = jnp.where(lanes == x, total[:128], message)
        message = jnp.where(lanes == 16 + x, total[128:], message)
    for c in range(2):
        for h in range(2):
            msg[pl.ds(2 * c + h, PEERS, stride=ROWS), :] = running[128 * c : 128 * c + 128, 128 * h : 128 * h + 128]
    msg[pl.ds(4, PEERS, stride=ROWS), :] = message
    for x in range(XB):
        leaving(x).wait()


def observations(cc, share, mh, ml, th, tl, entered, coly, level_weights):
    return pl.pallas_call(
        observe_kernel,
        in_specs=[ANY] * 4 + [VMEM] * 5,
        out_specs=[ANY, VMEM],
        out_shape=[
            jax.ShapeDtypeStruct((XB, CH, YB), f32),
            jax.ShapeDtypeStruct((PEERS * ROWS, 128), f32),
        ],
        scratch_shapes=[
            pltpu.VMEM((XB * LEVELS, YB), bf16),
            pltpu.VMEM((XB * LEVELS, YB), bf16),
            pltpu.VMEM((XB * LEVELS, YB), f32),
            pltpu.VMEM((XB, CH, YB), f32),
            pltpu.VMEM((XB, LEVELS, YB), f32),
            pltpu.VMEM((XB, LEVELS, CH), bf16),
            pltpu.VMEM((XB, LEVELS, CH), bf16),
            pltpu.VMEM((XB, CH, YB), f32),
            pltpu.SemaphoreType.DMA((XB, 4)),
            pltpu.SemaphoreType.DMA((XB,)),
        ],
        compiler_params=params(57),
        name="observations",
    )(cc, share, mh, ml, th, tl, entered, coly, level_weights)


def local_back_kernel(control_a, control_b, running, colx, coly, out):
    high, low = split(running[...].reshape(XB * BLOCK, YB))
    sums = lower()
    summed = mm(high, sums) + mm(low, sums)
    factor = wide(jnp.exp(colx[...]))
    scale = grow(coly[...], BLOCK)
    for x in range(XB):
        plane = take_plane((control_a, control_b), x, BLOCK)
        out[x] = plane + scale * summed[x * BLOCK : (x + 1) * BLOCK, :]
        scale = scale * factor


def local_back(control, running, colx, coly):
    return pl.pallas_call(
        local_back_kernel,
        grid=(CH // BLOCK,),
        in_specs=CONTROL + [PLANES, STEPS, STEPS],
        out_specs=PLANES,
        out_shape=jax.ShapeDtypeStruct((XB, CH, YB), f32),
        compiler_params=params(57),
        cost_estimate=pl.CostEstimate(flops=2 * 2 * 4096 * 256 * 256, bytes_accessed=12 << 20, transcendentals=1 << 20),
        name="local_back",
    )(control, control, running, colx, coly)


def final_kernel(partial, entered, colx, coly, out, whole_a, whole_b, sems):
    b = pl.program_id(0)
    start = (b % 4) * (BLOCK * ROWS)
    entering = jnp.concatenate(
        [entered[pl.ds(start + 2 * (b // 4) + h, BLOCK, stride=ROWS), :] for h in range(2)], axis=1
    )
    high, low = split(entering)
    sums = lower()
    entering = mm(high, sums) + mm(low, sums)
    tail = entered[pl.ds(start + 4, BLOCK, stride=ROWS), :]
    mine = jnp.where(b < 4, tail, pltpu.roll(tail, 112, 1))
    factor = wide(jnp.exp(colx[...]))
    scale = grow(coly[...], BLOCK)
    for x in range(XB):
        plane = partial[x] + scale * (entering + mine[:, x : x + 1])
        scale = scale * factor
        at = pl.ds(b * (BLOCK * XB) + x, BLOCK, stride=XB)
        whole_a[at, :] = plane[:, :128]
        whole_b[at, :] = plane[:, 128:]

    def copies(step):
        at = pl.ds(pl.multiple_of(step * (BLOCK * XB), BLOCK * XB), BLOCK * XB)
        return (
            pltpu.make_async_copy(whole_a.at[at, :], out.at[at, pl.ds(0, 128)], sems.at[step, 0]),
            pltpu.make_async_copy(whole_b.at[at, :], out.at[at, pl.ds(128, 128)], sems.at[step, 1]),
        )

    for copy in copies(b):
        copy.start()

    @pl.when(b == CH // BLOCK - 1)
    def _():
        for step in range(CH // BLOCK):
            for copy in copies(step):
                copy.wait()


def final(partial, entered, colx, coly):
    return pl.pallas_call(
        final_kernel,
        grid=(CH // BLOCK,),
        in_specs=[PLANES, whole((PEERS * ROWS, 128)), STEPS, STEPS],
        out_specs=ANY,
        out_shape=jax.ShapeDtypeStruct((CH * XB, YB), f32),
        scratch_shapes=[
            pltpu.VMEM((CH * XB, 128), f32),
            pltpu.VMEM((CH * XB, 128), f32),
            pltpu.SemaphoreType.DMA((CH // BLOCK, 2)),
        ],
        compiler_params=params(57),
        name="final",
    )(partial, entered, colx, coly)


def departures_kernel(rank, returned, out):
    total = jnp.zeros((1, OBS), f32)
    values = returned[pl.ds(4, PEERS, stride=ROWS), :]
    for r in range(CAP):
        value = values[:, REQ + r : REQ + r + 1]
        total = total + jnp.sum(jnp.where(rank[...] == float(r), value, 0.0), axis=0, keepdims=True)
    out[...] = total


def departures(rank, returned):
    return pl.pallas_call(
        departures_kernel,
        in_specs=[VMEM] * 2,
        out_specs=VMEM,
        out_shape=jax.ShapeDtypeStruct((1, OBS), f32),
        compiler_params=params(8),
        cost_estimate=pl.CostEstimate(flops=1 << 20, bytes_accessed=1 << 19, transcendentals=0),
        name="departures",
    )(rank, returned)


def everywhere(rows):
    shaped = rows.reshape(PEERS * ROWS, 1, 128)
    moved = lax.all_to_all(shaped, ("gx", "gy"), split_axis=0, concat_axis=0, tiled=True)
    return moved.reshape(PEERS * ROWS, 128)


def body(
    control,
    background,
    vert_factor,
    length_rates,
    flash_weights,
    level_weights,
    obs_owner,
    obs_cell,
    obs_count,
    flash_obs,
    obs_error,
):
    shape = control.shape
    flat = control.reshape(CH * XB, YB)
    msg, colx, coly = edges(flat, length_rates)
    asked = everywhere(msg)

    gx, gy = lax.axis_index("gx"), lax.axis_index("gy")
    place = jnp.stack([gx, gy, gx * N_Y + gy]).astype(jnp.int32)
    rates = length_rates.reshape(2, CH)
    requests, rank, ahead, behind, down = prepare(
        place, obs_count, rates, obs_owner.reshape(1, OBS), obs_cell.reshape(1, OBS),
        flash_obs.reshape(1, OBS), obs_error.reshape(1, OBS),
    )
    step_x, step_y = length_rates[0] / (XB * N_X), length_rates[1] / (YB * N_Y)
    gain = jnp.sqrt(-jnp.expm1(-2.0 * step_x)) * jnp.sqrt(-jnp.expm1(-2.0 * step_y))
    mixed = flash_weights[:, :, None] * vert_factor * gain[:, None, :]
    matrix = mixed.transpose(1, 0, 2).reshape(LEVELS, CH)
    matrix_t = mixed.transpose(0, 2, 1).reshape(CH, LEVELS)
    cc, share, mh, ml, th, tl = local(
        flat, colx, coly, rates, background.reshape(4, LEVELS * XB, YB), flash_weights.T, matrix, matrix_t
    )
    entered = everywhere(carry(asked, ahead, down, requests))
    running, msg_back = observations(
        cc, share, mh, ml, th, tl, entered, coly, level_weights.reshape(LEVELS, 1)
    )
    returned = everywhere(msg_back)
    partial = local_back(flat, running, colx, coly)
    entered_back = everywhere(carry(returned, behind, down))
    departure = departures(rank, returned)
    grad = final(partial, entered_back, colx, coly)
    return (grad.reshape(shape), departure.reshape(OBS))


def solution(mesh):
    placed = (
        P(None, None, "gx", "gy"),
        P(None, None, "gx", "gy"),
        P(),
        P(),
        P(),
        P(),
        P(("gx", "gy"), None),
        P(("gx", "gy")),
        P(("gx", "gy")),
        P(("gx", "gy")),
        P(("gx", "gy")),
    )
    return jax.shard_map(
        body,
        mesh=mesh,
        in_specs=placed,
        out_specs=(P(None, None, "gx", "gy"), P(("gx", "gy"))),
        check_vma=False,
    )
```

```python
import functools

import jax
import jax.numpy as jnp
from jax import lax
from jax.experimental import pallas as pl
from jax.experimental.pallas import tpu as pltpu
from jax.sharding import PartitionSpec as P

highest = lax.Precision.HIGHEST
f32 = jnp.float32
bf16 = jnp.bfloat16

CH, LEVELS, XB, YB = 256, 64, 16, 256
OBS, PEERS, CAP = 512, 128, 8
N_X, N_Y = 8, 16
BLOCK = 32
REQ = 32
ROWS = 5
MIB = 1024 * 1024


def iota(shape, dim):
    return lax.broadcasted_iota(jnp.int32, shape, dim)


def split(value):
    high = value.astype(bf16)
    return high, (value - high.astype(f32)).astype(bf16)


def split3(value):
    high = value.astype(bf16)
    rest = value - high.astype(f32)
    middle = rest.astype(bf16)
    return high, middle, (rest - middle.astype(f32)).astype(bf16)


def mm(a, b):
    return jnp.dot(a, b, preferred_element_type=f32)


def mm_nt(a, b):
    return lax.dot_general(a, b, (((1,), (1,)), ((), ())), preferred_element_type=f32)


def wide(col):
    return jnp.concatenate([col, col], axis=1)


def upper():
    return jnp.where(iota((YB, YB), 0) <= iota((YB, YB), 1), 1.0, 0.0).astype(bf16)


def lower():
    return jnp.where(iota((YB, YB), 0) >= iota((YB, YB), 1), 1.0, 0.0).astype(bf16)


def softplus(x):
    return jnp.maximum(x, 0.0) + jnp.log1p(jnp.exp(-jnp.abs(x)))


def sigmoid(x):
    return 1.0 / (1.0 + jnp.exp(-x))


def take_plane(halves, x, rows, *lead):
    at = lead + (pl.ds(x, rows, stride=XB), slice(None))
    return jnp.concatenate([half[at] for half in halves], axis=1)


def params(mib, **more):
    return pltpu.CompilerParams(vmem_limit_bytes=mib * MIB, **more)


def whole(shape):
    return pl.BlockSpec(shape, lambda b: (0,) * len(shape))


VMEM = pl.BlockSpec(memory_space=pltpu.VMEM)
SMEM = pl.BlockSpec(memory_space=pltpu.SMEM)
ANY = pl.BlockSpec(memory_space=pl.ANY)
CONTROL = [
    pl.BlockSpec((BLOCK * XB, 128), lambda b: (b, 0)),
    pl.BlockSpec((BLOCK * XB, 128), lambda b: (b, 1)),
]
PLANES = pl.BlockSpec((XB, BLOCK, YB), lambda b: (0, b, 0))
STEPS = pl.BlockSpec((BLOCK, 128), lambda b: (b, 0))


def grow(step_y, rows, sign=1.0):
    return jnp.exp(wide(step_y) * (iota((rows, YB), 1).astype(f32) * sign))


def edges_kernel(control_a, control_b, rates, msg, colx, coly, line, tail):
    b = pl.program_id(0)

    @pl.when(b == 0)
    def _():
        for i, (out, count) in enumerate(((colx, 128.0), (coly, 4096.0))):
            for v in range(4):
                line[0:1, 0:LEVELS] = rates[i, v : v + 1, :]
                turned = jnp.broadcast_to(line[0:1, :], (128, 128)).T
                out[v * LEVELS : (v + 1) * LEVELS, :] = turned[0:LEVELS, :] * (1.0 / count)
        tail[...] = jnp.zeros((PEERS, 128), f32)

    rows = pl.ds(pl.multiple_of(b * BLOCK, BLOCK), BLOCK)
    factor = wide(jnp.exp(colx[rows, :]))
    scale = grow(coly[rows, :], BLOCK)
    running = jnp.zeros((BLOCK, YB), f32)
    place = iota((BLOCK, 128), 1) - 16 * (b // 4)
    sums = jnp.zeros((BLOCK, 128), f32)
    for x in range(XB):
        running = running + take_plane((control_a, control_b), x, BLOCK) * scale
        scale = scale * factor
        sums = jnp.where(place == x, jnp.sum(running, axis=1, keepdims=True), sums)
    start = (b % 4) * (BLOCK * ROWS) + 2 * (b // 4)
    msg[pl.ds(start, BLOCK, stride=ROWS), :] = running[:, :128]
    msg[pl.ds(start + 1, BLOCK, stride=ROWS), :] = running[:, 128:]
    back = pl.ds(pl.multiple_of((b % 4) * BLOCK, BLOCK), BLOCK)
    tail[back, :] = tail[back, :] + sums

    @pl.when(b == CH // BLOCK - 1)
    def _():
        msg[pl.ds(4, PEERS, stride=ROWS), :] = tail[...]


def edges(control, length_rates):
    return pl.pallas_call(
        edges_kernel,
        grid=(CH // BLOCK,),
        in_specs=CONTROL + [whole((2, 4, LEVELS))],
        out_specs=[whole((PEERS * ROWS, 128)), whole((CH, 128)), whole((CH, 128))],
        out_shape=[
            jax.ShapeDtypeStruct((PEERS * ROWS, 128), f32),
            jax.ShapeDtypeStruct((CH, 128), f32),
            jax.ShapeDtypeStruct((CH, 128), f32),
        ],
        scratch_shapes=[pltpu.VMEM((8, 128), f32), pltpu.VMEM((PEERS, 128), f32)],
        compiler_params=params(57),
        name="edges",
    )(control, control, length_rates)


def prepare_kernel(place, count, rates, owner, cell, flash, sigma, requests, rank_out, ahead, behind, down):
    live = iota((PEERS, OBS), 1) < count[0]
    chosen = (owner[...] == iota((PEERS, OBS), 0)) & live
    earlier = jnp.where(iota((OBS, OBS), 0) < iota((OBS, OBS), 1), 1.0, 0.0).astype(bf16)
    rank = mm(jnp.where(chosen, 1.0, 0.0).astype(bf16), earlier)
    rank = jnp.where(chosen, rank, -1.0)
    rank_out[...] = rank
    rows = iota((8, OBS), 0)
    values = jnp.where(
        rows == 0,
        cell[...].astype(f32) + 1.0,
        jnp.where(rows == 1, flash[...], jnp.where(rows == 2, sigma[...], 0.0)),
    )
    values = jnp.concatenate([values, jnp.zeros((120, OBS), f32)], axis=0)
    pieces = split3(jnp.concatenate([values[:, i : i + 128].T for i in range(0, OBS, 128)], axis=0))
    total = jnp.zeros((PEERS, 128), f32)
    for r in range(CAP):
        taken = jnp.where(rank == float(r), 1.0, 0.0).astype(bf16)
        found = (mm(taken, pieces[0]) + mm(taken, pieces[1])) + mm(taken, pieces[2])
        total = total + pltpu.roll(found, REQ + 3 * r, 1)
    requests[...] = total

    me = place[2]
    d, e = iota((PEERS, PEERS), 0), iota((PEERS, PEERS), 1)
    far_x = (d // N_Y) - (e // N_Y)
    far_y = (d % N_Y) - (e % N_Y)
    for c in range(2):
        mine = iota((2, CH), 1) == me + 128 * c
        rate = jnp.sum(jnp.where(mine, rates[...], 0.0), axis=1, keepdims=True)
        down_x = rate[0:1, :] * (XB / 128.0)
        down_y = rate[1:2, :] * (YB / 4096.0)
        down[c : c + 1, :] = jnp.broadcast_to(jnp.exp(-down_x), (1, 128))
        along = jnp.exp(-jnp.abs(far_y).astype(f32) * down_y)
        across = along * jnp.exp(-jnp.abs(far_x).astype(f32) * down_x)
        for out, sign in ((ahead, 1), (behind, -1)):
            past_x, past_y = far_x * sign > 0, far_y * sign > 0
            out[:, 256 * c : 256 * c + 128] = jnp.where((far_x == 0) & past_y, along, 0.0)
            out[:, 256 * c + 128 : 256 * c + 256] = jnp.where(past_x & past_y, across, 0.0)
    down[2:8, :] = jnp.zeros((6, 128), f32)


def prepare(place, count, rates, owner, cell, flash, sigma):
    return pl.pallas_call(
        prepare_kernel,
        in_specs=[SMEM, SMEM] + [VMEM] * 5,
        out_specs=[VMEM] * 5,
        out_shape=[
            jax.ShapeDtypeStruct((PEERS, 128), f32),
            jax.ShapeDtypeStruct((PEERS, OBS), f32),
            jax.ShapeDtypeStruct((PEERS, 4 * 128), f32),
            jax.ShapeDtypeStruct((PEERS, 4 * 128), f32),
            jax.ShapeDtypeStruct((8, 128), f32),
        ],
        compiler_params=params(16),
        cost_estimate=pl.CostEstimate(flops=1 << 30, bytes_accessed=1 << 20, transcendentals=1 << 16),
        name="prepare",
    )(place, count, rates, owner, cell, flash, sigma)


def local_kernel(control_a, control_b, colx, coly, cc):
    factor = wide(jnp.exp(colx[...]))
    scale = grow(coly[...], BLOCK)
    running = jnp.zeros((BLOCK, YB), f32)
    sums = upper()
    highs, lows = [], []
    for x in range(XB):
        running = running + take_plane((control_a, control_b), x, BLOCK) * scale
        scale = scale * factor
        high, low = split(running)
        highs.append(high)
        lows.append(low)
    summed = mm(jnp.concatenate(highs, axis=0), sums) + mm(jnp.concatenate(lows, axis=0), sums)
    cc[...] = summed.reshape(XB, BLOCK, YB)


def local(control, colx, coly):
    return pl.pallas_call(
        local_kernel,
        grid=(CH // BLOCK,),
        in_specs=CONTROL + [STEPS, STEPS],
        out_specs=PLANES,
        out_shape=jax.ShapeDtypeStruct((XB, CH, YB), f32),
        compiler_params=params(57),
        cost_estimate=pl.CostEstimate(flops=2 * 2 * 4096 * 256 * 256, bytes_accessed=8 << 20, transcendentals=1 << 16),
        name="local",
    )(control, control, colx, coly)


def share_kernel(background_a, background_b, weights, share):
    for x in range(XB):
        part = jnp.zeros((8, YB), f32)
        for v in range(4):
            part = part + take_plane((background_a, background_b), x, 8, v) * weights[:, v : v + 1]
        share[x] = part


def background_share(background, weights):
    return pl.pallas_call(
        share_kernel,
        grid=(8,),
        in_specs=[
            pl.BlockSpec((4, 128, 128), lambda b: (0, b, 0)),
            pl.BlockSpec((4, 128, 128), lambda b: (0, b, 1)),
            pl.BlockSpec((8, 4), lambda b: (b, 0)),
        ],
        out_specs=pl.BlockSpec((XB, 8, YB), lambda b: (0, b, 0)),
        out_shape=jax.ShapeDtypeStruct((XB, LEVELS, YB), f32),
        compiler_params=params(57),
        cost_estimate=pl.CostEstimate(flops=1 << 21, bytes_accessed=5 << 20, transcendentals=0),
        name="share",
    )(background, background, weights)


def levels_kernel(cc, share, coly, rates, matrix, level, scaled, turned_high, turned_low, decay):
    b = pl.program_id(0)

    @pl.when(b == 0)
    def _():
        decay[...] = grow(coly[...], CH, -1.0)

    for i in range(2):
        x = (2 * b + i).astype(f32)
        at = slice(i * LEVELS, (i + 1) * LEVELS)
        part = matrix[...] * jnp.exp(rates[0:1, :] * (x * (-1.0 / 128.0)))
        scaled[at, :] = part
        mh, ml = split(part)
        high, low = split(decay[...] * cc[i])
        level[at, :] = (mm(mh, high) + (mm(ml, high) + mm(mh, low))) + share[i]
    turned = jnp.concatenate([scaled[:, :128].T, scaled[:, 128:].T], axis=0)
    turned_high[...], turned_low[...] = split(turned)


def levels_of(cc, share, coly, rates, matrix):
    two = lambda shape: pl.BlockSpec(shape, lambda b: (b,) + (0,) * (len(shape) - 1))
    lanes = pl.BlockSpec((CH, 128), lambda b: (0, b))
    return pl.pallas_call(
        levels_kernel,
        grid=(XB // 2,),
        in_specs=[two((2, CH, YB)), two((2, LEVELS, YB)), whole((CH, 128)), whole((2, CH)), whole((LEVELS, CH))],
        out_specs=[two((128, YB)), two((128, CH)), lanes, lanes],
        out_shape=[
            jax.ShapeDtypeStruct((XB * LEVELS, YB), f32),
            jax.ShapeDtypeStruct((XB * LEVELS, CH), f32),
            jax.ShapeDtypeStruct((CH, XB * LEVELS), bf16),
            jax.ShapeDtypeStruct((CH, XB * LEVELS), bf16),
        ],
        scratch_shapes=[pltpu.VMEM((CH, YB), f32)],
        compiler_params=params(57),
        cost_estimate=pl.CostEstimate(flops=2 * 3 * 1024 * 256 * 256, bytes_accessed=8 << 20, transcendentals=1 << 18),
        name="levels",
    )(cc, share, coly, rates, matrix)


def carry_kernel(reverse, sums, weights, down, requests, out):
    order = list(range(N_X))
    if reverse:
        order = order[::-1]
    for row in range(4):
        decay = down[row // 2 : row // 2 + 1, :]
        total = jnp.zeros((N_Y, 128), f32)
        for g in order:
            at = pl.ds(g * N_Y * ROWS + row, N_Y, stride=ROWS)
            out[at, :] = total
            total = decay * (total + sums[at, :])
    tail = sums[pl.ds(4, PEERS, stride=ROWS), :]
    lanes = iota((PEERS, 128), 1)
    right = []
    for c in range(2):
        own = (lanes >= 16 * c) & (lanes < 16 * c + 16)
        right.append(jnp.where(own, tail, 0.0))
        last = 16 * c if reverse else 16 * c + 15
        total = jnp.sum(jnp.where(lanes == last, tail, 0.0), axis=1, keepdims=True)
        right.append(jnp.where(own, total, 0.0))
    entering = jnp.dot(
        weights[...], jnp.concatenate(right, axis=0), precision=highest, preferred_element_type=f32
    )
    if requests is not None:
        entering = entering + requests[...]
    out[pl.ds(4, PEERS, stride=ROWS), :] = entering


def carry(sums, weights, down, requests=None):
    shape = jax.ShapeDtypeStruct((PEERS * ROWS, 128), f32)
    if requests is None:
        kernel = lambda *refs: carry_kernel(True, *refs[:3], None, refs[3])
        return pl.pallas_call(
            kernel, in_specs=[VMEM] * 3, out_specs=VMEM, out_shape=shape,
            compiler_params=params(8), name="carry_back",
        )(sums, weights, down)
    return pl.pallas_call(
        functools.partial(carry_kernel, False), in_specs=[VMEM] * 4, out_specs=VMEM, out_shape=shape,
        compiler_params=params(8), name="carry",
    )(sums, weights, down, requests)


def stack_rows(*parts):
    return jnp.concatenate(parts, axis=0)


def stack_lanes(*parts):
    return jnp.concatenate(parts, axis=1)


def observe_kernel(
    level, scaled, turned_high, turned_low, entered, coly, rates, level_weights,
    forced_out, msg, left, both, spread, marks,
):
    decay_y = grow(coly[...], CH, -1.0)
    pick = lambda row: entered[pl.ds(row, PEERS, stride=ROWS), :]
    high, low = split(stack_rows(stack_lanes(pick(0), pick(1)), stack_lanes(pick(2), pick(3))))
    sums = upper()
    eh, el = split(decay_y * (mm(high, sums) + mm(low, sums)))
    dh, dl = split(decay_y)
    requests = pick(4).T
    for x in range(XB):
        at = slice(x * LEVELS, (x + 1) * LEVELS)
        part = scaled[at, :]
        high, low = split(part)
        left[at, 0:256], left[at, 256:512], left[at, 512:768] = high, low, high
        col = stack_lanes(requests[x : x + 1, :], requests[16 + x : 17 + x, :])
        high, low = split(part * col)
        left[at, 768:1024], left[at, 1024:1280], left[at, 1280:1536] = high, low, high
    total = level[...] + mm(left[...], stack_rows(eh, eh, el, dh, dh, dl))
    both[:, 0:256], both[:, 256:512] = split(total)

    weights = level_weights[...]
    departures = []
    for r in range(0, CAP, 2):
        first, second = REQ + 3 * r, REQ + 3 * r + 3
        row = lambda i: stack_lanes(requests[first + i : first + i + 1, :], requests[second + i : second + i + 1, :])
        where = row(0).astype(jnp.int32) - 1
        valid = where >= 0
        at_x, at_y = where // YB, where % YB
        at_x = jnp.where(valid, at_x, -1)
        chosen = jnp.where(iota((YB, 256), 0) == at_y, 1.0, 0.0).astype(bf16)
        picked = mm(both[...], stack_rows(chosen, chosen))
        levels = jnp.zeros((LEVELS, 256), f32)
        for x in range(XB):
            levels = jnp.where(at_x == x, picked[x * LEVELS : (x + 1) * LEVELS, :], levels)
        total = jnp.sum(weights * softplus(levels), axis=0, keepdims=True)
        miss = jnp.where(valid, softplus(total) - row(1), 0.0)
        error = jnp.where(valid, row(2), 1.0)
        scale = miss / (error * error) * sigmoid(total)
        adjoint = scale * (weights * sigmoid(levels))
        high = adjoint.astype(bf16).astype(f32)
        low = adjoint - high
        lanes = 256 * r
        for x in range(XB):
            at = slice(x * LEVELS, (x + 1) * LEVELS)
            spread[at, lanes : lanes + 256] = jnp.where(at_x == x, high, 0.0).astype(bf16)
            spread[at, lanes + 256 : lanes + 512] = jnp.where(at_x == x, low, 0.0).astype(bf16)
        marks[:, lanes : lanes + 256] = chosen
        marks[:, lanes + 256 : lanes + 512] = chosen
        departures += [miss[:, :128], miss[:, 128:]]
    forced = mm_nt(spread[...], marks[...])
    forced_out[...] = forced

    gh, gl = split(forced)
    th, tl = turned_high[...], turned_low[...]
    along_x = mm(stack_lanes(th, tl, th), stack_rows(gh, gh, gl)) * decay_y
    for c in range(2):
        for h in range(2):
            msg[pl.ds(2 * c + h, PEERS, stride=ROWS), :] = along_x[128 * c : 128 * c + 128, 128 * h : 128 * h + 128]
    down = jnp.exp(rates[1:2, :] * (iota((YB, CH), 0).astype(f32) * (-1.0 / 4096.0)))
    dh, dl = split(down)
    weighed = mm(stack_lanes(gh, gl, gh), stack_rows(dh, dh, dl))
    running = jnp.zeros((1, CH), f32)
    rows = [None] * XB
    for x in range(XB - 1, -1, -1):
        at = slice(x * LEVELS, (x + 1) * LEVELS)
        running = running + jnp.sum(weighed[at, :] * scaled[at, :], axis=0, keepdims=True)
        rows[x] = running
    turned = [row[:, :128] for row in rows] + [row[:, 128:] for row in rows] + departures
    turned.append(jnp.zeros((128 - len(turned), 128), f32))
    msg[pl.ds(4, PEERS, stride=ROWS), :] = stack_rows(*turned).T


def observations(level, scaled, turned_high, turned_low, entered, coly, rates, level_weights):
    return pl.pallas_call(
        observe_kernel,
        in_specs=[VMEM] * 8,
        out_specs=[VMEM, VMEM],
        out_shape=[
            jax.ShapeDtypeStruct((XB * LEVELS, YB), f32),
            jax.ShapeDtypeStruct((PEERS * ROWS, 128), f32),
        ],
        scratch_shapes=[
            pltpu.VMEM((XB * LEVELS, 6 * 256), bf16),
            pltpu.VMEM((XB * LEVELS, 2 * YB), bf16),
            pltpu.VMEM((XB * LEVELS, 2 * PEERS * CAP), bf16),
            pltpu.VMEM((YB, 2 * PEERS * CAP), bf16),
        ],
        compiler_params=params(40),
        name="observations",
    )(level, scaled, turned_high, turned_low, entered, coly, rates, level_weights)


def planes_back_kernel(forced, turned_high, turned_low, colx, coly, out, running, decay, scale, shrink):
    b = pl.program_id(0)

    @pl.when(b == 0)
    def _():
        running[...] = jnp.zeros((CH, YB), f32)
        decay[...] = grow(coly[...], CH, -1.0)
        scale[...] = grow(coly[...], CH) * wide(jnp.exp(colx[...] * float(XB - 1)))
        shrink[...] = wide(jnp.exp(-colx[...]))

    sums = lower()
    gh, gl = split(forced[...])
    none = jnp.zeros((LEVELS, YB), bf16)
    for i in (1, 0):
        half = slice(i * LEVELS, (i + 1) * LEVELS)
        fill = lambda part: stack_rows(none, part[half]) if i else stack_rows(part[half], none)
        high, low = fill(gh), fill(gl)
        back = mm(turned_high[...], high) + (mm(turned_low[...], high) + mm(turned_high[...], low))
        total = running[...] + back * decay[...]
        running[...] = total
        high, low = split(total)
        out[i] = scale[...] * (mm(high, sums) + mm(low, sums))
        scale[...] = scale[...] * shrink[...]


def planes_back(forced, turned_high, turned_low, colx, coly):
    last = XB // 2 - 1
    lanes = pl.BlockSpec((CH, 128), lambda b: (0, last - b))
    field = pltpu.VMEM((CH, YB), f32)
    return pl.pallas_call(
        planes_back_kernel,
        grid=(XB // 2,),
        in_specs=[pl.BlockSpec((128, YB), lambda b: (last - b, 0)), lanes, lanes, whole((CH, 128)), whole((CH, 128))],
        out_specs=pl.BlockSpec((2, CH, YB), lambda b: (last - b, 0, 0)),
        out_shape=jax.ShapeDtypeStruct((XB, CH, YB), f32),
        scratch_shapes=[field, field, field, field],
        compiler_params=params(57),
        cost_estimate=pl.CostEstimate(flops=2 * 4 * 4096 * 256 * 256, bytes_accessed=8 << 20, transcendentals=1 << 16),
        name="planes_back",
    )(forced, turned_high, turned_low, colx, coly)


def join_kernel(control_a, control_b, planes, out):
    for x in range(XB):
        out[x] = planes[x] + take_plane((control_a, control_b), x, BLOCK)


def join(control, planes):
    return pl.pallas_call(
        join_kernel,
        grid=(CH // BLOCK,),
        in_specs=CONTROL + [PLANES],
        out_specs=PLANES,
        out_shape=jax.ShapeDtypeStruct((XB, CH, YB), f32),
        compiler_params=params(57),
        cost_estimate=pl.CostEstimate(flops=1 << 20, bytes_accessed=12 << 20, transcendentals=0),
        name="join",
    )(control, control, planes)


def final_kernel(partial, entered, colx, coly, out, whole_a, whole_b, sems):
    b = pl.program_id(0)
    start = (b % 4) * (BLOCK * ROWS)
    entering = jnp.concatenate(
        [entered[pl.ds(start + 2 * (b // 4) + h, BLOCK, stride=ROWS), :] for h in range(2)], axis=1
    )
    high, low = split(entering)
    sums = lower()
    entering = mm(high, sums) + mm(low, sums)
    tail = entered[pl.ds(start + 4, BLOCK, stride=ROWS), :]
    mine = jnp.where(b < 4, tail, pltpu.roll(tail, 112, 1))
    factor = wide(jnp.exp(colx[...]))
    scale = grow(coly[...], BLOCK)
    for x in range(XB):
        plane = partial[x] + scale * (entering + mine[:, x : x + 1])
        scale = scale * factor
        at = pl.ds(b * (BLOCK * XB) + x, BLOCK, stride=XB)
        whole_a[at, :] = plane[:, :128]
        whole_b[at, :] = plane[:, 128:]

    def copies(step):
        at = pl.ds(pl.multiple_of(step * (BLOCK * XB), BLOCK * XB), BLOCK * XB)
        return (
            pltpu.make_async_copy(whole_a.at[at, :], out.at[at, pl.ds(0, 128)], sems.at[step, 0]),
            pltpu.make_async_copy(whole_b.at[at, :], out.at[at, pl.ds(128, 128)], sems.at[step, 1]),
        )

    for copy in copies(b):
        copy.start()

    @pl.when(b == CH // BLOCK - 1)
    def _():
        for step in range(CH // BLOCK):
            for copy in copies(step):
                copy.wait()


def final(partial, entered, colx, coly):
    return pl.pallas_call(
        final_kernel,
        grid=(CH // BLOCK,),
        in_specs=[PLANES, whole((PEERS * ROWS, 128)), STEPS, STEPS],
        out_specs=ANY,
        out_shape=jax.ShapeDtypeStruct((CH * XB, YB), f32),
        scratch_shapes=[
            pltpu.VMEM((CH * XB, 128), f32),
            pltpu.VMEM((CH * XB, 128), f32),
            pltpu.SemaphoreType.DMA((CH // BLOCK, 2)),
        ],
        compiler_params=params(57),
        name="final",
    )(partial, entered, colx, coly)


def departures_kernel(rank, returned, out):
    total = jnp.zeros((1, OBS), f32)
    values = returned[pl.ds(4, PEERS, stride=ROWS), :]
    for r in range(CAP):
        value = values[:, REQ + r : REQ + r + 1]
        total = total + jnp.sum(jnp.where(rank[...] == float(r), value, 0.0), axis=0, keepdims=True)
    out[...] = total


def departures(rank, returned):
    return pl.pallas_call(
        departures_kernel,
        in_specs=[VMEM] * 2,
        out_specs=VMEM,
        out_shape=jax.ShapeDtypeStruct((1, OBS), f32),
        compiler_params=params(8),
        cost_estimate=pl.CostEstimate(flops=1 << 20, bytes_accessed=1 << 19, transcendentals=0),
        name="departures",
    )(rank, returned)


def everywhere(rows):
    shaped = rows.reshape(PEERS * ROWS, 1, 128)
    moved = lax.all_to_all(shaped, ("gx", "gy"), split_axis=0, concat_axis=0, tiled=True)
    return moved.reshape(PEERS * ROWS, 128)


def body(
    control,
    background,
    vert_factor,
    length_rates,
    flash_weights,
    level_weights,
    obs_owner,
    obs_cell,
    obs_count,
    flash_obs,
    obs_error,
):
    shape = control.shape
    flat = control.reshape(CH * XB, YB)
    msg, colx, coly = edges(flat, length_rates)
    asked = everywhere(msg)

    gx, gy = lax.axis_index("gx"), lax.axis_index("gy")
    place = jnp.stack([gx, gy, gx * N_Y + gy]).astype(jnp.int32)
    rates = length_rates.reshape(2, CH)
    requests, rank, ahead, behind, down = prepare(
        place, obs_count, rates, obs_owner.reshape(1, OBS), obs_cell.reshape(1, OBS),
        flash_obs.reshape(1, OBS), obs_error.reshape(1, OBS),
    )
    step_x, step_y = length_rates[0] / (XB * N_X), length_rates[1] / (YB * N_Y)
    gain = jnp.sqrt(-jnp.expm1(-2.0 * step_x)) * jnp.sqrt(-jnp.expm1(-2.0 * step_y))
    mixed = flash_weights[:, :, None] * vert_factor * gain[:, None, :]
    matrix = mixed.transpose(1, 0, 2).reshape(LEVELS, CH)
    cc = local(flat, colx, coly)
    asked, cc = lax.optimization_barrier((asked, cc))
    entered = everywhere(carry(asked, ahead, down, requests))
    share = background_share(background.reshape(4, LEVELS * XB, YB), flash_weights.T)
    level, scaled, turned_high, turned_low = levels_of(cc, share, coly, rates, matrix)
    forced, msg_back = observations(
        level, scaled, turned_high, turned_low, entered, coly, rates, level_weights.reshape(LEVELS, 1)
    )
    returned = everywhere(msg_back)
    planes = planes_back(forced, turned_high, turned_low, colx, coly)
    returned, planes = lax.optimization_barrier((returned, planes))
    entered_back = everywhere(carry(returned, behind, down))
    partial = join(flat, planes)
    departure = departures(rank, returned)
    grad = final(partial, entered_back, colx, coly)
    return (grad.reshape(shape), departure.reshape(OBS))


def solution(mesh):
    placed = (
        P(None, None, "gx", "gy"),
        P(None, None, "gx", "gy"),
        P(),
        P(),
        P(),
        P(),
        P(("gx", "gy"), None),
        P(("gx", "gy")),
        P(("gx", "gy")),
        P(("gx", "gy")),
        P(("gx", "gy")),
    )
    return jax.shard_map(
        body,
        mesh=mesh,
        in_specs=placed,
        out_specs=(P(None, None, "gx", "gy"), P(("gx", "gy"))),
        check_vma=False,
    )
```

```python
import functools

import jax
import jax.numpy as jnp
from jax import lax
from jax.experimental import pallas as pl
from jax.experimental.pallas import tpu as pltpu
from jax.sharding import PartitionSpec as P

highest = lax.Precision.HIGHEST
f32 = jnp.float32
bf16 = jnp.bfloat16

CH, LEVELS, XB, YB = 256, 64, 16, 256
OBS, PEERS, CAP = 512, 128, 8
N_X, N_Y = 8, 16
BLOCK = 32
REQ = 32
ROWS = 5
MIB = 1024 * 1024


def iota(shape, dim):
    return lax.broadcasted_iota(jnp.int32, shape, dim)


def split(value):
    high = value.astype(bf16)
    return high, (value - high.astype(f32)).astype(bf16)


def split3(value):
    high = value.astype(bf16)
    rest = value - high.astype(f32)
    middle = rest.astype(bf16)
    return high, middle, (rest - middle.astype(f32)).astype(bf16)


def mm(a, b):
    return jnp.dot(a, b, preferred_element_type=f32)


def mm_nt(a, b):
    return lax.dot_general(a, b, (((1,), (1,)), ((), ())), preferred_element_type=f32)


def wide(col):
    return jnp.concatenate([col, col], axis=1)


def upper():
    return jnp.where(iota((YB, YB), 0) <= iota((YB, YB), 1), 1.0, 0.0).astype(bf16)


def lower():
    return jnp.where(iota((YB, YB), 0) >= iota((YB, YB), 1), 1.0, 0.0).astype(bf16)


def softplus(x):
    return jnp.maximum(x, 0.0) + jnp.log1p(jnp.exp(-jnp.abs(x)))


def sigmoid(x):
    return 1.0 / (1.0 + jnp.exp(-x))


def take_plane(halves, x, rows, *lead):
    at = lead + (pl.ds(x, rows, stride=XB), slice(None))
    return jnp.concatenate([half[at] for half in halves], axis=1)


def params(mib, **more):
    return pltpu.CompilerParams(vmem_limit_bytes=mib * MIB, **more)


def whole(shape):
    return pl.BlockSpec(shape, lambda b: (0,) * len(shape))


VMEM = pl.BlockSpec(memory_space=pltpu.VMEM)
SMEM = pl.BlockSpec(memory_space=pltpu.SMEM)
ANY = pl.BlockSpec(memory_space=pl.ANY)
CONTROL = [
    pl.BlockSpec((BLOCK * XB, 128), lambda b: (b, 0)),
    pl.BlockSpec((BLOCK * XB, 128), lambda b: (b, 1)),
]
PLANES = pl.BlockSpec((XB, BLOCK, YB), lambda b: (0, b, 0))
STEPS = pl.BlockSpec((BLOCK, 128), lambda b: (b, 0))


def grow(step_y, rows, sign=1.0):
    return jnp.exp(wide(step_y) * (iota((rows, YB), 1).astype(f32) * sign))


def edges_kernel(control_a, control_b, rates, msg, colx, coly, planes, line, tail):
    b = pl.program_id(0)

    @pl.when(b == 0)
    def _():
        for i, (out, count) in enumerate(((colx, 128.0), (coly, 4096.0))):
            for v in range(4):
                line[0:1, 0:LEVELS] = rates[i, v : v + 1, :]
                turned = jnp.broadcast_to(line[0:1, :], (128, 128)).T
                out[v * LEVELS : (v + 1) * LEVELS, :] = turned[0:LEVELS, :] * (1.0 / count)
        tail[...] = jnp.zeros((PEERS, 128), f32)

    rows = pl.ds(pl.multiple_of(b * BLOCK, BLOCK), BLOCK)
    factor = wide(jnp.exp(colx[rows, :]))
    scale = grow(coly[rows, :], BLOCK)
    running = jnp.zeros((BLOCK, YB), f32)
    place = iota((BLOCK, 128), 1) - 16 * (b // 4)
    sums = jnp.zeros((BLOCK, 128), f32)
    for x in range(XB):
        plane = take_plane((control_a, control_b), x, BLOCK)
        planes[x] = plane
        running = running + plane * scale
        scale = scale * factor
        sums = jnp.where(place == x, jnp.sum(running, axis=1, keepdims=True), sums)
    start = (b % 4) * (BLOCK * ROWS) + 2 * (b // 4)
    msg[pl.ds(start, BLOCK, stride=ROWS), :] = running[:, :128]
    msg[pl.ds(start + 1, BLOCK, stride=ROWS), :] = running[:, 128:]
    back = pl.ds(pl.multiple_of((b % 4) * BLOCK, BLOCK), BLOCK)
    tail[back, :] = tail[back, :] + sums

    @pl.when(b == CH // BLOCK - 1)
    def _():
        msg[pl.ds(4, PEERS, stride=ROWS), :] = tail[...]


def edges(control, length_rates):
    return pl.pallas_call(
        edges_kernel,
        grid=(CH // BLOCK,),
        in_specs=CONTROL + [whole((2, 4, LEVELS))],
        out_specs=[whole((PEERS * ROWS, 128)), whole((CH, 128)), whole((CH, 128)), PLANES],
        out_shape=[
            jax.ShapeDtypeStruct((PEERS * ROWS, 128), f32),
            jax.ShapeDtypeStruct((CH, 128), f32),
            jax.ShapeDtypeStruct((CH, 128), f32),
            jax.ShapeDtypeStruct((XB, CH, YB), f32),
        ],
        scratch_shapes=[pltpu.VMEM((8, 128), f32), pltpu.VMEM((PEERS, 128), f32)],
        compiler_params=params(57),
        name="edges",
    )(control, control, length_rates)


def prepare_kernel(place, count, rates, owner, cell, flash, sigma, requests, rank_out, ahead, behind, down):
    live = iota((PEERS, OBS), 1) < count[0]
    chosen = (owner[...] == iota((PEERS, OBS), 0)) & live
    earlier = jnp.where(iota((OBS, OBS), 0) < iota((OBS, OBS), 1), 1.0, 0.0).astype(bf16)
    rank = mm(jnp.where(chosen, 1.0, 0.0).astype(bf16), earlier)
    rank = jnp.where(chosen, rank, -1.0)
    rank_out[...] = rank
    rows = iota((8, OBS), 0)
    values = jnp.where(
        rows == 0,
        cell[...].astype(f32) + 1.0,
        jnp.where(rows == 1, flash[...], jnp.where(rows == 2, sigma[...], 0.0)),
    )
    values = jnp.concatenate([values, jnp.zeros((120, OBS), f32)], axis=0)
    pieces = split3(jnp.concatenate([values[:, i : i + 128].T for i in range(0, OBS, 128)], axis=0))
    total = jnp.zeros((PEERS, 128), f32)
    for r in range(CAP):
        taken = jnp.where(rank == float(r), 1.0, 0.0).astype(bf16)
        found = (mm(taken, pieces[0]) + mm(taken, pieces[1])) + mm(taken, pieces[2])
        total = total + pltpu.roll(found, REQ + 3 * r, 1)
    requests[...] = total

    me = place[2]
    d, e = iota((PEERS, PEERS), 0), iota((PEERS, PEERS), 1)
    far_x = (d // N_Y) - (e // N_Y)
    far_y = (d % N_Y) - (e % N_Y)
    for c in range(2):
        mine = iota((2, CH), 1) == me + 128 * c
        rate = jnp.sum(jnp.where(mine, rates[...], 0.0), axis=1, keepdims=True)
        down_x = rate[0:1, :] * (XB / 128.0)
        down_y = rate[1:2, :] * (YB / 4096.0)
        down[c : c + 1, :] = jnp.broadcast_to(jnp.exp(-down_x), (1, 128))
        along = jnp.exp(-jnp.abs(far_y).astype(f32) * down_y)
        across = along * jnp.exp(-jnp.abs(far_x).astype(f32) * down_x)
        for out, sign in ((ahead, 1), (behind, -1)):
            past_x, past_y = far_x * sign > 0, far_y * sign > 0
            out[:, 256 * c : 256 * c + 128] = jnp.where((far_x == 0) & past_y, along, 0.0)
            out[:, 256 * c + 128 : 256 * c + 256] = jnp.where(past_x & past_y, across, 0.0)
    down[2:8, :] = jnp.zeros((6, 128), f32)


def prepare(place, count, rates, owner, cell, flash, sigma):
    return pl.pallas_call(
        prepare_kernel,
        in_specs=[SMEM, SMEM] + [VMEM] * 5,
        out_specs=[VMEM] * 5,
        out_shape=[
            jax.ShapeDtypeStruct((PEERS, 128), f32),
            jax.ShapeDtypeStruct((PEERS, OBS), f32),
            jax.ShapeDtypeStruct((PEERS, 4 * 128), f32),
            jax.ShapeDtypeStruct((PEERS, 4 * 128), f32),
            jax.ShapeDtypeStruct((8, 128), f32),
        ],
        compiler_params=params(16),
        cost_estimate=pl.CostEstimate(flops=1 << 30, bytes_accessed=1 << 20, transcendentals=1 << 16),
        name="prepare",
    )(place, count, rates, owner, cell, flash, sigma)


def local_kernel(planes, colx, coly, cc):
    factor = wide(jnp.exp(colx[...]))
    scale = grow(coly[...], BLOCK)
    running = jnp.zeros((BLOCK, YB), f32)
    sums = upper()
    highs, lows = [], []
    for x in range(XB):
        running = running + planes[x] * scale
        scale = scale * factor
        high, low = split(running)
        highs.append(high)
        lows.append(low)
    summed = mm(jnp.concatenate(highs, axis=0), sums) + mm(jnp.concatenate(lows, axis=0), sums)
    cc[...] = summed.reshape(XB, BLOCK, YB)


def local(planes, colx, coly):
    return pl.pallas_call(
        local_kernel,
        grid=(CH // BLOCK,),
        in_specs=[PLANES, STEPS, STEPS],
        out_specs=PLANES,
        out_shape=jax.ShapeDtypeStruct((XB, CH, YB), f32),
        compiler_params=params(57),
        cost_estimate=pl.CostEstimate(flops=2 * 2 * 4096 * 256 * 256, bytes_accessed=8 << 20, transcendentals=1 << 16),
        name="local",
    )(planes, colx, coly)


def share_kernel(background, weights, share, half_a, half_b):
    total = background[0] * weights[:, 0:1]
    for v in range(1, 4):
        total = total + background[v] * weights[:, v : v + 1]
    half_a[...] = total[:, :128]
    half_b[...] = total[:, 128:]
    for x in range(XB):
        share[x] = take_plane((half_a, half_b), x, 8)


def background_share(background, weights):
    return pl.pallas_call(
        share_kernel,
        grid=(8,),
        in_specs=[
            pl.BlockSpec((4, 128, YB), lambda b: (0, b, 0)),
            pl.BlockSpec((128, 4), lambda b: (b, 0)),
        ],
        out_specs=pl.BlockSpec((XB, 8, YB), lambda b: (0, b, 0)),
        out_shape=jax.ShapeDtypeStruct((XB, LEVELS, YB), f32),
        scratch_shapes=[pltpu.VMEM((128, 128), f32), pltpu.VMEM((128, 128), f32)],
        compiler_params=params(57),
        cost_estimate=pl.CostEstimate(flops=1 << 21, bytes_accessed=5 << 20, transcendentals=0),
        name="share",
    )(background, weights)


def levels_kernel(cc, share, coly, rates, matrix, level, scaled, turned_high, turned_low, decay):
    b = pl.program_id(0)

    @pl.when(b == 0)
    def _():
        decay[...] = grow(coly[...], CH, -1.0)

    for i in range(2):
        x = (2 * b + i).astype(f32)
        at = slice(i * LEVELS, (i + 1) * LEVELS)
        part = matrix[...] * jnp.exp(rates[0:1, :] * (x * (-1.0 / 128.0)))
        scaled[at, :] = part
        mh, ml = split(part)
        high, low = split(decay[...] * cc[i])
        pair = mm(jnp.concatenate([mh, ml], axis=0), high)
        level[at, :] = (pair[:LEVELS] + (pair[LEVELS:] + mm(mh, low))) + share[i]
    turned = jnp.concatenate([scaled[:, :128].T, scaled[:, 128:].T], axis=0)
    turned_high[...], turned_low[...] = split(turned)


def levels_of(cc, share, coly, rates, matrix):
    two = lambda shape: pl.BlockSpec(shape, lambda b: (b,) + (0,) * (len(shape) - 1))
    lanes = pl.BlockSpec((CH, 128), lambda b: (0, b))
    return pl.pallas_call(
        levels_kernel,
        grid=(XB // 2,),
        in_specs=[two((2, CH, YB)), two((2, LEVELS, YB)), whole((CH, 128)), whole((2, CH)), whole((LEVELS, CH))],
        out_specs=[two((128, YB)), two((128, CH)), lanes, lanes],
        out_shape=[
            jax.ShapeDtypeStruct((XB * LEVELS, YB), f32),
            jax.ShapeDtypeStruct((XB * LEVELS, CH), f32),
            jax.ShapeDtypeStruct((CH, XB * LEVELS), bf16),
            jax.ShapeDtypeStruct((CH, XB * LEVELS), bf16),
        ],
        scratch_shapes=[pltpu.VMEM((CH, YB), f32)],
        compiler_params=params(57),
        cost_estimate=pl.CostEstimate(flops=2 * 3 * 1024 * 256 * 256, bytes_accessed=8 << 20, transcendentals=1 << 18),
        name="levels",
    )(cc, share, coly, rates, matrix)


def carry_kernel(reverse, sums, weights, down, requests, out):
    order = list(range(N_X))
    if reverse:
        order = order[::-1]
    for row in range(4):
        decay = down[row // 2 : row // 2 + 1, :]
        total = jnp.zeros((N_Y, 128), f32)
        for g in order:
            at = pl.ds(g * N_Y * ROWS + row, N_Y, stride=ROWS)
            out[at, :] = total
            total = decay * (total + sums[at, :])
    tail = sums[pl.ds(4, PEERS, stride=ROWS), :]
    lanes = iota((PEERS, 128), 1)
    right = []
    for c in range(2):
        own = (lanes >= 16 * c) & (lanes < 16 * c + 16)
        right.append(jnp.where(own, tail, 0.0))
        last = 16 * c if reverse else 16 * c + 15
        total = jnp.sum(jnp.where(lanes == last, tail, 0.0), axis=1, keepdims=True)
        right.append(jnp.where(own, total, 0.0))
    entering = jnp.dot(
        weights[...], jnp.concatenate(right, axis=0), precision=highest, preferred_element_type=f32
    )
    if requests is not None:
        entering = entering + requests[...]
    out[pl.ds(4, PEERS, stride=ROWS), :] = entering


def carry(sums, weights, down, requests=None):
    shape = jax.ShapeDtypeStruct((PEERS * ROWS, 128), f32)
    if requests is None:
        kernel = lambda *refs: carry_kernel(True, *refs[:3], None, refs[3])
        return pl.pallas_call(
            kernel, in_specs=[VMEM] * 3, out_specs=VMEM, out_shape=shape,
            compiler_params=params(8), name="carry_back",
        )(sums, weights, down)
    return pl.pallas_call(
        functools.partial(carry_kernel, False), in_specs=[VMEM] * 4, out_specs=VMEM, out_shape=shape,
        compiler_params=params(8), name="carry",
    )(sums, weights, down, requests)


def stack_rows(*parts):
    return jnp.concatenate(parts, axis=0)


def stack_lanes(*parts):
    return jnp.concatenate(parts, axis=1)


def observe_kernel(
    level, scaled, turned_high, turned_low, entered, coly, rates, level_weights,
    forced_out, msg, left, both, spread, marks,
):
    decay_y = grow(coly[...], CH, -1.0)
    pick = lambda row: entered[pl.ds(row, PEERS, stride=ROWS), :]
    high, low = split(stack_rows(stack_lanes(pick(0), pick(1)), stack_lanes(pick(2), pick(3))))
    sums = upper()
    eh, el = split(decay_y * (mm(high, sums) + mm(low, sums)))
    dh, dl = split(decay_y)
    requests = pick(4).T
    for x in range(XB):
        at = slice(x * LEVELS, (x + 1) * LEVELS)
        part = scaled[at, :]
        high, low = split(part)
        left[at, 0:256], left[at, 256:512], left[at, 512:768] = high, low, high
        col = stack_lanes(requests[x : x + 1, :], requests[16 + x : 17 + x, :])
        high, low = split(part * col)
        left[at, 768:1024], left[at, 1024:1280], left[at, 1280:1536] = high, low, high
    total = level[...] + mm(left[...], stack_rows(eh, eh, el, dh, dh, dl))
    both[:, 0:256], both[:, 256:512] = split(total)

    weights = level_weights[...]
    departures = []
    for r in range(0, CAP, 2):
        first, second = REQ + 3 * r, REQ + 3 * r + 3
        row = lambda i: stack_lanes(requests[first + i : first + i + 1, :], requests[second + i : second + i + 1, :])
        where = row(0).astype(jnp.int32) - 1
        valid = where >= 0
        at_x, at_y = where // YB, where % YB
        at_x = jnp.where(valid, at_x, -1)
        chosen = jnp.where(iota((YB, 256), 0) == at_y, 1.0, 0.0).astype(bf16)
        picked = mm(both[...], stack_rows(chosen, chosen))
        levels = jnp.zeros((LEVELS, 256), f32)
        for x in range(XB):
            levels = jnp.where(at_x == x, picked[x * LEVELS : (x + 1) * LEVELS, :], levels)
        total = jnp.sum(weights * softplus(levels), axis=0, keepdims=True)
        miss = jnp.where(valid, softplus(total) - row(1), 0.0)
        error = jnp.where(valid, row(2), 1.0)
        scale = miss / (error * error) * sigmoid(total)
        adjoint = scale * (weights * sigmoid(levels))
        high = adjoint.astype(bf16).astype(f32)
        low = adjoint - high
        lanes = 256 * r
        for x in range(XB):
            at = slice(x * LEVELS, (x + 1) * LEVELS)
            spread[at, lanes : lanes + 256] = jnp.where(at_x == x, high, 0.0).astype(bf16)
            spread[at, lanes + 256 : lanes + 512] = jnp.where(at_x == x, low, 0.0).astype(bf16)
        marks[:, lanes : lanes + 256] = chosen
        marks[:, lanes + 256 : lanes + 512] = chosen
        departures += [miss[:, :128], miss[:, 128:]]
    forced = mm_nt(spread[...], marks[...])
    forced_out[...] = forced

    gh, gl = split(forced)
    th, tl = turned_high[...], turned_low[...]
    along_x = mm(stack_lanes(th, tl, th), stack_rows(gh, gh, gl)) * decay_y
    for c in range(2):
        for h in range(2):
            msg[pl.ds(2 * c + h, PEERS, stride=ROWS), :] = along_x[128 * c : 128 * c + 128, 128 * h : 128 * h + 128]
    down = jnp.exp(rates[1:2, :] * (iota((YB, CH), 0).astype(f32) * (-1.0 / 4096.0)))
    dh, dl = split(down)
    weighed = mm(stack_lanes(gh, gl, gh), stack_rows(dh, dh, dl))
    running = jnp.zeros((1, CH), f32)
    rows = [None] * XB
    for x in range(XB - 1, -1, -1):
        at = slice(x * LEVELS, (x + 1) * LEVELS)
        running = running + jnp.sum(weighed[at, :] * scaled[at, :], axis=0, keepdims=True)
        rows[x] = running
    turned = [row[:, :128] for row in rows] + [row[:, 128:] for row in rows] + departures
    turned.append(jnp.zeros((128 - len(turned), 128), f32))
    msg[pl.ds(4, PEERS, stride=ROWS), :] = stack_rows(*turned).T


def observations(level, scaled, turned_high, turned_low, entered, coly, rates, level_weights):
    return pl.pallas_call(
        observe_kernel,
        in_specs=[VMEM] * 8,
        out_specs=[VMEM, VMEM],
        out_shape=[
            jax.ShapeDtypeStruct((XB * LEVELS, YB), f32),
            jax.ShapeDtypeStruct((PEERS * ROWS, 128), f32),
        ],
        scratch_shapes=[
            pltpu.VMEM((XB * LEVELS, 6 * 256), bf16),
            pltpu.VMEM((XB * LEVELS, 2 * YB), bf16),
            pltpu.VMEM((XB * LEVELS, 2 * PEERS * CAP), bf16),
            pltpu.VMEM((YB, 2 * PEERS * CAP), bf16),
        ],
        compiler_params=params(57),
        name="observations",
    )(level, scaled, turned_high, turned_low, entered, coly, rates, level_weights)


def planes_back_kernel(forced, turned_high, turned_low, coly, out, running, decay):
    b = pl.program_id(0)

    @pl.when(b == 0)
    def _():
        running[...] = jnp.zeros((CH, YB), f32)
        decay[...] = grow(coly[...], CH, -1.0)

    gh, gl = split(forced[...])
    th, tl = turned_high[...], turned_low[...]
    none = jnp.zeros((LEVELS, YB), bf16)
    for i in (1, 0):
        half = slice(i * LEVELS, (i + 1) * LEVELS)
        fill = lambda part: stack_rows(none, part[half]) if i else stack_rows(part[half], none)
        high, low = fill(gh), fill(gl)
        back = mm(stack_lanes(th, tl), stack_rows(high, high)) + mm(th, low)
        running[...] = running[...] + back * decay[...]
        out[i] = running[...]


def planes_back(forced, turned_high, turned_low, coly):
    last = XB // 2 - 1
    lanes = pl.BlockSpec((CH, 128), lambda b: (0, last - b))
    field = pltpu.VMEM((CH, YB), f32)
    return pl.pallas_call(
        planes_back_kernel,
        grid=(XB // 2,),
        in_specs=[pl.BlockSpec((128, YB), lambda b: (last - b, 0)), lanes, lanes, whole((CH, 128))],
        out_specs=pl.BlockSpec((2, CH, YB), lambda b: (last - b, 0, 0)),
        out_shape=jax.ShapeDtypeStruct((XB, CH, YB), f32),
        scratch_shapes=[field, field],
        compiler_params=params(57),
        cost_estimate=pl.CostEstimate(flops=2 * 4 * 4096 * 256 * 256, bytes_accessed=8 << 20, transcendentals=1 << 16),
        name="planes_back",
    )(forced, turned_high, turned_low, coly)


def join_kernel(control, running, colx, coly, out):
    high, low = split(running[...].reshape(XB * BLOCK, YB))
    sums = lower()
    summed = mm(high, sums) + mm(low, sums)
    factor = wide(jnp.exp(colx[...]))
    scale = grow(coly[...], BLOCK)
    for x in range(XB):
        out[x] = control[x] + scale * summed[x * BLOCK : (x + 1) * BLOCK, :]
        scale = scale * factor


def join(control, running, colx, coly):
    return pl.pallas_call(
        join_kernel,
        grid=(CH // BLOCK,),
        in_specs=[PLANES, PLANES, STEPS, STEPS],
        out_specs=PLANES,
        out_shape=jax.ShapeDtypeStruct((XB, CH, YB), f32),
        compiler_params=params(57),
        cost_estimate=pl.CostEstimate(flops=2 * 2 * 4096 * 256 * 256, bytes_accessed=12 << 20, transcendentals=0),
        name="join",
    )(control, running, colx, coly)


def final_kernel(partial, entered, colx, coly, out, whole_a, whole_b, sems):
    b = pl.program_id(0)
    start = (b % 4) * (BLOCK * ROWS)
    entering = jnp.concatenate(
        [entered[pl.ds(start + 2 * (b // 4) + h, BLOCK, stride=ROWS), :] for h in range(2)], axis=1
    )
    high, low = split(entering)
    sums = lower()
    entering = mm(high, sums) + mm(low, sums)
    tail = entered[pl.ds(start + 4, BLOCK, stride=ROWS), :]
    mine = jnp.where(b < 4, tail, pltpu.roll(tail, 112, 1))
    factor = wide(jnp.exp(colx[...]))
    scale = grow(coly[...], BLOCK)
    for x in range(XB):
        plane = partial[x] + scale * (entering + mine[:, x : x + 1])
        scale = scale * factor
        at = pl.ds(b * (BLOCK * XB) + x, BLOCK, stride=XB)
        whole_a[at, :] = plane[:, :128]
        whole_b[at, :] = plane[:, 128:]

    def copies(step):
        at = pl.ds(pl.multiple_of(step * (BLOCK * XB), BLOCK * XB), BLOCK * XB)
        return (
            pltpu.make_async_copy(whole_a.at[at, :], out.at[at, pl.ds(0, 128)], sems.at[step, 0]),
            pltpu.make_async_copy(whole_b.at[at, :], out.at[at, pl.ds(128, 128)], sems.at[step, 1]),
        )

    for copy in copies(b):
        copy.start()

    @pl.when(b == CH // BLOCK - 1)
    def _():
        for step in range(CH // BLOCK):
            for copy in copies(step):
                copy.wait()


def final(partial, entered, colx, coly):
    return pl.pallas_call(
        final_kernel,
        grid=(CH // BLOCK,),
        in_specs=[PLANES, whole((PEERS * ROWS, 128)), STEPS, STEPS],
        out_specs=ANY,
        out_shape=jax.ShapeDtypeStruct((CH * XB, YB), f32),
        scratch_shapes=[
            pltpu.VMEM((CH * XB, 128), f32),
            pltpu.VMEM((CH * XB, 128), f32),
            pltpu.SemaphoreType.DMA((CH // BLOCK, 2)),
        ],
        compiler_params=params(57),
        name="final",
    )(partial, entered, colx, coly)


def departures_kernel(rank, returned, out):
    total = jnp.zeros((1, OBS), f32)
    values = returned[pl.ds(4, PEERS, stride=ROWS), :]
    for r in range(CAP):
        value = values[:, REQ + r : REQ + r + 1]
        total = total + jnp.sum(jnp.where(rank[...] == float(r), value, 0.0), axis=0, keepdims=True)
    out[...] = total


def departures(rank, returned):
    return pl.pallas_call(
        departures_kernel,
        in_specs=[VMEM] * 2,
        out_specs=VMEM,
        out_shape=jax.ShapeDtypeStruct((1, OBS), f32),
        compiler_params=params(8),
        cost_estimate=pl.CostEstimate(flops=1 << 20, bytes_accessed=1 << 19, transcendentals=0),
        name="departures",
    )(rank, returned)


def everywhere(rows):
    shaped = rows.reshape(PEERS * ROWS, 1, 128)
    moved = lax.all_to_all(shaped, ("gx", "gy"), split_axis=0, concat_axis=0, tiled=True)
    return moved.reshape(PEERS * ROWS, 128)


def body(
    control,
    background,
    vert_factor,
    length_rates,
    flash_weights,
    level_weights,
    obs_owner,
    obs_cell,
    obs_count,
    flash_obs,
    obs_error,
):
    shape = control.shape
    flat = control.reshape(CH * XB, YB)
    msg, colx, coly, control_planes = edges(flat, length_rates)
    asked = everywhere(msg)

    gx, gy = lax.axis_index("gx"), lax.axis_index("gy")
    place = jnp.stack([gx, gy, gx * N_Y + gy]).astype(jnp.int32)
    rates = length_rates.reshape(2, CH)
    requests, rank, ahead, behind, down = prepare(
        place, obs_count, rates, obs_owner.reshape(1, OBS), obs_cell.reshape(1, OBS),
        flash_obs.reshape(1, OBS), obs_error.reshape(1, OBS),
    )
    step_x, step_y = length_rates[0] / (XB * N_X), length_rates[1] / (YB * N_Y)
    gain = jnp.sqrt(-jnp.expm1(-2.0 * step_x)) * jnp.sqrt(-jnp.expm1(-2.0 * step_y))
    mixed = flash_weights[:, :, None] * vert_factor * gain[:, None, :]
    matrix = mixed.transpose(1, 0, 2).reshape(LEVELS, CH)
    cc = local(control_planes, colx, coly)
    asked, cc = lax.optimization_barrier((asked, cc))
    entered = everywhere(carry(asked, ahead, down, requests))
    share = background_share(background.reshape(4, LEVELS * XB, YB), jnp.repeat(flash_weights.T, XB, axis=0))
    level, scaled, turned_high, turned_low = levels_of(cc, share, coly, rates, matrix)
    forced, msg_back = observations(
        level, scaled, turned_high, turned_low, entered, coly, rates, level_weights.reshape(LEVELS, 1)
    )
    returned = everywhere(msg_back)
    planes = planes_back(forced, turned_high, turned_low, coly)
    returned, planes = lax.optimization_barrier((returned, planes))
    entered_back = everywhere(carry(returned, behind, down))
    partial = join(control_planes, planes, colx, coly)
    departure = departures(rank, returned)
    grad = final(partial, entered_back, colx, coly)
    return (grad.reshape(shape), departure.reshape(OBS))


def solution(mesh):
    placed = (
        P(None, None, "gx", "gy"),
        P(None, None, "gx", "gy"),
        P(),
        P(),
        P(),
        P(),
        P(("gx", "gy"), None),
        P(("gx", "gy")),
        P(("gx", "gy")),
        P(("gx", "gy")),
        P(("gx", "gy")),
    )
    return jax.shard_map(
        body,
        mesh=mesh,
        in_specs=placed,
        out_specs=(P(None, None, "gx", "gy"), P(("gx", "gy"))),
        check_vma=False,
    )
```

```python
import functools

import jax
import jax.numpy as jnp
from jax import lax
from jax.experimental import pallas as pl
from jax.experimental.pallas import tpu as pltpu
from jax.sharding import PartitionSpec as P

highest = lax.Precision.HIGHEST
f32 = jnp.float32
bf16 = jnp.bfloat16

CH, LEVELS, XB, YB = 256, 64, 16, 256
OBS, PEERS, CAP = 512, 128, 8
N_X, N_Y = 8, 16
BLOCK = 64
HALF = 128 // BLOCK
DEEP = 4
REQ = 32
ROWS = 5
MIB = 1024 * 1024


def iota(shape, dim):
    return lax.broadcasted_iota(jnp.int32, shape, dim)


def split(value):
    high = value.astype(bf16)
    return high, (value - high.astype(f32)).astype(bf16)


def split3(value):
    high = value.astype(bf16)
    rest = value - high.astype(f32)
    middle = rest.astype(bf16)
    return high, middle, (rest - middle.astype(f32)).astype(bf16)


def mm(a, b):
    return jnp.dot(a, b, preferred_element_type=f32)


def mm_nt(a, b):
    return lax.dot_general(a, b, (((1,), (1,)), ((), ())), preferred_element_type=f32)


def wide(col):
    return jnp.concatenate([col, col], axis=1)


def upper():
    return jnp.where(iota((YB, YB), 0) <= iota((YB, YB), 1), 1.0, 0.0).astype(bf16)


def lower():
    return jnp.where(iota((YB, YB), 0) >= iota((YB, YB), 1), 1.0, 0.0).astype(bf16)


def softplus(x):
    return jnp.maximum(x, 0.0) + jnp.log1p(jnp.exp(-jnp.abs(x)))


def sigmoid(x):
    return 1.0 / (1.0 + jnp.exp(-x))


def take_plane(halves, x, rows, *lead):
    at = lead + (pl.ds(x, rows, stride=XB), slice(None))
    return jnp.concatenate([half[at] for half in halves], axis=1)


def params(mib, **more):
    return pltpu.CompilerParams(vmem_limit_bytes=mib * MIB, **more)


def whole(shape):
    return pl.BlockSpec(shape, lambda b: (0,) * len(shape))


VMEM = pl.BlockSpec(memory_space=pltpu.VMEM)
SMEM = pl.BlockSpec(memory_space=pltpu.SMEM)
ANY = pl.BlockSpec(memory_space=pl.ANY)
CONTROL = [
    pl.BlockSpec((BLOCK * XB, 128), lambda b: (b, 0)),
    pl.BlockSpec((BLOCK * XB, 128), lambda b: (b, 1)),
]
PLANES = pl.BlockSpec((XB, BLOCK, YB), lambda b: (0, b, 0))
STEPS = pl.BlockSpec((BLOCK, 128), lambda b: (b, 0))


def grow(step_y, rows, sign=1.0):
    return jnp.exp(wide(step_y) * (iota((rows, YB), 1).astype(f32) * sign))


def edges_kernel(control_a, control_b, rates, msg, colx, coly, planes, line, tail):
    b = pl.program_id(0)

    @pl.when(b == 0)
    def _():
        for i, (out, count) in enumerate(((colx, 128.0), (coly, 4096.0))):
            for v in range(4):
                line[0:1, 0:LEVELS] = rates[i, v : v + 1, :]
                turned = jnp.broadcast_to(line[0:1, :], (128, 128)).T
                out[v * LEVELS : (v + 1) * LEVELS, :] = turned[0:LEVELS, :] * (1.0 / count)
        tail[...] = jnp.zeros((PEERS, 128), f32)

    rows = pl.ds(pl.multiple_of(b * BLOCK, BLOCK), BLOCK)
    factor = wide(jnp.exp(colx[rows, :]))
    scale = grow(coly[rows, :], BLOCK)
    running = jnp.zeros((BLOCK, YB), f32)
    place = iota((BLOCK, 128), 1) - 16 * (b // HALF)
    sums = jnp.zeros((BLOCK, 128), f32)
    for x in range(XB):
        plane = take_plane((control_a, control_b), x, BLOCK)
        planes[x] = plane
        running = running + plane * scale
        scale = scale * factor
        sums = jnp.where(place == x, jnp.sum(running, axis=1, keepdims=True), sums)
    start = (b % HALF) * (BLOCK * ROWS) + 2 * (b // HALF)
    msg[pl.ds(start, BLOCK, stride=ROWS), :] = running[:, :128]
    msg[pl.ds(start + 1, BLOCK, stride=ROWS), :] = running[:, 128:]
    back = pl.ds(pl.multiple_of((b % HALF) * BLOCK, BLOCK), BLOCK)
    tail[back, :] = tail[back, :] + sums

    @pl.when(b == CH // BLOCK - 1)
    def _():
        msg[pl.ds(4, PEERS, stride=ROWS), :] = tail[...]


def edges(control, length_rates):
    return pl.pallas_call(
        edges_kernel,
        grid=(CH // BLOCK,),
        in_specs=CONTROL + [whole((2, 4, LEVELS))],
        out_specs=[whole((PEERS * ROWS, 128)), whole((CH, 128)), whole((CH, 128)), PLANES],
        out_shape=[
            jax.ShapeDtypeStruct((PEERS * ROWS, 128), f32),
            jax.ShapeDtypeStruct((CH, 128), f32),
            jax.ShapeDtypeStruct((CH, 128), f32),
            jax.ShapeDtypeStruct((XB, CH, YB), f32),
        ],
        scratch_shapes=[pltpu.VMEM((8, 128), f32), pltpu.VMEM((PEERS, 128), f32)],
        compiler_params=params(57),
        name="edges",
    )(control, control, length_rates)


def prepare_kernel(place, count, rates, owner, cell, flash, sigma, requests, rank_out, ahead, behind, down):
    live = iota((PEERS, OBS), 1) < count[0]
    chosen = (owner[...] == iota((PEERS, OBS), 0)) & live
    earlier = jnp.where(iota((OBS, OBS), 0) < iota((OBS, OBS), 1), 1.0, 0.0).astype(bf16)
    rank = mm(jnp.where(chosen, 1.0, 0.0).astype(bf16), earlier)
    rank = jnp.where(chosen, rank, -1.0)
    rank_out[...] = rank
    rows = iota((8, OBS), 0)
    values = jnp.where(
        rows == 0,
        cell[...].astype(f32) + 1.0,
        jnp.where(rows == 1, flash[...], jnp.where(rows == 2, sigma[...], 0.0)),
    )
    values = jnp.concatenate([values, jnp.zeros((120, OBS), f32)], axis=0)
    pieces = split3(jnp.concatenate([values[:, i : i + 128].T for i in range(0, OBS, 128)], axis=0))
    total = jnp.zeros((PEERS, 128), f32)
    for r in range(CAP):
        taken = jnp.where(rank == float(r), 1.0, 0.0).astype(bf16)
        found = (mm(taken, pieces[0]) + mm(taken, pieces[1])) + mm(taken, pieces[2])
        total = total + pltpu.roll(found, REQ + 3 * r, 1)
    requests[...] = total

    me = place[2]
    d, e = iota((PEERS, PEERS), 0), iota((PEERS, PEERS), 1)
    far_x = (d // N_Y) - (e // N_Y)
    far_y = (d % N_Y) - (e % N_Y)
    for c in range(2):
        mine = iota((2, CH), 1) == me + 128 * c
        rate = jnp.sum(jnp.where(mine, rates[...], 0.0), axis=1, keepdims=True)
        down_x = rate[0:1, :] * (XB / 128.0)
        down_y = rate[1:2, :] * (YB / 4096.0)
        down[c : c + 1, :] = jnp.broadcast_to(jnp.exp(-down_x), (1, 128))
        along = jnp.exp(-jnp.abs(far_y).astype(f32) * down_y)
        across = along * jnp.exp(-jnp.abs(far_x).astype(f32) * down_x)
        for out, sign in ((ahead, 1), (behind, -1)):
            past_x, past_y = far_x * sign > 0, far_y * sign > 0
            out[:, 256 * c : 256 * c + 128] = jnp.where((far_x == 0) & past_y, along, 0.0)
            out[:, 256 * c + 128 : 256 * c + 256] = jnp.where(past_x & past_y, across, 0.0)
    down[2:8, :] = jnp.zeros((6, 128), f32)


def prepare(place, count, rates, owner, cell, flash, sigma):
    return pl.pallas_call(
        prepare_kernel,
        in_specs=[SMEM, SMEM] + [VMEM] * 5,
        out_specs=[VMEM] * 5,
        out_shape=[
            jax.ShapeDtypeStruct((PEERS, 128), f32),
            jax.ShapeDtypeStruct((PEERS, OBS), f32),
            jax.ShapeDtypeStruct((PEERS, 4 * 128), f32),
            jax.ShapeDtypeStruct((PEERS, 4 * 128), f32),
            jax.ShapeDtypeStruct((8, 128), f32),
        ],
        compiler_params=params(16),
        cost_estimate=pl.CostEstimate(flops=1 << 30, bytes_accessed=1 << 20, transcendentals=1 << 16),
        name="prepare",
    )(place, count, rates, owner, cell, flash, sigma)


def local_kernel(planes, colx, coly, cc):
    factor = wide(jnp.exp(colx[...]))
    scale = grow(coly[...], BLOCK)
    running = jnp.zeros((BLOCK, YB), f32)
    sums = upper()
    highs, lows = [], []
    for x in range(XB):
        running = running + planes[x] * scale
        scale = scale * factor
        high, low = split(running)
        highs.append(high)
        lows.append(low)
    summed = mm(jnp.concatenate(highs, axis=0), sums) + mm(jnp.concatenate(lows, axis=0), sums)
    cc[...] = summed.reshape(XB, BLOCK, YB)


def local(planes, colx, coly):
    return pl.pallas_call(
        local_kernel,
        grid=(CH // BLOCK,),
        in_specs=[PLANES, STEPS, STEPS],
        out_specs=PLANES,
        out_shape=jax.ShapeDtypeStruct((XB, CH, YB), f32),
        compiler_params=params(57),
        cost_estimate=pl.CostEstimate(flops=2 * 2 * 4096 * 256 * 256, bytes_accessed=8 << 20, transcendentals=1 << 16),
        name="local",
    )(planes, colx, coly)


def share_kernel(background, weights, share, half_a, half_b):
    total = background[0] * weights[:, 0:1]
    for v in range(1, 4):
        total = total + background[v] * weights[:, v : v + 1]
    half_a[...] = total[:, :128]
    half_b[...] = total[:, 128:]
    for x in range(XB):
        share[x] = take_plane((half_a, half_b), x, 32)


def background_share(background, weights):
    return pl.pallas_call(
        share_kernel,
        grid=(2,),
        in_specs=[
            pl.BlockSpec((4, 512, YB), lambda b: (0, b, 0)),
            pl.BlockSpec((512, 4), lambda b: (b, 0)),
        ],
        out_specs=pl.BlockSpec((XB, 32, YB), lambda b: (0, b, 0)),
        out_shape=jax.ShapeDtypeStruct((XB, LEVELS, YB), f32),
        scratch_shapes=[pltpu.VMEM((512, 128), f32), pltpu.VMEM((512, 128), f32)],
        compiler_params=params(57),
        cost_estimate=pl.CostEstimate(flops=1 << 21, bytes_accessed=5 << 20, transcendentals=0),
        name="share",
    )(background, weights)


def levels_kernel(cc, share, coly, rates, matrix, level, scaled, turned_high, turned_low, decay):
    b = pl.program_id(0)

    @pl.when(b == 0)
    def _():
        decay[...] = grow(coly[...], CH, -1.0)

    for i in range(DEEP):
        x = (DEEP * b + i).astype(f32)
        at = slice(i * LEVELS, (i + 1) * LEVELS)
        part = matrix[...] * jnp.exp(rates[0:1, :] * (x * (-1.0 / 128.0)))
        scaled[at, :] = part
        mh, ml = split(part)
        high, low = split(decay[...] * cc[i])
        pair = mm(jnp.concatenate([mh, ml], axis=0), high)
        level[at, :] = (pair[:LEVELS] + (pair[LEVELS:] + mm(mh, low))) + share[i]
    for i in range(0, DEEP * LEVELS, 128):
        part = scaled[i : i + 128, :]
        turned = jnp.concatenate([part[:, :128].T, part[:, 128:].T], axis=0)
        turned_high[:, i : i + 128], turned_low[:, i : i + 128] = split(turned)


def levels_of(cc, share, coly, rates, matrix):
    two = lambda shape: pl.BlockSpec(shape, lambda b: (b,) + (0,) * (len(shape) - 1))
    lanes = pl.BlockSpec((CH, DEEP * LEVELS), lambda b: (0, b))
    return pl.pallas_call(
        levels_kernel,
        grid=(XB // DEEP,),
        in_specs=[two((DEEP, CH, YB)), two((DEEP, LEVELS, YB)), whole((CH, 128)), whole((2, CH)), whole((LEVELS, CH))],
        out_specs=[two((DEEP * LEVELS, YB)), two((DEEP * LEVELS, CH)), lanes, lanes],
        out_shape=[
            jax.ShapeDtypeStruct((XB * LEVELS, YB), f32),
            jax.ShapeDtypeStruct((XB * LEVELS, CH), f32),
            jax.ShapeDtypeStruct((CH, XB * LEVELS), bf16),
            jax.ShapeDtypeStruct((CH, XB * LEVELS), bf16),
        ],
        scratch_shapes=[pltpu.VMEM((CH, YB), f32)],
        compiler_params=params(57),
        cost_estimate=pl.CostEstimate(flops=2 * 3 * 1024 * 256 * 256, bytes_accessed=8 << 20, transcendentals=1 << 18),
        name="levels",
    )(cc, share, coly, rates, matrix)


def carry_kernel(reverse, sums, weights, down, requests, out):
    order = list(range(N_X))
    if reverse:
        order = order[::-1]
    for row in range(4):
        decay = down[row // 2 : row // 2 + 1, :]
        total = jnp.zeros((N_Y, 128), f32)
        for g in order:
            at = pl.ds(g * N_Y * ROWS + row, N_Y, stride=ROWS)
            out[at, :] = total
            total = decay * (total + sums[at, :])
    tail = sums[pl.ds(4, PEERS, stride=ROWS), :]
    lanes = iota((PEERS, 128), 1)
    right = []
    for c in range(2):
        own = (lanes >= 16 * c) & (lanes < 16 * c + 16)
        right.append(jnp.where(own, tail, 0.0))
        last = 16 * c if reverse else 16 * c + 15
        total = jnp.sum(jnp.where(lanes == last, tail, 0.0), axis=1, keepdims=True)
        right.append(jnp.where(own, total, 0.0))
    entering = jnp.dot(
        weights[...], jnp.concatenate(right, axis=0), precision=highest, preferred_element_type=f32
    )
    if requests is not None:
        entering = entering + requests[...]
    out[pl.ds(4, PEERS, stride=ROWS), :] = entering


def carry(sums, weights, down, requests=None):
    shape = jax.ShapeDtypeStruct((PEERS * ROWS, 128), f32)
    if requests is None:
        kernel = lambda *refs: carry_kernel(True, *refs[:3], None, refs[3])
        return pl.pallas_call(
            kernel, in_specs=[VMEM] * 3, out_specs=VMEM, out_shape=shape,
            compiler_params=params(8), name="carry_back",
        )(sums, weights, down)
    return pl.pallas_call(
        functools.partial(carry_kernel, False), in_specs=[VMEM] * 4, out_specs=VMEM, out_shape=shape,
        compiler_params=params(8), name="carry",
    )(sums, weights, down, requests)


def stack_rows(*parts):
    return jnp.concatenate(parts, axis=0)


def stack_lanes(*parts):
    return jnp.concatenate(parts, axis=1)


def observe_kernel(
    level, scaled, turned_high, turned_low, entered, coly, rates, level_weights,
    forced_out, msg, left, both, spread, marks,
):
    decay_y = grow(coly[...], CH, -1.0)
    pick = lambda row: entered[pl.ds(row, PEERS, stride=ROWS), :]
    high, low = split(stack_rows(stack_lanes(pick(0), pick(1)), stack_lanes(pick(2), pick(3))))
    sums = upper()
    eh, el = split(decay_y * (mm(high, sums) + mm(low, sums)))
    dh, dl = split(decay_y)
    requests = pick(4).T
    for x in range(XB):
        at = slice(x * LEVELS, (x + 1) * LEVELS)
        part = scaled[at, :]
        high, low = split(part)
        left[at, 0:256], left[at, 256:512], left[at, 512:768] = high, low, high
        col = stack_lanes(requests[x : x + 1, :], requests[16 + x : 17 + x, :])
        high, low = split(part * col)
        left[at, 768:1024], left[at, 1024:1280], left[at, 1280:1536] = high, low, high
    total = level[...] + mm(left[...], stack_rows(eh, eh, el, dh, dh, dl))
    both[:, 0:256], both[:, 256:512] = split(total)

    weights = level_weights[...]
    departures = []
    for r in range(0, CAP, 2):
        first, second = REQ + 3 * r, REQ + 3 * r + 3
        row = lambda i: stack_lanes(requests[first + i : first + i + 1, :], requests[second + i : second + i + 1, :])
        where = row(0).astype(jnp.int32) - 1
        valid = where >= 0
        at_x, at_y = where // YB, where % YB
        at_x = jnp.where(valid, at_x, -1)
        chosen = jnp.where(iota((YB, 256), 0) == at_y, 1.0, 0.0).astype(bf16)
        picked = mm(both[...], stack_rows(chosen, chosen))
        levels = jnp.zeros((LEVELS, 256), f32)
        for x in range(XB):
            levels = jnp.where(at_x == x, picked[x * LEVELS : (x + 1) * LEVELS, :], levels)
        total = jnp.sum(weights * softplus(levels), axis=0, keepdims=True)
        miss = jnp.where(valid, softplus(total) - row(1), 0.0)
        error = jnp.where(valid, row(2), 1.0)
        scale = miss / (error * error) * sigmoid(total)
        adjoint = scale * (weights * sigmoid(levels))
        high = adjoint.astype(bf16).astype(f32)
        low = adjoint - high
        lanes = 256 * r
        for x in range(XB):
            at = slice(x * LEVELS, (x + 1) * LEVELS)
            spread[at, lanes : lanes + 256] = jnp.where(at_x == x, high, 0.0).astype(bf16)
            spread[at, lanes + 256 : lanes + 512] = jnp.where(at_x == x, low, 0.0).astype(bf16)
        marks[:, lanes : lanes + 256] = chosen
        marks[:, lanes + 256 : lanes + 512] = chosen
        departures += [miss[:, :128], miss[:, 128:]]
    forced = mm_nt(spread[...], marks[...])
    forced_out[...] = forced

    gh, gl = split(forced)
    th, tl = turned_high[...], turned_low[...]
    along_x = mm(stack_lanes(th, tl, th), stack_rows(gh, gh, gl)) * decay_y
    for c in range(2):
        for h in range(2):
            msg[pl.ds(2 * c + h, PEERS, stride=ROWS), :] = along_x[128 * c : 128 * c + 128, 128 * h : 128 * h + 128]
    down = jnp.exp(rates[1:2, :] * (iota((YB, CH), 0).astype(f32) * (-1.0 / 4096.0)))
    dh, dl = split(down)
    weighed = mm(stack_lanes(gh, gl, gh), stack_rows(dh, dh, dl))
    running = jnp.zeros((1, CH), f32)
    rows = [None] * XB
    for x in range(XB - 1, -1, -1):
        at = slice(x * LEVELS, (x + 1) * LEVELS)
        running = running + jnp.sum(weighed[at, :] * scaled[at, :], axis=0, keepdims=True)
        rows[x] = running
    turned = [row[:, :128] for row in rows] + [row[:, 128:] for row in rows] + departures
    turned.append(jnp.zeros((128 - len(turned), 128), f32))
    msg[pl.ds(4, PEERS, stride=ROWS), :] = stack_rows(*turned).T


def observations(level, scaled, turned_high, turned_low, entered, coly, rates, level_weights):
    return pl.pallas_call(
        observe_kernel,
        in_specs=[VMEM] * 8,
        out_specs=[VMEM, VMEM],
        out_shape=[
            jax.ShapeDtypeStruct((XB * LEVELS, YB), f32),
            jax.ShapeDtypeStruct((PEERS * ROWS, 128), f32),
        ],
        scratch_shapes=[
            pltpu.VMEM((XB * LEVELS, 6 * 256), bf16),
            pltpu.VMEM((XB * LEVELS, 2 * YB), bf16),
            pltpu.VMEM((XB * LEVELS, 2 * PEERS * CAP), bf16),
            pltpu.VMEM((YB, 2 * PEERS * CAP), bf16),
        ],
        compiler_params=params(57),
        name="observations",
    )(level, scaled, turned_high, turned_low, entered, coly, rates, level_weights)


def planes_back_kernel(forced, turned_high, turned_low, coly, out, running, decay):
    b = pl.program_id(0)

    @pl.when(b == 0)
    def _():
        running[...] = jnp.zeros((CH, YB), f32)
        decay[...] = grow(coly[...], CH, -1.0)

    gh, gl = split(forced[...])
    th, tl = turned_high[...], turned_low[...]
    none = jnp.zeros((LEVELS, YB), bf16)
    for i in range(DEEP - 1, -1, -1):
        half = slice(i * LEVELS, (i + 1) * LEVELS)
        at = slice(i // 2 * 128, i // 2 * 128 + 128)
        fill = lambda part: stack_rows(none, part[half]) if i % 2 else stack_rows(part[half], none)
        high, low = fill(gh), fill(gl)
        back = mm(stack_lanes(th[:, at], tl[:, at]), stack_rows(high, high)) + mm(th[:, at], low)
        running[...] = running[...] + back * decay[...]
        out[i] = running[...]


def planes_back(forced, turned_high, turned_low, coly):
    last = XB // DEEP - 1
    lanes = pl.BlockSpec((CH, DEEP * LEVELS), lambda b: (0, last - b))
    field = pltpu.VMEM((CH, YB), f32)
    return pl.pallas_call(
        planes_back_kernel,
        grid=(XB // DEEP,),
        in_specs=[pl.BlockSpec((DEEP * LEVELS, YB), lambda b: (last - b, 0)), lanes, lanes, whole((CH, 128))],
        out_specs=pl.BlockSpec((DEEP, CH, YB), lambda b: (last - b, 0, 0)),
        out_shape=jax.ShapeDtypeStruct((XB, CH, YB), f32),
        scratch_shapes=[field, field],
        compiler_params=params(57),
        cost_estimate=pl.CostEstimate(flops=2 * 4 * 4096 * 256 * 256, bytes_accessed=8 << 20, transcendentals=1 << 16),
        name="planes_back",
    )(forced, turned_high, turned_low, coly)


def join_kernel(control, running, colx, coly, out):
    high, low = split(running[...].reshape(XB * BLOCK, YB))
    sums = lower()
    summed = mm(high, sums) + mm(low, sums)
    factor = wide(jnp.exp(colx[...]))
    scale = grow(coly[...], BLOCK)
    for x in range(XB):
        out[x] = control[x] + scale * summed[x * BLOCK : (x + 1) * BLOCK, :]
        scale = scale * factor


def join(control, running, colx, coly):
    return pl.pallas_call(
        join_kernel,
        grid=(CH // BLOCK,),
        in_specs=[PLANES, PLANES, STEPS, STEPS],
        out_specs=PLANES,
        out_shape=jax.ShapeDtypeStruct((XB, CH, YB), f32),
        compiler_params=params(57),
        cost_estimate=pl.CostEstimate(flops=2 * 2 * 4096 * 256 * 256, bytes_accessed=12 << 20, transcendentals=0),
        name="join",
    )(control, running, colx, coly)


def final_kernel(partial, entered, colx, coly, out, whole_a, whole_b, sems):
    b = pl.program_id(0)
    start = (b % HALF) * (BLOCK * ROWS)
    entering = jnp.concatenate(
        [entered[pl.ds(start + 2 * (b // HALF) + h, BLOCK, stride=ROWS), :] for h in range(2)], axis=1
    )
    high, low = split(entering)
    sums = lower()
    entering = mm(high, sums) + mm(low, sums)
    tail = entered[pl.ds(start + 4, BLOCK, stride=ROWS), :]
    mine = jnp.where(b < HALF, tail, pltpu.roll(tail, 112, 1))
    factor = wide(jnp.exp(colx[...]))
    scale = grow(coly[...], BLOCK)
    for x in range(XB):
        plane = partial[x] + scale * (entering + mine[:, x : x + 1])
        scale = scale * factor
        at = pl.ds(b * (BLOCK * XB) + x, BLOCK, stride=XB)
        whole_a[at, :] = plane[:, :128]
        whole_b[at, :] = plane[:, 128:]

    def copies(step):
        at = pl.ds(pl.multiple_of(step * (BLOCK * XB), BLOCK * XB), BLOCK * XB)
        return (
            pltpu.make_async_copy(whole_a.at[at, :], out.at[at, pl.ds(0, 128)], sems.at[step, 0]),
            pltpu.make_async_copy(whole_b.at[at, :], out.at[at, pl.ds(128, 128)], sems.at[step, 1]),
        )

    for copy in copies(b):
        copy.start()

    @pl.when(b == CH // BLOCK - 1)
    def _():
        for step in range(CH // BLOCK):
            for copy in copies(step):
                copy.wait()


def final(partial, entered, colx, coly):
    return pl.pallas_call(
        final_kernel,
        grid=(CH // BLOCK,),
        in_specs=[PLANES, whole((PEERS * ROWS, 128)), STEPS, STEPS],
        out_specs=ANY,
        out_shape=jax.ShapeDtypeStruct((CH * XB, YB), f32),
        scratch_shapes=[
            pltpu.VMEM((CH * XB, 128), f32),
            pltpu.VMEM((CH * XB, 128), f32),
            pltpu.SemaphoreType.DMA((CH // BLOCK, 2)),
        ],
        compiler_params=params(57),
        name="final",
    )(partial, entered, colx, coly)


def departures_kernel(rank, returned, out):
    total = jnp.zeros((1, OBS), f32)
    values = returned[pl.ds(4, PEERS, stride=ROWS), :]
    for r in range(CAP):
        value = values[:, REQ + r : REQ + r + 1]
        total = total + jnp.sum(jnp.where(rank[...] == float(r), value, 0.0), axis=0, keepdims=True)
    out[...] = total


def departures(rank, returned):
    return pl.pallas_call(
        departures_kernel,
        in_specs=[VMEM] * 2,
        out_specs=VMEM,
        out_shape=jax.ShapeDtypeStruct((1, OBS), f32),
        compiler_params=params(8),
        cost_estimate=pl.CostEstimate(flops=1 << 20, bytes_accessed=1 << 19, transcendentals=0),
        name="departures",
    )(rank, returned)


def everywhere(rows):
    shaped = rows.reshape(PEERS * ROWS, 1, 128)
    moved = lax.all_to_all(shaped, ("gx", "gy"), split_axis=0, concat_axis=0, tiled=True)
    return moved.reshape(PEERS * ROWS, 128)


def body(
    control,
    background,
    vert_factor,
    length_rates,
    flash_weights,
    level_weights,
    obs_owner,
    obs_cell,
    obs_count,
    flash_obs,
    obs_error,
):
    shape = control.shape
    flat = control.reshape(CH * XB, YB)
    msg, colx, coly, control_planes = edges(flat, length_rates)
    asked = everywhere(msg)

    gx, gy = lax.axis_index("gx"), lax.axis_index("gy")
    place = jnp.stack([gx, gy, gx * N_Y + gy]).astype(jnp.int32)
    rates = length_rates.reshape(2, CH)
    requests, rank, ahead, behind, down = prepare(
        place, obs_count, rates, obs_owner.reshape(1, OBS), obs_cell.reshape(1, OBS),
        flash_obs.reshape(1, OBS), obs_error.reshape(1, OBS),
    )
    step_x, step_y = length_rates[0] / (XB * N_X), length_rates[1] / (YB * N_Y)
    gain = jnp.sqrt(-jnp.expm1(-2.0 * step_x)) * jnp.sqrt(-jnp.expm1(-2.0 * step_y))
    mixed = flash_weights[:, :, None] * vert_factor * gain[:, None, :]
    matrix = mixed.transpose(1, 0, 2).reshape(LEVELS, CH)
    cc = local(control_planes, colx, coly)
    asked, cc = lax.optimization_barrier((asked, cc))
    entered = everywhere(carry(asked, ahead, down, requests))
    share = background_share(background.reshape(4, LEVELS * XB, YB), jnp.repeat(flash_weights.T, XB, axis=0))
    level, scaled, turned_high, turned_low = levels_of(cc, share, coly, rates, matrix)
    forced, msg_back = observations(
        level, scaled, turned_high, turned_low, entered, coly, rates, level_weights.reshape(LEVELS, 1)
    )
    returned = everywhere(msg_back)
    planes = planes_back(forced, turned_high, turned_low, coly)
    returned, planes = lax.optimization_barrier((returned, planes))
    entered_back = everywhere(carry(returned, behind, down))
    partial = join(control_planes, planes, colx, coly)
    departure = departures(rank, returned)
    grad = final(partial, entered_back, colx, coly)
    return (grad.reshape(shape), departure.reshape(OBS))


def solution(mesh):
    placed = (
        P(None, None, "gx", "gy"),
        P(None, None, "gx", "gy"),
        P(),
        P(),
        P(),
        P(),
        P(("gx", "gy"), None),
        P(("gx", "gy")),
        P(("gx", "gy")),
        P(("gx", "gy")),
        P(("gx", "gy")),
    )
    return jax.shard_map(
        body,
        mesh=mesh,
        in_specs=placed,
        out_specs=(P(None, None, "gx", "gy"), P(("gx", "gy"))),
        check_vma=False,
    )
```

```python
import functools

import jax
import jax.numpy as jnp
from jax import lax
from jax.experimental import pallas as pl
from jax.experimental.pallas import tpu as pltpu
from jax.sharding import PartitionSpec as P

highest = lax.Precision.HIGHEST
f32 = jnp.float32
bf16 = jnp.bfloat16

CH, LEVELS, XB, YB = 256, 64, 16, 256
OBS, PEERS, CAP = 512, 128, 8
N_X, N_Y = 8, 16
BLOCK = 128
SUB = 32
HALF = 128 // BLOCK
DEEP = 8
REQ = 32
ROWS = 5
MIB = 1024 * 1024


def iota(shape, dim):
    return lax.broadcasted_iota(jnp.int32, shape, dim)


def split(value):
    high = value.astype(bf16)
    return high, (value - high.astype(f32)).astype(bf16)


def split3(value):
    high = value.astype(bf16)
    rest = value - high.astype(f32)
    middle = rest.astype(bf16)
    return high, middle, (rest - middle.astype(f32)).astype(bf16)


def mm(a, b):
    return jnp.dot(a, b, preferred_element_type=f32)


def mm_nt(a, b):
    return lax.dot_general(a, b, (((1,), (1,)), ((), ())), preferred_element_type=f32)


def wide(col):
    return jnp.concatenate([col, col], axis=1)


def upper():
    return jnp.where(iota((YB, YB), 0) <= iota((YB, YB), 1), 1.0, 0.0).astype(bf16)


def lower():
    return jnp.where(iota((YB, YB), 0) >= iota((YB, YB), 1), 1.0, 0.0).astype(bf16)


def softplus(x):
    return jnp.maximum(x, 0.0) + jnp.log1p(jnp.exp(-jnp.abs(x)))


def sigmoid(x):
    return 1.0 / (1.0 + jnp.exp(-x))


def take_plane(halves, x, rows, *lead):
    at = lead + (pl.ds(x, rows, stride=XB), slice(None))
    return jnp.concatenate([half[at] for half in halves], axis=1)


def params(mib, **more):
    return pltpu.CompilerParams(vmem_limit_bytes=mib * MIB, **more)


def whole(shape):
    return pl.BlockSpec(shape, lambda b: (0,) * len(shape))


VMEM = pl.BlockSpec(memory_space=pltpu.VMEM)
SMEM = pl.BlockSpec(memory_space=pltpu.SMEM)
ANY = pl.BlockSpec(memory_space=pl.ANY)
CONTROL = [
    pl.BlockSpec((BLOCK * XB, 128), lambda b: (b, 0)),
    pl.BlockSpec((BLOCK * XB, 128), lambda b: (b, 1)),
]
PLANES = pl.BlockSpec((XB, BLOCK, YB), lambda b: (0, b, 0))
STEPS = pl.BlockSpec((BLOCK, 128), lambda b: (b, 0))


def grow(step_y, rows, sign=1.0):
    return jnp.exp(wide(step_y) * (iota((rows, YB), 1).astype(f32) * sign))


def edges_kernel(control_a, control_b, rates, msg, colx, coly, planes, line, tail):
    b = pl.program_id(0)

    @pl.when(b == 0)
    def _():
        for i, (out, count) in enumerate(((colx, 128.0), (coly, 4096.0))):
            for v in range(4):
                line[0:1, 0:LEVELS] = rates[i, v : v + 1, :]
                turned = jnp.broadcast_to(line[0:1, :], (128, 128)).T
                out[v * LEVELS : (v + 1) * LEVELS, :] = turned[0:LEVELS, :] * (1.0 / count)
        tail[...] = jnp.zeros((PEERS, 128), f32)

    place = iota((SUB, 128), 1) - 16 * (b // HALF)
    for s in range(0, BLOCK, SUB):
        rows = pl.ds(pl.multiple_of(b * BLOCK + s, SUB), SUB)
        factor = wide(jnp.exp(colx[rows, :]))
        scale = grow(coly[rows, :], SUB)
        running = jnp.zeros((SUB, YB), f32)
        sums = jnp.zeros((SUB, 128), f32)
        for x in range(XB):
            plane = take_plane((control_a, control_b), s * XB + x, SUB)
            planes[x, s : s + SUB, :] = plane
            running = running + plane * scale
            scale = scale * factor
            sums = jnp.where(place == x, jnp.sum(running, axis=1, keepdims=True), sums)
        start = ((b % HALF) * BLOCK + s) * ROWS + 2 * (b // HALF)
        msg[pl.ds(start, SUB, stride=ROWS), :] = running[:, :128]
        msg[pl.ds(start + 1, SUB, stride=ROWS), :] = running[:, 128:]
        back = pl.ds(pl.multiple_of((b % HALF) * BLOCK + s, SUB), SUB)
        tail[back, :] = tail[back, :] + sums

    @pl.when(b == CH // BLOCK - 1)
    def _():
        msg[pl.ds(4, PEERS, stride=ROWS), :] = tail[...]


def edges(control, length_rates):
    return pl.pallas_call(
        edges_kernel,
        grid=(CH // BLOCK,),
        in_specs=CONTROL + [whole((2, 4, LEVELS))],
        out_specs=[whole((PEERS * ROWS, 128)), whole((CH, 128)), whole((CH, 128)), PLANES],
        out_shape=[
            jax.ShapeDtypeStruct((PEERS * ROWS, 128), f32),
            jax.ShapeDtypeStruct((CH, 128), f32),
            jax.ShapeDtypeStruct((CH, 128), f32),
            jax.ShapeDtypeStruct((XB, CH, YB), f32),
        ],
        scratch_shapes=[pltpu.VMEM((8, 128), f32), pltpu.VMEM((PEERS, 128), f32)],
        compiler_params=params(57),
        name="edges",
    )(control, control, length_rates)


def prepare_kernel(place, count, rates, owner, cell, flash, sigma, requests, rank_out, ahead, behind, down):
    live = iota((PEERS, OBS), 1) < count[0]
    chosen = (owner[...] == iota((PEERS, OBS), 0)) & live
    earlier = jnp.where(iota((OBS, OBS), 0) < iota((OBS, OBS), 1), 1.0, 0.0).astype(bf16)
    rank = mm(jnp.where(chosen, 1.0, 0.0).astype(bf16), earlier)
    rank = jnp.where(chosen, rank, -1.0)
    rank_out[...] = rank
    rows = iota((8, OBS), 0)
    values = jnp.where(
        rows == 0,
        cell[...].astype(f32) + 1.0,
        jnp.where(rows == 1, flash[...], jnp.where(rows == 2, sigma[...], 0.0)),
    )
    values = jnp.concatenate([values, jnp.zeros((120, OBS), f32)], axis=0)
    pieces = split3(jnp.concatenate([values[:, i : i + 128].T for i in range(0, OBS, 128)], axis=0))
    total = jnp.zeros((PEERS, 128), f32)
    for r in range(CAP):
        taken = jnp.where(rank == float(r), 1.0, 0.0).astype(bf16)
        found = (mm(taken, pieces[0]) + mm(taken, pieces[1])) + mm(taken, pieces[2])
        total = total + pltpu.roll(found, REQ + 3 * r, 1)
    requests[...] = total

    me = place[2]
    d, e = iota((PEERS, PEERS), 0), iota((PEERS, PEERS), 1)
    far_x = (d // N_Y) - (e // N_Y)
    far_y = (d % N_Y) - (e % N_Y)
    for c in range(2):
        mine = iota((2, CH), 1) == me + 128 * c
        rate = jnp.sum(jnp.where(mine, rates[...], 0.0), axis=1, keepdims=True)
        down_x = rate[0:1, :] * (XB / 128.0)
        down_y = rate[1:2, :] * (YB / 4096.0)
        down[c : c + 1, :] = jnp.broadcast_to(jnp.exp(-down_x), (1, 128))
        along = jnp.exp(-jnp.abs(far_y).astype(f32) * down_y)
        across = along * jnp.exp(-jnp.abs(far_x).astype(f32) * down_x)
        for out, sign in ((ahead, 1), (behind, -1)):
            past_x, past_y = far_x * sign > 0, far_y * sign > 0
            out[:, 256 * c : 256 * c + 128] = jnp.where((far_x == 0) & past_y, along, 0.0)
            out[:, 256 * c + 128 : 256 * c + 256] = jnp.where(past_x & past_y, across, 0.0)
    down[2:8, :] = jnp.zeros((6, 128), f32)


def prepare(place, count, rates, owner, cell, flash, sigma):
    return pl.pallas_call(
        prepare_kernel,
        in_specs=[SMEM, SMEM] + [VMEM] * 5,
        out_specs=[VMEM] * 5,
        out_shape=[
            jax.ShapeDtypeStruct((PEERS, 128), f32),
            jax.ShapeDtypeStruct((PEERS, OBS), f32),
            jax.ShapeDtypeStruct((PEERS, 4 * 128), f32),
            jax.ShapeDtypeStruct((PEERS, 4 * 128), f32),
            jax.ShapeDtypeStruct((8, 128), f32),
        ],
        compiler_params=params(16),
        cost_estimate=pl.CostEstimate(flops=1 << 30, bytes_accessed=1 << 20, transcendentals=1 << 16),
        name="prepare",
    )(place, count, rates, owner, cell, flash, sigma)


def local_kernel(planes, colx, coly, cc):
    sums = upper()
    for s in range(0, BLOCK, SUB):
        at = slice(s, s + SUB)
        factor = wide(jnp.exp(colx[at, :]))
        scale = grow(coly[at, :], SUB)
        running = jnp.zeros((SUB, YB), f32)
        highs, lows = [], []
        for x in range(XB):
            running = running + planes[x, at, :] * scale
            scale = scale * factor
            high, low = split(running)
            highs.append(high)
            lows.append(low)
        summed = mm(jnp.concatenate(highs, axis=0), sums) + mm(jnp.concatenate(lows, axis=0), sums)
        cc[:, at, :] = summed.reshape(XB, SUB, YB)


def local(planes, colx, coly):
    return pl.pallas_call(
        local_kernel,
        grid=(CH // BLOCK,),
        in_specs=[PLANES, STEPS, STEPS],
        out_specs=PLANES,
        out_shape=jax.ShapeDtypeStruct((XB, CH, YB), f32),
        compiler_params=params(57),
        cost_estimate=pl.CostEstimate(flops=2 * 2 * 4096 * 256 * 256, bytes_accessed=8 << 20, transcendentals=1 << 16),
        name="local",
    )(planes, colx, coly)


def share_kernel(background, weights, share, half_a, half_b):
    total = background[0] * weights[:, 0:1]
    for v in range(1, 4):
        total = total + background[v] * weights[:, v : v + 1]
    half_a[...] = total[:, :128]
    half_b[...] = total[:, 128:]
    for x in range(XB):
        share[x] = take_plane((half_a, half_b), x, 32)


def background_share(background, weights):
    return pl.pallas_call(
        share_kernel,
        grid=(2,),
        in_specs=[
            pl.BlockSpec((4, 512, YB), lambda b: (0, b, 0)),
            pl.BlockSpec((512, 4), lambda b: (b, 0)),
        ],
        out_specs=pl.BlockSpec((XB, 32, YB), lambda b: (0, b, 0)),
        out_shape=jax.ShapeDtypeStruct((XB, LEVELS, YB), f32),
        scratch_shapes=[pltpu.VMEM((512, 128), f32), pltpu.VMEM((512, 128), f32)],
        compiler_params=params(57),
        cost_estimate=pl.CostEstimate(flops=1 << 21, bytes_accessed=5 << 20, transcendentals=0),
        name="share",
    )(background, weights)


def levels_kernel(cc, share, coly, rates, matrix, level, scaled, turned_high, turned_low, decay):
    b = pl.program_id(0)

    @pl.when(b == 0)
    def _():
        decay[...] = grow(coly[...], CH, -1.0)

    for i in range(DEEP):
        x = (DEEP * b + i).astype(f32)
        at = slice(i * LEVELS, (i + 1) * LEVELS)
        part = matrix[...] * jnp.exp(rates[0:1, :] * (x * (-1.0 / 128.0)))
        scaled[at, :] = part
        mh, ml = split(part)
        high, low = split(decay[...] * cc[i])
        pair = mm(jnp.concatenate([mh, ml], axis=0), high)
        level[at, :] = (pair[:LEVELS] + (pair[LEVELS:] + mm(mh, low))) + share[i]
    for i in range(0, DEEP * LEVELS, 128):
        part = scaled[i : i + 128, :]
        turned = jnp.concatenate([part[:, :128].T, part[:, 128:].T], axis=0)
        turned_high[:, i : i + 128], turned_low[:, i : i + 128] = split(turned)


def levels_of(cc, share, coly, rates, matrix):
    two = lambda shape: pl.BlockSpec(shape, lambda b: (b,) + (0,) * (len(shape) - 1))
    lanes = pl.BlockSpec((CH, DEEP * LEVELS), lambda b: (0, b))
    return pl.pallas_call(
        levels_kernel,
        grid=(XB // DEEP,),
        in_specs=[two((DEEP, CH, YB)), two((DEEP, LEVELS, YB)), whole((CH, 128)), whole((2, CH)), whole((LEVELS, CH))],
        out_specs=[two((DEEP * LEVELS, YB)), two((DEEP * LEVELS, CH)), lanes, lanes],
        out_shape=[
            jax.ShapeDtypeStruct((XB * LEVELS, YB), f32),
            jax.ShapeDtypeStruct((XB * LEVELS, CH), f32),
            jax.ShapeDtypeStruct((CH, XB * LEVELS), bf16),
            jax.ShapeDtypeStruct((CH, XB * LEVELS), bf16),
        ],
        scratch_shapes=[pltpu.VMEM((CH, YB), f32)],
        compiler_params=params(57),
        cost_estimate=pl.CostEstimate(flops=2 * 3 * 1024 * 256 * 256, bytes_accessed=8 << 20, transcendentals=1 << 18),
        name="levels",
    )(cc, share, coly, rates, matrix)


def carry_kernel(reverse, sums, weights, down, requests, out):
    order = list(range(N_X))
    if reverse:
        order = order[::-1]
    for row in range(4):
        decay = down[row // 2 : row // 2 + 1, :]
        total = jnp.zeros((N_Y, 128), f32)
        for g in order:
            at = pl.ds(g * N_Y * ROWS + row, N_Y, stride=ROWS)
            out[at, :] = total
            total = decay * (total + sums[at, :])
    tail = sums[pl.ds(4, PEERS, stride=ROWS), :]
    lanes = iota((PEERS, 128), 1)
    right = []
    for c in range(2):
        own = (lanes >= 16 * c) & (lanes < 16 * c + 16)
        right.append(jnp.where(own, tail, 0.0))
        last = 16 * c if reverse else 16 * c + 15
        total = jnp.sum(jnp.where(lanes == last, tail, 0.0), axis=1, keepdims=True)
        right.append(jnp.where(own, total, 0.0))
    entering = jnp.dot(
        weights[...], jnp.concatenate(right, axis=0), precision=highest, preferred_element_type=f32
    )
    if requests is not None:
        entering = entering + requests[...]
    out[pl.ds(4, PEERS, stride=ROWS), :] = entering


def carry(sums, weights, down, requests=None):
    shape = jax.ShapeDtypeStruct((PEERS * ROWS, 128), f32)
    if requests is None:
        kernel = lambda *refs: carry_kernel(True, *refs[:3], None, refs[3])
        return pl.pallas_call(
            kernel, in_specs=[VMEM] * 3, out_specs=VMEM, out_shape=shape,
            compiler_params=params(8), name="carry_back",
        )(sums, weights, down)
    return pl.pallas_call(
        functools.partial(carry_kernel, False), in_specs=[VMEM] * 4, out_specs=VMEM, out_shape=shape,
        compiler_params=params(8), name="carry",
    )(sums, weights, down, requests)


def stack_rows(*parts):
    return jnp.concatenate(parts, axis=0)


def stack_lanes(*parts):
    return jnp.concatenate(parts, axis=1)


def observe_kernel(
    level, scaled, turned_high, turned_low, entered, coly, rates, level_weights,
    forced_out, msg, left, both, spread, marks, line,
):
    decay_y = grow(coly[...], CH, -1.0)
    pick = lambda row: entered[pl.ds(row, PEERS, stride=ROWS), :]
    high, low = split(stack_rows(stack_lanes(pick(0), pick(1)), stack_lanes(pick(2), pick(3))))
    sums = upper()
    eh, el = split(decay_y * (mm(high, sums) + mm(low, sums)))
    dh, dl = split(decay_y)
    requests = pick(4).T
    for x in range(XB):
        at = slice(x * LEVELS, (x + 1) * LEVELS)
        part = scaled[at, :]
        high, low = split(part)
        left[at, 0:256], left[at, 256:512], left[at, 512:768] = high, low, high
        col = stack_lanes(requests[x : x + 1, :], requests[16 + x : 17 + x, :])
        high, low = split(part * col)
        left[at, 768:1024], left[at, 1024:1280], left[at, 1280:1536] = high, low, high
    total = level[...] + mm(left[...], stack_rows(eh, eh, el, dh, dh, dl))
    both[:, 0:256], both[:, 256:512] = split(total)

    line[0:1, 0:LEVELS] = level_weights[...]
    weights = wide(jnp.broadcast_to(line[0:1, :], (128, 128)).T[:LEVELS, :])
    departures = []
    for r in range(0, CAP, 2):
        first, second = REQ + 3 * r, REQ + 3 * r + 3
        row = lambda i: stack_lanes(requests[first + i : first + i + 1, :], requests[second + i : second + i + 1, :])
        where = row(0).astype(jnp.int32) - 1
        valid = where >= 0
        at_x, at_y = where // YB, where % YB
        at_x = jnp.where(valid, at_x, -1)
        chosen = jnp.where(iota((YB, 256), 0) == at_y, 1.0, 0.0).astype(bf16)
        picked = mm(both[...], stack_rows(chosen, chosen))
        levels = jnp.zeros((LEVELS, 256), f32)
        for x in range(XB):
            levels = jnp.where(at_x == x, picked[x * LEVELS : (x + 1) * LEVELS, :], levels)
        total = jnp.sum(weights * softplus(levels), axis=0, keepdims=True)
        miss = jnp.where(valid, softplus(total) - row(1), 0.0)
        error = jnp.where(valid, row(2), 1.0)
        scale = miss / (error * error) * sigmoid(total)
        adjoint = scale * (weights * sigmoid(levels))
        high = adjoint.astype(bf16).astype(f32)
        low = adjoint - high
        lanes = 256 * r
        for x in range(XB):
            at = slice(x * LEVELS, (x + 1) * LEVELS)
            spread[at, lanes : lanes + 256] = jnp.where(at_x == x, high, 0.0).astype(bf16)
            spread[at, lanes + 256 : lanes + 512] = jnp.where(at_x == x, low, 0.0).astype(bf16)
        marks[:, lanes : lanes + 256] = chosen
        marks[:, lanes + 256 : lanes + 512] = chosen
        departures += [miss[:, :128], miss[:, 128:]]
    forced = mm_nt(spread[...], marks[...])
    forced_out[...] = forced

    gh, gl = split(forced)
    th, tl = turned_high[...], turned_low[...]
    along_x = mm(stack_lanes(th, tl, th), stack_rows(gh, gh, gl)) * decay_y
    for c in range(2):
        for h in range(2):
            msg[pl.ds(2 * c + h, PEERS, stride=ROWS), :] = along_x[128 * c : 128 * c + 128, 128 * h : 128 * h + 128]
    down = jnp.exp(rates[1:2, :] * (iota((YB, CH), 0).astype(f32) * (-1.0 / 4096.0)))
    dh, dl = split(down)
    weighed = mm(stack_lanes(gh, gl, gh), stack_rows(dh, dh, dl))
    running = jnp.zeros((1, CH), f32)
    rows = [None] * XB
    for x in range(XB - 1, -1, -1):
        at = slice(x * LEVELS, (x + 1) * LEVELS)
        running = running + jnp.sum(weighed[at, :] * scaled[at, :], axis=0, keepdims=True)
        rows[x] = running
    turned = [row[:, :128] for row in rows] + [row[:, 128:] for row in rows] + departures
    turned.append(jnp.zeros((128 - len(turned), 128), f32))
    msg[pl.ds(4, PEERS, stride=ROWS), :] = stack_rows(*turned).T


def observations(level, scaled, turned_high, turned_low, entered, coly, rates, level_weights):
    return pl.pallas_call(
        observe_kernel,
        in_specs=[VMEM] * 8,
        out_specs=[VMEM, VMEM],
        out_shape=[
            jax.ShapeDtypeStruct((XB * LEVELS, YB), f32),
            jax.ShapeDtypeStruct((PEERS * ROWS, 128), f32),
        ],
        scratch_shapes=[
            pltpu.VMEM((XB * LEVELS, 6 * 256), bf16),
            pltpu.VMEM((XB * LEVELS, 2 * YB), bf16),
            pltpu.VMEM((XB * LEVELS, 2 * PEERS * CAP), bf16),
            pltpu.VMEM((YB, 2 * PEERS * CAP), bf16),
            pltpu.VMEM((8, 128), f32),
        ],
        compiler_params=params(57),
        name="observations",
    )(level, scaled, turned_high, turned_low, entered, coly, rates, level_weights)


def planes_back_kernel(forced, turned_high, turned_low, coly, out, running, decay):
    b = pl.program_id(0)

    @pl.when(b == 0)
    def _():
        running[...] = jnp.zeros((CH, YB), f32)
        decay[...] = grow(coly[...], CH, -1.0)

    gh, gl = split(forced[...])
    th, tl = turned_high[...], turned_low[...]
    none = jnp.zeros((LEVELS, YB), bf16)
    for i in range(DEEP - 1, -1, -1):
        half = slice(i * LEVELS, (i + 1) * LEVELS)
        at = slice(i // 2 * 128, i // 2 * 128 + 128)
        fill = lambda part: stack_rows(none, part[half]) if i % 2 else stack_rows(part[half], none)
        high, low = fill(gh), fill(gl)
        back = mm(stack_lanes(th[:, at], tl[:, at]), stack_rows(high, high)) + mm(th[:, at], low)
        running[...] = running[...] + back * decay[...]
        out[i] = running[...]


def planes_back(forced, turned_high, turned_low, coly):
    last = XB // DEEP - 1
    lanes = pl.BlockSpec((CH, DEEP * LEVELS), lambda b: (0, last - b))
    field = pltpu.VMEM((CH, YB), f32)
    return pl.pallas_call(
        planes_back_kernel,
        grid=(XB // DEEP,),
        in_specs=[pl.BlockSpec((DEEP * LEVELS, YB), lambda b: (last - b, 0)), lanes, lanes, whole((CH, 128))],
        out_specs=pl.BlockSpec((DEEP, CH, YB), lambda b: (last - b, 0, 0)),
        out_shape=jax.ShapeDtypeStruct((XB, CH, YB), f32),
        scratch_shapes=[field, field],
        compiler_params=params(57),
        cost_estimate=pl.CostEstimate(flops=2 * 4 * 4096 * 256 * 256, bytes_accessed=8 << 20, transcendentals=1 << 16),
        name="planes_back",
    )(forced, turned_high, turned_low, coly)


def join_kernel(control, running, colx, coly, out):
    sums = lower()
    for s in range(0, BLOCK, SUB):
        at = slice(s, s + SUB)
        high, low = split(running[:, at, :].reshape(XB * SUB, YB))
        summed = mm(high, sums) + mm(low, sums)
        factor = wide(jnp.exp(colx[at, :]))
        scale = grow(coly[at, :], SUB)
        for x in range(XB):
            out[x, at, :] = control[x, at, :] + scale * summed[x * SUB : (x + 1) * SUB, :]
            scale = scale * factor


def join(control, running, colx, coly):
    return pl.pallas_call(
        join_kernel,
        grid=(CH // BLOCK,),
        in_specs=[PLANES, PLANES, STEPS, STEPS],
        out_specs=PLANES,
        out_shape=jax.ShapeDtypeStruct((XB, CH, YB), f32),
        compiler_params=params(57),
        cost_estimate=pl.CostEstimate(flops=2 * 2 * 4096 * 256 * 256, bytes_accessed=12 << 20, transcendentals=0),
        name="join",
    )(control, running, colx, coly)


def final_kernel(partial, entered, colx, coly, out, whole_a, whole_b, sems):
    b = pl.program_id(0)
    start = (b % HALF) * (BLOCK * ROWS)
    entering = jnp.concatenate(
        [entered[pl.ds(start + 2 * (b // HALF) + h, BLOCK, stride=ROWS), :] for h in range(2)], axis=1
    )
    high, low = split(entering)
    sums = lower()
    entering = mm(high, sums) + mm(low, sums)
    tail = entered[pl.ds(start + 4, BLOCK, stride=ROWS), :]
    mine = jnp.where(b < HALF, tail, pltpu.roll(tail, 112, 1))
    for s in range(0, BLOCK, SUB):
        own = slice(s, s + SUB)
        factor = wide(jnp.exp(colx[own, :]))
        scale = grow(coly[own, :], SUB)
        for x in range(XB):
            plane = partial[x, own, :] + scale * (entering[own, :] + mine[own, x : x + 1])
            scale = scale * factor
            at = pl.ds((b * BLOCK + s) * XB + x, SUB, stride=XB)
            whole_a[at, :] = plane[:, :128]
            whole_b[at, :] = plane[:, 128:]

    def copies(step):
        at = pl.ds(pl.multiple_of(step * (BLOCK * XB), BLOCK * XB), BLOCK * XB)
        return (
            pltpu.make_async_copy(whole_a.at[at, :], out.at[at, pl.ds(0, 128)], sems.at[step, 0]),
            pltpu.make_async_copy(whole_b.at[at, :], out.at[at, pl.ds(128, 128)], sems.at[step, 1]),
        )

    for copy in copies(b):
        copy.start()

    @pl.when(b == CH // BLOCK - 1)
    def _():
        for step in range(CH // BLOCK):
            for copy in copies(step):
                copy.wait()


def final(partial, entered, colx, coly):
    return pl.pallas_call(
        final_kernel,
        grid=(CH // BLOCK,),
        in_specs=[PLANES, whole((PEERS * ROWS, 128)), STEPS, STEPS],
        out_specs=ANY,
        out_shape=jax.ShapeDtypeStruct((CH * XB, YB), f32),
        scratch_shapes=[
            pltpu.VMEM((CH * XB, 128), f32),
            pltpu.VMEM((CH * XB, 128), f32),
            pltpu.SemaphoreType.DMA((CH // BLOCK, 2)),
        ],
        compiler_params=params(57),
        name="final",
    )(partial, entered, colx, coly)


def departures_kernel(rank, returned, out):
    total = jnp.zeros((1, OBS), f32)
    values = returned[pl.ds(4, PEERS, stride=ROWS), :]
    for r in range(CAP):
        value = values[:, REQ + r : REQ + r + 1]
        total = total + jnp.sum(jnp.where(rank[...] == float(r), value, 0.0), axis=0, keepdims=True)
    out[...] = total


def departures(rank, returned):
    return pl.pallas_call(
        departures_kernel,
        in_specs=[VMEM] * 2,
        out_specs=VMEM,
        out_shape=jax.ShapeDtypeStruct((1, OBS), f32),
        compiler_params=params(8),
        cost_estimate=pl.CostEstimate(flops=1 << 20, bytes_accessed=1 << 19, transcendentals=0),
        name="departures",
    )(rank, returned)


def everywhere(rows):
    shaped = rows.reshape(PEERS * ROWS, 1, 128)
    moved = lax.all_to_all(shaped, ("gx", "gy"), split_axis=0, concat_axis=0, tiled=True)
    return moved.reshape(PEERS * ROWS, 128)


def body(
    control,
    background,
    vert_factor,
    length_rates,
    flash_weights,
    level_weights,
    obs_owner,
    obs_cell,
    obs_count,
    flash_obs,
    obs_error,
):
    shape = control.shape
    flat = control.reshape(CH * XB, YB)
    msg, colx, coly, control_planes = edges(flat, length_rates)
    asked = everywhere(msg)

    gx, gy = lax.axis_index("gx"), lax.axis_index("gy")
    place = jnp.stack([gx, gy, gx * N_Y + gy]).astype(jnp.int32)
    rates = length_rates.reshape(2, CH)
    requests, rank, ahead, behind, down = prepare(
        place, obs_count, rates, obs_owner.reshape(1, OBS), obs_cell.reshape(1, OBS),
        flash_obs.reshape(1, OBS), obs_error.reshape(1, OBS),
    )
    step_x, step_y = length_rates[0] / (XB * N_X), length_rates[1] / (YB * N_Y)
    gain = jnp.sqrt(-jnp.expm1(-2.0 * step_x)) * jnp.sqrt(-jnp.expm1(-2.0 * step_y))
    mixed = flash_weights[:, :, None] * vert_factor * gain[:, None, :]
    matrix = mixed.transpose(1, 0, 2).reshape(LEVELS, CH)
    cc = local(control_planes, colx, coly)
    asked, cc = lax.optimization_barrier((asked, cc))
    entered = everywhere(carry(asked, ahead, down, requests))
    share = background_share(background.reshape(4, LEVELS * XB, YB), jnp.repeat(flash_weights.T, XB, axis=0))
    level, scaled, turned_high, turned_low = levels_of(cc, share, coly, rates, matrix)
    forced, msg_back = observations(
        level, scaled, turned_high, turned_low, entered, coly, rates, level_weights.reshape(1, LEVELS)
    )
    returned = everywhere(msg_back)
    planes = planes_back(forced, turned_high, turned_low, coly)
    returned, planes = lax.optimization_barrier((returned, planes))
    entered_back = everywhere(carry(returned, behind, down))
    partial = join(control_planes, planes, colx, coly)
    departure = departures(rank, returned)
    grad = final(partial, entered_back, colx, coly)
    return (grad.reshape(shape), departure.reshape(OBS))


def solution(mesh):
    placed = (
        P(None, None, "gx", "gy"),
        P(None, None, "gx", "gy"),
        P(),
        P(),
        P(),
        P(),
        P(("gx", "gy"), None),
        P(("gx", "gy")),
        P(("gx", "gy")),
        P(("gx", "gy")),
        P(("gx", "gy")),
    )
    return jax.shard_map(
        body,
        mesh=mesh,
        in_specs=placed,
        out_specs=(P(None, None, "gx", "gy"), P(("gx", "gy"))),
        check_vma=False,
    )
```

```python
import functools

import jax
import jax.numpy as jnp
from jax import lax
from jax.experimental import pallas as pl
from jax.experimental.pallas import tpu as pltpu
from jax.sharding import PartitionSpec as P

highest = lax.Precision.HIGHEST
f32 = jnp.float32
bf16 = jnp.bfloat16

CH, LEVELS, XB, YB = 256, 64, 16, 256
OBS, PEERS, CAP = 512, 128, 8
N_X, N_Y = 8, 16
BLOCK = 128
SUB = 32
HALF = 128 // BLOCK
DEEP = 8
REQ = 32
ROWS = 5
MIB = 1024 * 1024


def iota(shape, dim):
    return lax.broadcasted_iota(jnp.int32, shape, dim)


def split(value):
    high = value.astype(bf16)
    return high, (value - high.astype(f32)).astype(bf16)


def split3(value):
    high = value.astype(bf16)
    rest = value - high.astype(f32)
    middle = rest.astype(bf16)
    return high, middle, (rest - middle.astype(f32)).astype(bf16)


def mm(a, b):
    return jnp.dot(a, b, preferred_element_type=f32)


def mm_nt(a, b):
    return lax.dot_general(a, b, (((1,), (1,)), ((), ())), preferred_element_type=f32)


def wide(col):
    return jnp.concatenate([col, col], axis=1)


def upper():
    return jnp.where(iota((YB, YB), 0) <= iota((YB, YB), 1), 1.0, 0.0).astype(bf16)


def lower():
    return jnp.where(iota((YB, YB), 0) >= iota((YB, YB), 1), 1.0, 0.0).astype(bf16)


def softplus(x):
    return jnp.maximum(x, 0.0) + jnp.log1p(jnp.exp(-jnp.abs(x)))


def sigmoid(x):
    return 1.0 / (1.0 + jnp.exp(-x))


def take_plane(halves, x, rows, *lead):
    at = lead + (pl.ds(x, rows, stride=XB), slice(None))
    return jnp.concatenate([half[at] for half in halves], axis=1)


def params(mib, **more):
    return pltpu.CompilerParams(vmem_limit_bytes=mib * MIB, **more)


def whole(shape):
    return pl.BlockSpec(shape, lambda b: (0,) * len(shape))


VMEM = pl.BlockSpec(memory_space=pltpu.VMEM)
SMEM = pl.BlockSpec(memory_space=pltpu.SMEM)
ANY = pl.BlockSpec(memory_space=pl.ANY)
CONTROL = [
    pl.BlockSpec((BLOCK * XB, 128), lambda b: (b, 0)),
    pl.BlockSpec((BLOCK * XB, 128), lambda b: (b, 1)),
]
PLANES = pl.BlockSpec((XB, BLOCK, YB), lambda b: (0, b, 0))
STEPS = pl.BlockSpec((BLOCK, 128), lambda b: (b, 0))


def grow(step_y, rows, sign=1.0):
    return jnp.exp(wide(step_y) * (iota((rows, YB), 1).astype(f32) * sign))


def edges_kernel(control_a, control_b, rates, msg, colx, coly, planes, line, tail):
    b = pl.program_id(0)

    @pl.when(b == 0)
    def _():
        for i, (out, count) in enumerate(((colx, 128.0), (coly, 4096.0))):
            for v in range(4):
                line[0:1, 0:LEVELS] = rates[i, v : v + 1, :]
                turned = jnp.broadcast_to(line[0:1, :], (128, 128)).T
                out[v * LEVELS : (v + 1) * LEVELS, :] = turned[0:LEVELS, :] * (1.0 / count)
        tail[...] = jnp.zeros((PEERS, 128), f32)

    place = iota((SUB, 128), 1) - 16 * (b // HALF)
    for s in range(0, BLOCK, SUB):
        rows = pl.ds(pl.multiple_of(b * BLOCK + s, SUB), SUB)
        factor = wide(jnp.exp(colx[rows, :]))
        scale = grow(coly[rows, :], SUB)
        running = jnp.zeros((SUB, YB), f32)
        sums = jnp.zeros((SUB, 128), f32)
        for x in range(XB):
            plane = take_plane((control_a, control_b), s * XB + x, SUB)
            planes[x, s : s + SUB, :] = plane
            running = running + plane * scale
            scale = scale * factor
            sums = jnp.where(place == x, jnp.sum(running, axis=1, keepdims=True), sums)
        start = ((b % HALF) * BLOCK + s) * ROWS + 2 * (b // HALF)
        msg[pl.ds(start, SUB, stride=ROWS), :] = running[:, :128]
        msg[pl.ds(start + 1, SUB, stride=ROWS), :] = running[:, 128:]
        back = pl.ds(pl.multiple_of((b % HALF) * BLOCK + s, SUB), SUB)
        tail[back, :] = tail[back, :] + sums

    @pl.when(b == CH // BLOCK - 1)
    def _():
        msg[pl.ds(4, PEERS, stride=ROWS), :] = tail[...]


def edges(control, length_rates):
    return pl.pallas_call(
        edges_kernel,
        grid=(CH // BLOCK,),
        in_specs=CONTROL + [whole((2, 4, LEVELS))],
        out_specs=[whole((PEERS * ROWS, 128)), whole((CH, 128)), whole((CH, 128)), PLANES],
        out_shape=[
            jax.ShapeDtypeStruct((PEERS * ROWS, 128), f32),
            jax.ShapeDtypeStruct((CH, 128), f32),
            jax.ShapeDtypeStruct((CH, 128), f32),
            jax.ShapeDtypeStruct((XB, CH, YB), f32),
        ],
        scratch_shapes=[pltpu.VMEM((8, 128), f32), pltpu.VMEM((PEERS, 128), f32)],
        compiler_params=params(57),
        name="edges",
    )(control, control, length_rates)


def prepare_kernel(place, count, rates, owner, cell, flash, sigma, requests, rank_out, ahead, behind, down):
    live = iota((PEERS, OBS), 1) < count[0]
    chosen = (owner[...] == iota((PEERS, OBS), 0)) & live
    earlier = jnp.where(iota((OBS, OBS), 0) < iota((OBS, OBS), 1), 1.0, 0.0).astype(bf16)
    rank = mm(jnp.where(chosen, 1.0, 0.0).astype(bf16), earlier)
    rank = jnp.where(chosen, rank, -1.0)
    rank_out[...] = rank
    rows = iota((8, OBS), 0)
    values = jnp.where(
        rows == 0,
        cell[...].astype(f32) + 1.0,
        jnp.where(rows == 1, flash[...], jnp.where(rows == 2, sigma[...], 0.0)),
    )
    values = jnp.concatenate([values, jnp.zeros((120, OBS), f32)], axis=0)
    pieces = split3(jnp.concatenate([values[:, i : i + 128].T for i in range(0, OBS, 128)], axis=0))
    total = jnp.zeros((PEERS, 128), f32)
    for r in range(CAP):
        taken = jnp.where(rank == float(r), 1.0, 0.0).astype(bf16)
        found = (mm(taken, pieces[0]) + mm(taken, pieces[1])) + mm(taken, pieces[2])
        total = total + pltpu.roll(found, REQ + 3 * r, 1)
    requests[...] = total

    me = place[2]
    d, e = iota((PEERS, PEERS), 0), iota((PEERS, PEERS), 1)
    far_x = (d // N_Y) - (e // N_Y)
    far_y = (d % N_Y) - (e % N_Y)
    for c in range(2):
        mine = iota((2, CH), 1) == me + 128 * c
        rate = jnp.sum(jnp.where(mine, rates[...], 0.0), axis=1, keepdims=True)
        down_x = rate[0:1, :] * (XB / 128.0)
        down_y = rate[1:2, :] * (YB / 4096.0)
        down[c : c + 1, :] = jnp.broadcast_to(jnp.exp(-down_x), (1, 128))
        along = jnp.exp(-jnp.abs(far_y).astype(f32) * down_y)
        across = along * jnp.exp(-jnp.abs(far_x).astype(f32) * down_x)
        for out, sign in ((ahead, 1), (behind, -1)):
            past_x, past_y = far_x * sign > 0, far_y * sign > 0
            out[:, 256 * c : 256 * c + 128] = jnp.where((far_x == 0) & past_y, along, 0.0)
            out[:, 256 * c + 128 : 256 * c + 256] = jnp.where(past_x & past_y, across, 0.0)
    down[2:8, :] = jnp.zeros((6, 128), f32)


def prepare(place, count, rates, owner, cell, flash, sigma):
    return pl.pallas_call(
        prepare_kernel,
        in_specs=[SMEM, SMEM] + [VMEM] * 5,
        out_specs=[VMEM] * 5,
        out_shape=[
            jax.ShapeDtypeStruct((PEERS, 128), f32),
            jax.ShapeDtypeStruct((PEERS, OBS), f32),
            jax.ShapeDtypeStruct((PEERS, 4 * 128), f32),
            jax.ShapeDtypeStruct((PEERS, 4 * 128), f32),
            jax.ShapeDtypeStruct((8, 128), f32),
        ],
        compiler_params=params(16),
        cost_estimate=pl.CostEstimate(flops=1 << 30, bytes_accessed=1 << 20, transcendentals=1 << 16),
        name="prepare",
    )(place, count, rates, owner, cell, flash, sigma)


def local_kernel(planes, colx, coly, cc):
    sums = upper()
    for s in range(0, BLOCK, SUB):
        at = slice(s, s + SUB)
        factor = wide(jnp.exp(colx[at, :]))
        scale = grow(coly[at, :], SUB)
        running = jnp.zeros((SUB, YB), f32)
        highs, lows = [], []
        for x in range(XB):
            running = running + planes[x, at, :] * scale
            scale = scale * factor
            high, low = split(running)
            highs.append(high)
            lows.append(low)
        summed = mm(jnp.concatenate(highs, axis=0), sums) + mm(jnp.concatenate(lows, axis=0), sums)
        cc[:, at, :] = summed.reshape(XB, SUB, YB)


def local(planes, colx, coly):
    return pl.pallas_call(
        local_kernel,
        grid=(CH // BLOCK,),
        in_specs=[PLANES, STEPS, STEPS],
        out_specs=PLANES,
        out_shape=jax.ShapeDtypeStruct((XB, CH, YB), f32),
        compiler_params=params(57),
        cost_estimate=pl.CostEstimate(flops=2 * 2 * 4096 * 256 * 256, bytes_accessed=8 << 20, transcendentals=1 << 16),
        name="local",
    )(planes, colx, coly)


def share_kernel(background, weights, share, half_a, half_b):
    total = background[0] * weights[:, 0:1]
    for v in range(1, 4):
        total = total + background[v] * weights[:, v : v + 1]
    half_a[...] = total[:, :128]
    half_b[...] = total[:, 128:]
    for x in range(XB):
        share[x] = take_plane((half_a, half_b), x, 32)


def background_share(background, weights):
    return pl.pallas_call(
        share_kernel,
        grid=(2,),
        in_specs=[
            pl.BlockSpec((4, 512, YB), lambda b: (0, b, 0)),
            pl.BlockSpec((512, 4), lambda b: (b, 0)),
        ],
        out_specs=pl.BlockSpec((XB, 32, YB), lambda b: (0, b, 0)),
        out_shape=jax.ShapeDtypeStruct((XB, LEVELS, YB), f32),
        scratch_shapes=[pltpu.VMEM((512, 128), f32), pltpu.VMEM((512, 128), f32)],
        compiler_params=params(57),
        cost_estimate=pl.CostEstimate(flops=1 << 21, bytes_accessed=5 << 20, transcendentals=0),
        name="share",
    )(background, weights)


def levels_kernel(cc, share, coly, rates, matrix, level, scaled, turned_high, turned_low, decay):
    b = pl.program_id(0)

    @pl.when(b == 0)
    def _():
        decay[...] = grow(coly[...], CH, -1.0)

    for i in range(DEEP):
        x = (DEEP * b + i).astype(f32)
        at = slice(i * LEVELS, (i + 1) * LEVELS)
        part = matrix[...] * jnp.exp(rates[0:1, :] * (x * (-1.0 / 128.0)))
        scaled[at, :] = part
        mh, ml = split(part)
        high, low = split(decay[...] * cc[i])
        pair = mm(jnp.concatenate([mh, ml], axis=0), high)
        level[at, :] = (pair[:LEVELS] + (pair[LEVELS:] + mm(mh, low))) + share[i]
    for i in range(0, DEEP * LEVELS, 128):
        part = scaled[i : i + 128, :]
        turned = jnp.concatenate([part[:, :128].T, part[:, 128:].T], axis=0)
        turned_high[:, i : i + 128], turned_low[:, i : i + 128] = split(turned)


def levels_of(cc, share, coly, rates, matrix):
    two = lambda shape: pl.BlockSpec(shape, lambda b: (b,) + (0,) * (len(shape) - 1))
    lanes = pl.BlockSpec((CH, DEEP * LEVELS), lambda b: (0, b))
    return pl.pallas_call(
        levels_kernel,
        grid=(XB // DEEP,),
        in_specs=[two((DEEP, CH, YB)), two((DEEP, LEVELS, YB)), whole((CH, 128)), whole((2, CH)), whole((LEVELS, CH))],
        out_specs=[two((DEEP * LEVELS, YB)), two((DEEP * LEVELS, CH)), lanes, lanes],
        out_shape=[
            jax.ShapeDtypeStruct((XB * LEVELS, YB), f32),
            jax.ShapeDtypeStruct((XB * LEVELS, CH), f32),
            jax.ShapeDtypeStruct((CH, XB * LEVELS), bf16),
            jax.ShapeDtypeStruct((CH, XB * LEVELS), bf16),
        ],
        scratch_shapes=[pltpu.VMEM((CH, YB), f32)],
        compiler_params=params(57),
        cost_estimate=pl.CostEstimate(flops=2 * 3 * 1024 * 256 * 256, bytes_accessed=8 << 20, transcendentals=1 << 18),
        name="levels",
    )(cc, share, coly, rates, matrix)


def carry_kernel(reverse, sums, weights, down, requests, out):
    order = list(range(N_X))
    if reverse:
        order = order[::-1]
    for row in range(4):
        decay = down[row // 2 : row // 2 + 1, :]
        total = jnp.zeros((N_Y, 128), f32)
        for g in order:
            at = pl.ds(g * N_Y * ROWS + row, N_Y, stride=ROWS)
            out[at, :] = total
            total = decay * (total + sums[at, :])
    tail = sums[pl.ds(4, PEERS, stride=ROWS), :]
    lanes = iota((PEERS, 128), 1)
    right = []
    for c in range(2):
        own = (lanes >= 16 * c) & (lanes < 16 * c + 16)
        right.append(jnp.where(own, tail, 0.0))
        last = 16 * c if reverse else 16 * c + 15
        total = jnp.sum(jnp.where(lanes == last, tail, 0.0), axis=1, keepdims=True)
        right.append(jnp.where(own, total, 0.0))
    entering = jnp.dot(
        weights[...], jnp.concatenate(right, axis=0), precision=highest, preferred_element_type=f32
    )
    if requests is not None:
        entering = entering + requests[...]
    out[pl.ds(4, PEERS, stride=ROWS), :] = entering


def carry(sums, weights, down, requests=None):
    shape = jax.ShapeDtypeStruct((PEERS * ROWS, 128), f32)
    if requests is None:
        kernel = lambda *refs: carry_kernel(True, *refs[:3], None, refs[3])
        return pl.pallas_call(
            kernel, in_specs=[VMEM] * 3, out_specs=VMEM, out_shape=shape,
            compiler_params=params(8), name="carry_back",
        )(sums, weights, down)
    return pl.pallas_call(
        functools.partial(carry_kernel, False), in_specs=[VMEM] * 4, out_specs=VMEM, out_shape=shape,
        compiler_params=params(8), name="carry",
    )(sums, weights, down, requests)


def stack_rows(*parts):
    return jnp.concatenate(parts, axis=0)


def stack_lanes(*parts):
    return jnp.concatenate(parts, axis=1)


def observe_kernel(
    level_hbm, scaled, high_hbm, low_hbm, entered, coly, rates, level_weights,
    forced_hbm, msg, left, both, spread, marks, line, level, turned_high, turned_low, forced_out, sems,
):
    arrivals = [
        pltpu.make_async_copy(level_hbm, level, sems.at[0]),
        pltpu.make_async_copy(high_hbm, turned_high, sems.at[1]),
        pltpu.make_async_copy(low_hbm, turned_low, sems.at[2]),
    ]
    for copy in arrivals:
        copy.start()
    decay_y = grow(coly[...], CH, -1.0)
    pick = lambda row: entered[pl.ds(row, PEERS, stride=ROWS), :]
    high, low = split(stack_rows(stack_lanes(pick(0), pick(1)), stack_lanes(pick(2), pick(3))))
    sums = upper()
    eh, el = split(decay_y * (mm(high, sums) + mm(low, sums)))
    dh, dl = split(decay_y)
    requests = pick(4).T
    for x in range(XB):
        at = slice(x * LEVELS, (x + 1) * LEVELS)
        part = scaled[at, :]
        high, low = split(part)
        left[at, 0:256], left[at, 256:512], left[at, 512:768] = high, low, high
        col = stack_lanes(requests[x : x + 1, :], requests[16 + x : 17 + x, :])
        high, low = split(part * col)
        left[at, 768:1024], left[at, 1024:1280], left[at, 1280:1536] = high, low, high
    arrivals[0].wait()
    total = level[...] + mm(left[...], stack_rows(eh, eh, el, dh, dh, dl))
    both[:, 0:256], both[:, 256:512] = split(total)

    line[0:1, 0:LEVELS] = level_weights[...]
    weights = wide(jnp.broadcast_to(line[0:1, :], (128, 128)).T[:LEVELS, :])
    departures = []
    for r in range(0, CAP, 2):
        first, second = REQ + 3 * r, REQ + 3 * r + 3
        row = lambda i: stack_lanes(requests[first + i : first + i + 1, :], requests[second + i : second + i + 1, :])
        where = row(0).astype(jnp.int32) - 1
        valid = where >= 0
        at_x, at_y = where // YB, where % YB
        at_x = jnp.where(valid, at_x, -1)
        chosen = jnp.where(iota((YB, 256), 0) == at_y, 1.0, 0.0).astype(bf16)
        picked = mm(both[...], stack_rows(chosen, chosen))
        levels = jnp.zeros((LEVELS, 256), f32)
        for x in range(XB):
            levels = jnp.where(at_x == x, picked[x * LEVELS : (x + 1) * LEVELS, :], levels)
        total = jnp.sum(weights * softplus(levels), axis=0, keepdims=True)
        miss = jnp.where(valid, softplus(total) - row(1), 0.0)
        error = jnp.where(valid, row(2), 1.0)
        scale = miss / (error * error) * sigmoid(total)
        adjoint = scale * (weights * sigmoid(levels))
        high = adjoint.astype(bf16).astype(f32)
        low = adjoint - high
        lanes = 256 * r
        for x in range(XB):
            at = slice(x * LEVELS, (x + 1) * LEVELS)
            spread[at, lanes : lanes + 256] = jnp.where(at_x == x, high, 0.0).astype(bf16)
            spread[at, lanes + 256 : lanes + 512] = jnp.where(at_x == x, low, 0.0).astype(bf16)
        marks[:, lanes : lanes + 256] = chosen
        marks[:, lanes + 256 : lanes + 512] = chosen
        departures += [miss[:, :128], miss[:, 128:]]
    forced = mm_nt(spread[...], marks[...])
    forced_out[...] = forced
    leaving = pltpu.make_async_copy(forced_out, forced_hbm, sems.at[3])
    leaving.start()
    arrivals[1].wait()
    arrivals[2].wait()

    gh, gl = split(forced)
    th, tl = turned_high[...], turned_low[...]
    along_x = mm(stack_lanes(th, tl, th), stack_rows(gh, gh, gl)) * decay_y
    for c in range(2):
        for h in range(2):
            msg[pl.ds(2 * c + h, PEERS, stride=ROWS), :] = along_x[128 * c : 128 * c + 128, 128 * h : 128 * h + 128]
    down = jnp.exp(rates[1:2, :] * (iota((YB, CH), 0).astype(f32) * (-1.0 / 4096.0)))
    dh, dl = split(down)
    weighed = mm(stack_lanes(gh, gl, gh), stack_rows(dh, dh, dl))
    running = jnp.zeros((1, CH), f32)
    rows = [None] * XB
    for x in range(XB - 1, -1, -1):
        at = slice(x * LEVELS, (x + 1) * LEVELS)
        running = running + jnp.sum(weighed[at, :] * scaled[at, :], axis=0, keepdims=True)
        rows[x] = running
    turned = [row[:, :128] for row in rows] + [row[:, 128:] for row in rows] + departures
    turned.append(jnp.zeros((128 - len(turned), 128), f32))
    msg[pl.ds(4, PEERS, stride=ROWS), :] = stack_rows(*turned).T
    leaving.wait()


def observations(level, scaled, turned_high, turned_low, entered, coly, rates, level_weights):
    return pl.pallas_call(
        observe_kernel,
        in_specs=[ANY, VMEM, ANY, ANY] + [VMEM] * 4,
        out_specs=[ANY, VMEM],
        out_shape=[
            jax.ShapeDtypeStruct((XB * LEVELS, YB), f32),
            jax.ShapeDtypeStruct((PEERS * ROWS, 128), f32),
        ],
        scratch_shapes=[
            pltpu.VMEM((XB * LEVELS, 6 * 256), bf16),
            pltpu.VMEM((XB * LEVELS, 2 * YB), bf16),
            pltpu.VMEM((XB * LEVELS, 2 * PEERS * CAP), bf16),
            pltpu.VMEM((YB, 2 * PEERS * CAP), bf16),
            pltpu.VMEM((8, 128), f32),
            pltpu.VMEM((XB * LEVELS, YB), f32),
            pltpu.VMEM((CH, XB * LEVELS), bf16),
            pltpu.VMEM((CH, XB * LEVELS), bf16),
            pltpu.VMEM((XB * LEVELS, YB), f32),
            pltpu.SemaphoreType.DMA((4,)),
        ],
        compiler_params=params(57),
        name="observations",
    )(level, scaled, turned_high, turned_low, entered, coly, rates, level_weights)


def planes_back_kernel(forced, turned_high, turned_low, coly, out, running, decay):
    b = pl.program_id(0)

    @pl.when(b == 0)
    def _():
        running[...] = jnp.zeros((CH, YB), f32)
        decay[...] = grow(coly[...], CH, -1.0)

    gh, gl = split(forced[...])
    th, tl = turned_high[...], turned_low[...]
    none = jnp.zeros((LEVELS, YB), bf16)
    for i in range(DEEP - 1, -1, -1):
        half = slice(i * LEVELS, (i + 1) * LEVELS)
        at = slice(i // 2 * 128, i // 2 * 128 + 128)
        fill = lambda part: stack_rows(none, part[half]) if i % 2 else stack_rows(part[half], none)
        high, low = fill(gh), fill(gl)
        back = mm(stack_lanes(th[:, at], tl[:, at]), stack_rows(high, high)) + mm(th[:, at], low)
        running[...] = running[...] + back * decay[...]
        out[i] = running[...]


def planes_back(forced, turned_high, turned_low, coly):
    last = XB // DEEP - 1
    lanes = pl.BlockSpec((CH, DEEP * LEVELS), lambda b: (0, last - b))
    field = pltpu.VMEM((CH, YB), f32)
    return pl.pallas_call(
        planes_back_kernel,
        grid=(XB // DEEP,),
        in_specs=[pl.BlockSpec((DEEP * LEVELS, YB), lambda b: (last - b, 0)), lanes, lanes, whole((CH, 128))],
        out_specs=pl.BlockSpec((DEEP, CH, YB), lambda b: (last - b, 0, 0)),
        out_shape=jax.ShapeDtypeStruct((XB, CH, YB), f32),
        scratch_shapes=[field, field],
        compiler_params=params(57),
        cost_estimate=pl.CostEstimate(flops=2 * 4 * 4096 * 256 * 256, bytes_accessed=8 << 20, transcendentals=1 << 16),
        name="planes_back",
    )(forced, turned_high, turned_low, coly)


def join_kernel(control, running, colx, coly, out):
    sums = lower()
    for s in range(0, BLOCK, SUB):
        at = slice(s, s + SUB)
        high, low = split(running[:, at, :].reshape(XB * SUB, YB))
        summed = mm(high, sums) + mm(low, sums)
        factor = wide(jnp.exp(colx[at, :]))
        scale = grow(coly[at, :], SUB)
        for x in range(XB):
            out[x, at, :] = control[x, at, :] + scale * summed[x * SUB : (x + 1) * SUB, :]
            scale = scale * factor


def join(control, running, colx, coly):
    return pl.pallas_call(
        join_kernel,
        grid=(CH // BLOCK,),
        in_specs=[PLANES, PLANES, STEPS, STEPS],
        out_specs=PLANES,
        out_shape=jax.ShapeDtypeStruct((XB, CH, YB), f32),
        compiler_params=params(57),
        cost_estimate=pl.CostEstimate(flops=2 * 2 * 4096 * 256 * 256, bytes_accessed=12 << 20, transcendentals=0),
        name="join",
    )(control, running, colx, coly)


def final_kernel(partial, entered, colx, coly, out, whole_a, whole_b, sems):
    b = pl.program_id(0)
    start = (b % HALF) * (BLOCK * ROWS)
    entering = jnp.concatenate(
        [entered[pl.ds(start + 2 * (b // HALF) + h, BLOCK, stride=ROWS), :] for h in range(2)], axis=1
    )
    high, low = split(entering)
    sums = lower()
    entering = mm(high, sums) + mm(low, sums)
    tail = entered[pl.ds(start + 4, BLOCK, stride=ROWS), :]
    mine = jnp.where(b < HALF, tail, pltpu.roll(tail, 112, 1))
    for s in range(0, BLOCK, SUB):
        own = slice(s, s + SUB)
        factor = wide(jnp.exp(colx[own, :]))
        scale = grow(coly[own, :], SUB)
        for x in range(XB):
            plane = partial[x, own, :] + scale * (entering[own, :] + mine[own, x : x + 1])
            scale = scale * factor
            at = pl.ds((b * BLOCK + s) * XB + x, SUB, stride=XB)
            whole_a[at, :] = plane[:, :128]
            whole_b[at, :] = plane[:, 128:]

    def copies(step):
        at = pl.ds(pl.multiple_of(step * (BLOCK * XB), BLOCK * XB), BLOCK * XB)
        return (
            pltpu.make_async_copy(whole_a.at[at, :], out.at[at, pl.ds(0, 128)], sems.at[step, 0]),
            pltpu.make_async_copy(whole_b.at[at, :], out.at[at, pl.ds(128, 128)], sems.at[step, 1]),
        )

    for copy in copies(b):
        copy.start()

    @pl.when(b == CH // BLOCK - 1)
    def _():
        for step in range(CH // BLOCK):
            for copy in copies(step):
                copy.wait()


def final(partial, entered, colx, coly):
    return pl.pallas_call(
        final_kernel,
        grid=(CH // BLOCK,),
        in_specs=[PLANES, whole((PEERS * ROWS, 128)), STEPS, STEPS],
        out_specs=ANY,
        out_shape=jax.ShapeDtypeStruct((CH * XB, YB), f32),
        scratch_shapes=[
            pltpu.VMEM((CH * XB, 128), f32),
            pltpu.VMEM((CH * XB, 128), f32),
            pltpu.SemaphoreType.DMA((CH // BLOCK, 2)),
        ],
        compiler_params=params(57),
        name="final",
    )(partial, entered, colx, coly)


def departures_kernel(rank, returned, out):
    total = jnp.zeros((1, OBS), f32)
    values = returned[pl.ds(4, PEERS, stride=ROWS), :]
    for r in range(CAP):
        value = values[:, REQ + r : REQ + r + 1]
        total = total + jnp.sum(jnp.where(rank[...] == float(r), value, 0.0), axis=0, keepdims=True)
    out[...] = total


def departures(rank, returned):
    return pl.pallas_call(
        departures_kernel,
        in_specs=[VMEM] * 2,
        out_specs=VMEM,
        out_shape=jax.ShapeDtypeStruct((1, OBS), f32),
        compiler_params=params(8),
        cost_estimate=pl.CostEstimate(flops=1 << 20, bytes_accessed=1 << 19, transcendentals=0),
        name="departures",
    )(rank, returned)


def everywhere(rows):
    shaped = rows.reshape(PEERS * ROWS, 1, 128)
    moved = lax.all_to_all(shaped, ("gx", "gy"), split_axis=0, concat_axis=0, tiled=True)
    return moved.reshape(PEERS * ROWS, 128)


def body(
    control,
    background,
    vert_factor,
    length_rates,
    flash_weights,
    level_weights,
    obs_owner,
    obs_cell,
    obs_count,
    flash_obs,
    obs_error,
):
    shape = control.shape
    flat = control.reshape(CH * XB, YB)
    msg, colx, coly, control_planes = edges(flat, length_rates)
    asked = everywhere(msg)

    gx, gy = lax.axis_index("gx"), lax.axis_index("gy")
    place = jnp.stack([gx, gy, gx * N_Y + gy]).astype(jnp.int32)
    rates = length_rates.reshape(2, CH)
    requests, rank, ahead, behind, down = prepare(
        place, obs_count, rates, obs_owner.reshape(1, OBS), obs_cell.reshape(1, OBS),
        flash_obs.reshape(1, OBS), obs_error.reshape(1, OBS),
    )
    step_x, step_y = length_rates[0] / (XB * N_X), length_rates[1] / (YB * N_Y)
    gain = jnp.sqrt(-jnp.expm1(-2.0 * step_x)) * jnp.sqrt(-jnp.expm1(-2.0 * step_y))
    mixed = flash_weights[:, :, None] * vert_factor * gain[:, None, :]
    matrix = mixed.transpose(1, 0, 2).reshape(LEVELS, CH)
    cc = local(control_planes, colx, coly)
    asked, cc = lax.optimization_barrier((asked, cc))
    entered = everywhere(carry(asked, ahead, down, requests))
    share = background_share(background.reshape(4, LEVELS * XB, YB), jnp.repeat(flash_weights.T, XB, axis=0))
    level, scaled, turned_high, turned_low = levels_of(cc, share, coly, rates, matrix)
    forced, msg_back = observations(
        level, scaled, turned_high, turned_low, entered, coly, rates, level_weights.reshape(1, LEVELS)
    )
    returned = everywhere(msg_back)
    planes = planes_back(forced, turned_high, turned_low, coly)
    returned, planes = lax.optimization_barrier((returned, planes))
    entered_back = everywhere(carry(returned, behind, down))
    partial = join(control_planes, planes, colx, coly)
    departure = departures(rank, returned)
    grad = final(partial, entered_back, colx, coly)
    return (grad.reshape(shape), departure.reshape(OBS))


def solution(mesh):
    placed = (
        P(None, None, "gx", "gy"),
        P(None, None, "gx", "gy"),
        P(),
        P(),
        P(),
        P(),
        P(("gx", "gy"), None),
        P(("gx", "gy")),
        P(("gx", "gy")),
        P(("gx", "gy")),
        P(("gx", "gy")),
    )
    return jax.shard_map(
        body,
        mesh=mesh,
        in_specs=placed,
        out_specs=(P(None, None, "gx", "gy"), P(("gx", "gy"))),
        check_vma=False,
    )
```
